512 devices in a mesh: gx: 16 (over z_lo, core), gy: 8 (over z_hi, x), gz: 4 (over y).
Axes of the slice: x: 4, y: 4, z: 16 (z_hi: 2, z_lo: 8; z = z_hi * 8 + z_lo), core: 2. Of those that a mesh axis runs over, the one named last changes fastest.
Arguments:
- magnetization: float32 [3, 64, 1024, 1024], P(None, 'gz', 'gx', 'gy'), may hold values from -6 to 6
- stiffness: float32 [64, 1024, 1024], P('gz', 'gx', 'gy'), may hold values from 0.02 to 0.2
- residual_top: float32 [1024, 1024], P('gx', ('gy', 'gz')), may hold values from -6 to 6
- residual_side: float32 [1024, 64], P('gy', 'gz'), may hold values from -6 to 6
- top_kernel: float32 [2, 2, 2048, 2048], P(None, None, ('gx', 'gy', 'gz')), may hold values from -6 to 6
- side_kernel: float32 [2, 2, 128, 2048], P(None, None, ('gy', 'gz')), may hold values from -6 to 6
Outputs:
- gradient: float32 [3, 64, 1024, 1024], P(None, 'gz', 'gx', 'gy')
The draws below stay inside these ranges and needn't reach their ends.
All inputs are finite; a program needn't handle non-finite values.
Results may differ from the reference program's by a relative error of at most 0.0001.
Values sent between devices are 32-bit elements; how exact they have to be, the bound alone decides.
A program may use at most 64 MiB of HBM per device.

```python
import math
import jax
import jax.numpy as jnp
from jax import lax

NK = 2048
NKZ = 128
NX = 1024
NY = 1024
NZ = 64


def draw_residual_top(key, part):
    noise = jnp.clip(jax.random.normal(key, (NX, NY), jnp.float32), -6.0, 6.0)
    return noise


def level_of(stream_key, shape, shards, low, high):
    def one(axis_at, parts):
        draws = jax.random.uniform(jax.random.fold_in(jax.random.fold_in(stream_key, 6), axis_at), (parts,), jnp.float32, low / len(shards), high / len(shards))
        return jnp.repeat(jnp.exp(draws), shape[axis_at] // parts).reshape((-1,) + (1,) * (len(shape) - axis_at - 1))

    level = one(*shards[0])
    for cut in shards[1:]:
        level = level * one(*cut)
    return level


def scatter_about(rng, dims, width, bound, cuts=(), kind=jnp.bfloat16):
    loudness = level_of(rng, dims, cuts, -0.22, 0.18) if cuts else 1.0
    array = jax.random.normal(rng, dims, jnp.float32) * width * loudness
    return jnp.minimum(jnp.maximum(array, -bound), bound).astype(kind)


def setup_inputs(seed: int = 0) -> dict:
    key_list = jax.random.split(jax.random.key(seed), 7)
    return {
        "magnetization": scatter_about(key_list[0], (3, NZ, NX, NY), 1.0, 6.0, ((1, 4), (2, 16), (3, 8)), jnp.float32),
        "stiffness": jnp.clip(jnp.exp(math.log(0.2) - 2.3025851 * jax.random.uniform(key_list[1], (NZ, NX, NY), jnp.float32) ** level_of(key_list[1], (NZ, NX, NY), ((0, 4), (1, 16), (2, 8)), -0.2, 0.2)), 0.02, 0.2),
        "residual_top": draw_residual_top(jax.random.fold_in(key_list[6], 71), 0),
        "residual_side": scatter_about(key_list[3], (NY, NZ), 1.0, 6.0, ((0, 8), (1, 4)), jnp.float32),
        "top_kernel": scatter_about(key_list[4], (2, 2, NK, NK), 1.0, 6.0, ((2, 512),), jnp.float32),
        "side_kernel": scatter_about(key_list[5], (2, 2, NKZ, NK), 1.0, 6.0, ((2, 32),), jnp.float32),
    }


def harmonic(first, second):
    return 2.0 * first * second / (first + second)


def face_term(component_field, stiffness, dimension):
    extent = component_field.shape[dimension]
    upper_pad = [(0, 0), (0, 0), (0, 0)]
    upper_pad[dimension] = (0, 1)
    lower_pad = [(0, 0), (0, 0), (0, 0)]
    lower_pad[dimension] = (1, 0)
    upper_field = lax.slice_in_dim(jnp.pad(component_field, upper_pad), 1, extent + 1, axis=dimension)
    upper_stiff = lax.slice_in_dim(jnp.pad(stiffness, upper_pad), 1, extent + 1, axis=dimension)
    flux_up = harmonic(stiffness, upper_stiff) * (component_field - upper_field)
    flux_down = lax.slice_in_dim(jnp.pad(flux_up, lower_pad), 0, extent, axis=dimension)
    return flux_up - flux_down


def padded_adjoint(residual, kernel, first_size, second_size):
    first_extent, second_extent = residual.shape
    padded = jnp.pad(residual, ((0, first_size - first_extent), (0, second_size - second_extent)))
    spectrum = jnp.fft.fft2(padded)
    images = []
    for component in range(2):
        kernel_entry = lax.complex(kernel[component, 0], kernel[component, 1]).T
        inverse = jnp.fft.ifft2(jnp.conj(kernel_entry) * spectrum)
        images.append(jnp.real(inverse)[:first_extent, :second_extent])
    return images


def reference(magnetization, stiffness, residual_top, residual_side, top_kernel, side_kernel):
    top_grad = padded_adjoint(residual_top, top_kernel, NK, NK)
    side_grad = padded_adjoint(residual_side, side_kernel, NK, NKZ)
    outputs = []
    for component in range(3):
        component_field = magnetization[component]
        summed = face_term(component_field, stiffness, 0) + face_term(component_field, stiffness, 1)
        summed = summed + face_term(component_field, stiffness, 2)
        exchange = 2.0 * summed
        if component < 2:
            exchange = exchange + top_grad[component][None, :, :]
        if component > 0:
            exchange = exchange + side_grad[component - 1].T[:, None, :]
        outputs.append(exchange)
    return jnp.stack(outputs)
```

```python
import math

import jax
import jax.numpy as jnp
import numpy as np
from jax import lax
from jax.experimental import pallas as pl
from jax.experimental.pallas import tpu as pltpu
from jax.sharding import PartitionSpec as P

F32 = jnp.float32
MESH = pl.DeviceIdType.MESH
TOP_SCALE = 1.0 / 2048.0**2
SIDE_SCALE = 1.0 / (2048.0 * 128.0)


def _dot(a, b, ca=1, cb=0):
    return lax.dot_general(
        a, b, (((ca,), (cb,)), ((), ())), precision=lax.Precision.HIGHEST, preferred_element_type=F32
    )


def _cs(first, second, modulus):
    angle = 2.0 * np.pi * ((first * second) % modulus) / modulus
    return np.cos(angle), np.sin(angle)


def const_tables():
    i = np.arange
    c, s = _cs(i(16)[:, None], i(128)[None, :], 32)
    gl16 = np.concatenate([c, s], 1)
    gl32 = np.repeat(gl16, 2, axis=0)
    c, s = _cs(i(64)[:, None], i(128)[None, :], 2048)
    twist = np.concatenate([c, s], 0)
    c, s = _cs(i(16)[:, None], i(64)[None, :], 16)
    fwd = np.block([[c, s], [-s, c]])
    inv = np.block([[c.T, -s.T], [s.T, c.T]])
    back = gl16.reshape(16, 2, 128).transpose(1, 0, 2).reshape(32, 128)
    c, s = _cs(i(32)[:, None], i(32)[None, :], 32)
    fold = np.concatenate([c, s], 0)
    return [np.asarray(t, np.float32) for t in (gl32, gl16, twist, fwd, inv, back, fold)]


def _iota(shape, dim):
    return lax.broadcasted_iota(jnp.int32, shape, dim)


def _angle(product, modulus):
    return (product & (modulus - 1)).astype(F32) * (2.0 * math.pi / modulus)


def first_table(zh, n0):
    row = _iota((128, 256), 0)
    col = _iota((128, 256), 1)
    ky = 64 * (row // 4) + row % 4 + 4 * n0
    y = 32 * (col // 16) + col % 16 + 512 * zh
    parts = []
    for h in (0, 1):
        t = _angle(ky * (y + 16 * h), 2048)
        parts += [jnp.cos(t), -jnp.sin(t)]
    return parts


def last_table(zh, n0):
    row = _iota((16, 64), 0)
    col = _iota((16, 64), 1)
    s = 4 * (col % 16) + col // 16
    out = []
    for a in (0, 1):
        t = _angle(s * (32 * row + n0 + 16 * a + 512 * zh), 2048)
        out.append(jnp.concatenate([jnp.cos(t) * TOP_SCALE, jnp.sin(t) * TOP_SCALE], 0))
    return out


def side_table(zh, n0):
    row = _iota((16, 64), 0)
    z = _iota((16, 64), 1)
    own = jnp.where(row < 8, zh, 1 - zh)
    t = _angle((64 * own + 4 * n0 + row % 4) * z, 128)
    return jnp.where(row % 8 < 4, jnp.cos(t), -jnp.sin(t))


def side_last_table(yy):
    row = _iota((16, 128), 0)
    col = _iota((16, 128), 1)
    kz = 64 * (col % 2) + 4 * ((col // 2) % 16) + col // 32
    t = _angle(kz * (row + 16 * yy), 128)
    return jnp.concatenate([jnp.cos(t) * SIDE_SCALE, jnp.sin(t) * SIDE_SCALE], 0)


def first_stage(w, packed, roll):
    p = [_dot(t, packed) for t in w]
    low = _iota((128, 128), 1) < 64
    return jnp.where(low, p[0] + roll(p[2], 64), roll(p[1], 64) + p[3])


def side_first(w, data, roll):
    t = _dot(w, data)
    low = _iota((4, 128), 1) < 64
    own, other = [], []
    for x in range(4):
        for base, out in ((0, own), (8, other)):
            o = t[base : base + 8, 128 * x : 128 * x + 128]
            q = roll(o, 64)
            f0 = jnp.where(low, o[0:4], q[4:8])
            f1 = jnp.where(low, q[0:4], o[4:8])
            out.append(jnp.concatenate([f0, f1], 0))
    return own, other


def line_stage(rows, kernel_at, tabs, roll):
    gl, twist, fwd, inv, back = tabs
    twc, tws = twist[:64], twist[64:]
    p = _dot(jnp.concatenate(rows, 1), gl, 0, 0)
    mid = []
    for r in range(4):
        q = p[128 * r : 128 * r + 128]
        bre = q[:64, :128] + q[64:, 128:]
        bim = q[64:, :128] - q[:64, 128:]
        mid.append(jnp.concatenate([bre * twc + bim * tws, bim * twc - bre * tws], 0))
    spectrum = _dot(fwd, jnp.concatenate(mid, 1))
    weighted = []
    for c in range(2):
        for r in range(4):
            sre = spectrum[:16, 128 * r : 128 * r + 128]
            sim = spectrum[16:, 128 * r : 128 * r + 128]
            kre, kim = kernel_at(c, 0, r), kernel_at(c, 1, r)
            weighted.append(
                jnp.concatenate([kre * sre + kim * sim, kre * sim - kim * sre], 0)
            )
    v = _dot(inv, jnp.concatenate(weighted, 1))
    turned = []
    for cr in range(8):
        vre = v[:64, 128 * cr : 128 * cr + 128]
        vim = v[64:, 128 * cr : 128 * cr + 128]
        turned += [vre * twc - vim * tws, vim * twc + vre * tws]
    u = _dot(back, jnp.concatenate(turned, 0), 1, 1)
    return spread(u, 16, roll)


def spread(u, half, roll):
    sign = jnp.where(_iota((half, 128), 1) < 64, -1.0, 1.0)
    out = []
    for cr in range(8):
        lanes = slice(128 * cr, 128 * cr + 128)
        out.append(u[:half, lanes] + sign * roll(u[half:, lanes], 64))
    return out


def fold_stage(rows, fold, roll):
    return spread(_dot(fold, jnp.concatenate(rows, 1)), 32, roll)


def last_stage(table, rows, roll):
    g = _dot(table, jnp.concatenate(rows, 1))
    low = _iota((16, 128), 1) < 64
    part = [g[:16, 128 * c : 128 * c + 128] - roll(g[16:, 128 * c : 128 * c + 128], 64) for c in (0, 1)]
    return jnp.where(low, part[0], roll(part[1], 64))


def plane_id(zh, n):
    return {"gy": 4 * zh + n // 4, "gz": n % 4}


def ring_place(v):
    z = v // 2
    return 2 * (z % 8) + v % 2, z // 8


def rows8(start, size):
    return pl.ds(pl.multiple_of(start, 8), size)


def body(
    mag, stiff, rtop, rside, ktop, kside, gl32, gl16, twist, fwd, inv, back, fold,
    exch, top, side,
    field, kraw, kt, ks,
    send1, recv1, send2, recv2, send3, recv3, send4, recv4, send5, recv5,
    hop1, line1, own3, hop2, other3, recvs,
    hx_out_hi, hx_out_lo, hx_lo, hx_hi, hy_out_hi, hy_out_lo, hy_lo, hy_hi,
    local, ssem, rsem, hsend, hrecv,
):
    gx, gy, gz = lax.axis_index("gx"), lax.axis_index("gy"), lax.axis_index("gz")
    zh, xx = gy // 4, gy % 4
    n0 = 4 * xx + gz
    m0 = 2 * gx + zh
    v0 = 2 * (8 * zh + gx // 2) + gx % 2
    crosses = jnp.logical_or(gy == 3, gy == 4)
    far = {"gx": (gx + 8) % 16, "gy": 4 * (1 - zh) + xx}

    def roll(value, shift):
        return pltpu.roll(value, shift, 1)

    def over_plane(action):
        def step(k, carry):
            action((n0 + k) % 16)
            return carry

        lax.fori_loop(1, 16, step, 0)

    def over_column(action):
        def step(k, carry):
            half = (k + 1) // 2
            off = jnp.where(k % 2 == 1, 16 - half, 16 + half)
            px, ph = ring_place((v0 + off) % 32)
            action(2 * px + ph, {"gx": px, "gy": 4 * ph + xx})
            return carry

        lax.fori_loop(0, 31, step, 0)

    def remote(src, dst, sems, target):
        send_sem, recv_sem = sems
        return pltpu.make_async_remote_copy(
            src_ref=src, dst_ref=dst, send_sem=send_sem, recv_sem=recv_sem,
            device_id=target, device_id_type=MESH,
        )

    def wait_bytes(ref, sem):
        pltpu.make_async_copy(ref, ref, sem).wait()

    def pair(i):
        return ssem.at[i], rsem.at[i]

    loads = [
        pltpu.make_async_copy(mag, field.at[0:3, pl.ds(64, 1024)], local.at[0]),
        pltpu.make_async_copy(stiff, field.at[3:4, pl.ds(64, 1024)], local.at[1]),
        pltpu.make_async_copy(ktop, kraw.at[0], local.at[2]),
        pltpu.make_async_copy(kside, kraw.at[1], local.at[3]),
    ]
    for load in loads:
        load.start()
    barrier = pltpu.get_barrier_semaphore()
    over_plane(
        lambda n: pl.semaphore_signal(barrier, inc=1, device_id=plane_id(zh, n), device_id_type=MESH)
    )
    over_column(
        lambda m, target: pl.semaphore_signal(barrier, inc=1, device_id=target, device_id_type=MESH)
    )

    @pl.when(crosses)
    def _():
        pl.semaphore_signal(barrier, inc=1, device_id={"gy": 7 - gy}, device_id_type=MESH)

    send1[0:16, :] = jnp.concatenate([rtop[0:16, :], rtop[16:32, :]], 1)
    send1[16:32, :] = rside[...]
    recv1[rows8(32 * n0, 32), :] = send1[...]
    table1 = first_table(zh, n0)
    table_side = side_table(zh, n0)

    pl.semaphore_wait(barrier, 46 + crosses.astype(jnp.int32))

    over_plane(
        lambda n: remote(send1, recv1.at[rows8(32 * n0, 32)], pair(0), plane_id(zh, n)).start()
    )

    for load in loads:
        load.wait()
    zero_face = jnp.zeros((64, 128), F32)
    for c in range(4):
        hx_out_hi[16 * c : 16 * c + 16, :] = field[c, pl.ds(64 + 63, 16, stride=64), :]
        hx_out_lo[16 * c : 16 * c + 16, :] = field[c, pl.ds(64, 16, stride=64), :]
    lane = _iota((64, 128), 1)

    def pack(z, carry):
        hi, lo = carry
        for c in range(4):
            at = 16 * c + z
            turned = pltpu.roll(field[c, rows8(64 + 64 * z, 64), :], at + 1, 1)
            hi = jnp.where(lane == at, turned, hi)
            lo = jnp.where(lane == at + 1, turned, lo)
        return hi, lo

    packed_hi, packed_lo = lax.fori_loop(0, 16, pack, (zero_face, zero_face))
    hy_out_hi[...] = packed_hi
    hy_out_lo[...] = packed_lo

    x_up = (gx < 15, remote(hx_out_hi, hx_lo, (hsend.at[0], hrecv.at[0]), {"gx": (gx + 1) % 16}))
    x_dn = (gx > 0, remote(hx_out_lo, hx_hi, (hsend.at[1], hrecv.at[1]), {"gx": (gx + 15) % 16}))
    y_up = (gy < 7, remote(hy_out_hi, hy_lo, (hsend.at[2], hrecv.at[2]), {"gy": (gy + 1) % 8}))
    y_dn = (gy > 0, remote(hy_out_lo, hy_hi, (hsend.at[3], hrecv.at[3]), {"gy": (gy + 7) % 8}))
    z_up = (
        gz < 3,
        remote(field.at[:, pl.ds(1024, 64)], field.at[:, pl.ds(0, 64)],
               (hsend.at[4], hrecv.at[4]), {"gz": (gz + 1) % 4}),
    )
    z_dn = (
        gz > 0,
        remote(field.at[:, pl.ds(64, 64)], field.at[:, pl.ds(1088, 64)],
               (hsend.at[5], hrecv.at[5]), {"gz": (gz + 3) % 4}),
    )
    faces = (y_up, y_dn, z_up, z_dn, x_up, x_dn)
    for there, copy in faces:

        @pl.when(there)
        def _(copy=copy):
            copy.start()

    for missing, ref in ((gx == 0, hx_lo), (gx == 15, hx_hi), (gy == 0, hy_lo), (gy == 7, hy_hi)):

        @pl.when(missing)
        def _(ref=ref):
            ref[...] = zero_face

    for missing, start in ((gz == 0, 0), (gz == 3, 1088)):

        @pl.when(missing)
        def _(start=start):
            for c in range(4):
                field[c, pl.ds(start, 64), :] = zero_face

    for which, out in ((0, kt), (1, ks)):
        for cp in range(4):
            for j in range(16):
                out[pl.ds(64 * cp + j, 4, stride=16), :] = kraw[
                    which, cp // 2, cp % 2, :, 128 * j : 128 * j + 128
                ]

    wait_bytes(recv1.at[pl.ds(0, 480)], rsem.at[0])
    packed = jnp.concatenate([recv1[32 * n : 32 * n + 16, :] for n in range(16)], 0)
    first = first_stage(table1, packed, roll)
    for m in range(32):
        send2[m] = first[4 * m : 4 * m + 4]
    recv2[m0] = send2[m0]
    over_column(lambda m, target: remote(send2.at[m], recv2.at[m0], pair(1), target).start())

    data = jnp.concatenate(
        [
            jnp.concatenate(
                [recv1[32 * (4 * x + y) + 16 : 32 * (4 * x + y) + 32, :] for y in range(4)], 0
            )
            for x in range(4)
        ],
        1,
    )
    own, other = side_first(table_side, data, roll)
    for x in range(4):
        line1[rows8(32 * zh + 8 * x, 8), :] = own[x]
        hop1[8 * x : 8 * x + 8, :] = other[x]
    remote(hop1, line1.at[rows8(32 * zh, 32)], pair(5), far).start()

    table_last = last_table(zh, n0)
    table_side_last = side_last_table(gz)

    wait_bytes(recv2.at[pl.ds(0, 31)], rsem.at[1])
    shared = (twist[...], fwd[...], inv[...], back[...])
    lines = line_stage(
        [recv2[:, r, :] for r in range(4)],
        lambda c, p, r: kt[64 * (2 * c + p) + 16 * r : 64 * (2 * c + p) + 16 * r + 16, :],
        (gl32[...],) + shared,
        roll,
    )
    for cr in range(8):
        send3[pl.ds(cr, 16, stride=8), :] = lines[cr]
    recv3[rows8(8 * m0, 8), :] = send3[rows8(8 * gx, 8), :]
    over_column(
        lambda m, target: remote(
            send3.at[rows8(8 * (m // 2), 8)], recv3.at[rows8(8 * m0, 8)], pair(2), target
        ).start()
    )

    wait_bytes(line1.at[pl.ds(0, 32)], rsem.at[5])
    lines = line_stage(
        [line1[pl.ds(r, 16, stride=4), :] for r in range(4)],
        lambda c, p, r: ks[64 * (2 * c + p) + 16 * r : 64 * (2 * c + p) + 16 * r + 16, :],
        (gl16[...],) + shared,
        roll,
    )
    for cr in range(8):
        here, there = lines[cr][:8], lines[cr][8:]
        own3[pl.ds(cr, 8, stride=8), :] = jnp.where(zh == 0, here, there)
        hop2[pl.ds(cr, 8, stride=8), :] = jnp.where(zh == 0, there, here)
    remote(hop2, other3, pair(6), far).start()
    recvs[rows8(32 * n0 + 16 * zh, 16), :] = own3[rows8(16 * xx, 16), :]
    over_plane(
        lambda n: remote(
            own3.at[rows8(16 * (n // 4), 16)],
            recvs.at[rows8(32 * n0 + 16 * zh, 16)], pair(7), plane_id(zh, n),
        ).start()
    )

    arrivals = (
        (gx > 0, hx_lo, 0), (gx < 15, hx_hi, 1), (gy > 0, hy_lo, 2), (gy < 7, hy_hi, 3),
        (gz > 0, field.at[:, pl.ds(0, 64)], 4), (gz < 3, field.at[:, pl.ds(1088, 64)], 5),
    )
    for there, ref, i in arrivals:

        @pl.when(there)
        def _(ref=ref, i=i):
            wait_bytes(ref, hrecv.at[i])

    sub = _iota((64, 128), 0)

    def exchange(z, carry):
        def slab(c, step):
            return field[c, rows8(64 + 64 * (z + step), 64), :]

        def around(c):
            at = 16 * c + z
            center = slab(c, 0)
            below = jnp.where(sub == 0, hx_lo[pl.ds(at, 1), :], pltpu.roll(center, 1, 0))
            above = jnp.where(sub == 63, hx_hi[pl.ds(at, 1), :], pltpu.roll(center, 63, 0))
            left = jnp.where(lane == 0, pltpu.roll(hy_lo[...], 128 - at, 1), pltpu.roll(center, 1, 1))
            right = jnp.where(
                lane == 127, pltpu.roll(hy_hi[...], 126 - at, 1), pltpu.roll(center, 127, 1)
            )
            return center, (slab(c, -1), slab(c, 1), below, above, left, right)

        a, near = around(3)
        weights = [4.0 * a * b / (a + b) for b in near]
        for c in range(3):
            m, beside = around(c)
            total = weights[0] * (m - beside[0])
            for w, b in zip(weights[1:], beside[1:]):
                total = total + w * (m - b)
            exch[c, rows8(64 * z, 64), :] = total
        return carry

    lax.fori_loop(0, 16, exchange, 0)

    wait_bytes(other3, rsem.at[6])
    recvs[rows8(32 * n0 + 16 * (1 - zh), 16), :] = other3[rows8(16 * xx, 16), :]
    over_plane(
        lambda n: remote(
            other3.at[rows8(16 * (n // 4), 16)],
            recvs.at[rows8(32 * n0 + 16 * (1 - zh), 16)], pair(8), plane_id(zh, n),
        ).start()
    )

    wait_bytes(recv3.at[pl.ds(0, 248)], rsem.at[2])
    folded = fold_stage([recv3[pl.ds(cr, 32, stride=8), :] for cr in range(8)], fold[...], roll)
    for cr in range(8):
        send4[pl.ds(cr, 16, stride=16), :] = folded[cr][:16]
        send4[pl.ds(8 + cr, 16, stride=16), :] = folded[cr][16:]
    recv4[rows8(16 * n0, 16), :] = send4[rows8(16 * n0, 16), :]
    over_plane(
        lambda n: remote(
            send4.at[rows8(16 * n, 16)], recv4.at[rows8(16 * n0, 16)], pair(3), plane_id(zh, n)
        ).start()
    )

    wait_bytes(recvs.at[pl.ds(0, 240)], rsem.at[7])
    wait_bytes(recvs.at[pl.ds(0, 240)], rsem.at[8])
    columns = [
        jnp.concatenate([recvs[pl.ds(8 * e + 4 * c + r, 32, stride=16), :] for r in range(4)], 0)
        for c in range(2)
        for e in range(2)
    ]
    g = _dot(table_side_last, jnp.concatenate(columns, 1))
    low = _iota((16, 128), 1) < 64
    for c in range(2):
        halves = [
            g[:16, 128 * q : 128 * q + 128] - roll(g[16:, 128 * q : 128 * q + 128], 64)
            for q in (2 * c, 2 * c + 1)
        ]
        side[c] = jnp.where(low, halves[0], roll(halves[1], 64))

    wait_bytes(recv4.at[pl.ds(0, 240)], rsem.at[3])
    for a in range(2):
        rows = [
            jnp.concatenate(
                [recv4[pl.ds(8 * a + 4 * c + r, 16, stride=16), :] for r in range(4)], 0
            )
            for c in range(2)
        ]
        send5[pl.ds(a, 16, stride=2), :] = last_stage(table_last[a], rows, roll)
    recv5[rows8(8 * n0, 8), :] = send5[rows8(8 * xx, 8), :]
    over_plane(
        lambda n: remote(
            send5.at[rows8(8 * (n // 4), 8)], recv5.at[rows8(8 * n0, 8)], pair(4), plane_id(zh, n)
        ).start()
    )

    wait_bytes(recv1.at[pl.ds(0, 480)], ssem.at[0])
    wait_bytes(send2.at[pl.ds(0, 31)], ssem.at[1])
    wait_bytes(recv3.at[pl.ds(0, 248)], ssem.at[2])
    wait_bytes(recv4.at[pl.ds(0, 240)], ssem.at[3])
    wait_bytes(hop1, ssem.at[5])
    wait_bytes(hop2, ssem.at[6])
    wait_bytes(recvs.at[pl.ds(0, 240)], ssem.at[7])
    wait_bytes(recvs.at[pl.ds(0, 240)], ssem.at[8])
    for there, copy in faces:

        @pl.when(there)
        def _(copy=copy):
            copy.wait_send()

    wait_bytes(recv5.at[pl.ds(0, 120)], rsem.at[4])
    lines_y = jnp.concatenate([recv5[pl.ds(q, 16, stride=8), :] for q in range(8)], 0)
    top[...] = lines_y.T
    wait_bytes(recv5.at[pl.ds(0, 120)], ssem.at[4])


def on_device(magnetization, stiffness, residual_top, residual_side, top_kernel, side_kernel):
    tables = [jnp.asarray(t) for t in const_tables()]
    vmem = pl.BlockSpec(memory_space=pltpu.VMEM)
    anyspace = pl.BlockSpec(memory_space=pl.ANY)

    def buf(*shape):
        return pltpu.VMEM(shape, F32)

    scratch = [
        buf(4, 1152, 128), buf(2, 2, 2, 4, 2048), buf(256, 128), buf(256, 128),
        buf(32, 128), buf(512, 128), buf(32, 4, 128), buf(32, 4, 128),
        buf(128, 128), buf(256, 128), buf(256, 128), buf(256, 128), buf(32, 128), buf(128, 128),
        buf(32, 128), buf(64, 128), buf(64, 128), buf(64, 128), buf(64, 128), buf(512, 128),
        buf(64, 128), buf(64, 128), buf(64, 128), buf(64, 128),
        buf(64, 128), buf(64, 128), buf(64, 128), buf(64, 128),
        pltpu.SemaphoreType.DMA((4,)), pltpu.SemaphoreType.DMA((9,)), pltpu.SemaphoreType.DMA((9,)),
        pltpu.SemaphoreType.DMA((6,)), pltpu.SemaphoreType.DMA((6,)),
    ]
    exch, top, side = pl.pallas_call(
        body,
        out_shape=[
            jax.ShapeDtypeStruct((3, 1024, 128), F32),
            jax.ShapeDtypeStruct((128, 128), F32),
            jax.ShapeDtypeStruct((2, 16, 128), F32),
        ],
        in_specs=[anyspace, anyspace, vmem, vmem, anyspace, anyspace] + [vmem] * len(tables),
        out_specs=[vmem] * 3,
        scratch_shapes=scratch,
        compiler_params=pltpu.CompilerParams(
            collective_id=0, has_side_effects=True, vmem_limit_bytes=40 * 1024 * 1024
        ),
        name="adjoint",
    )(
        magnetization.reshape(3, 1024, 128),
        stiffness.reshape(1, 1024, 128),
        residual_top.T,
        residual_side.T,
        top_kernel,
        side_kernel,
        *tables,
    )
    exch = exch.reshape(3, 16, 64, 128)
    top = top.reshape(2, 1, 64, 128)
    side = side.reshape(2, 16, 1, 128)
    return jnp.stack([exch[0] + top[0], exch[1] + top[1] + side[0], exch[2] + side[1]])


def solution(mesh):
    placed = (
        P(None, "gz", "gx", "gy"),
        P("gz", "gx", "gy"),
        P("gx", ("gy", "gz")),
        P("gy", "gz"),
        P(None, None, ("gx", "gy", "gz"), None),
        P(None, None, ("gy", "gz"), None),
    )
    return jax.shard_map(
        on_device, mesh=mesh, in_specs=placed, out_specs=P(None, "gz", "gx", "gy"), check_vma=False
    )
```

```python
import math

import jax
import jax.numpy as jnp
import numpy as np
from jax import lax
from jax.experimental import pallas as pl
from jax.experimental.pallas import tpu as pltpu
from jax.sharding import PartitionSpec as P

F32 = jnp.float32
MESH = pl.DeviceIdType.MESH
TOP_SCALE = 1.0 / 2048.0**2
SIDE_SCALE = 1.0 / (2048.0 * 128.0)


def _dot(a, b, ca=1, cb=0):
    return lax.dot_general(
        a, b, (((ca,), (cb,)), ((), ())), precision=lax.Precision.HIGHEST, preferred_element_type=F32
    )


def _cs(first, second, modulus):
    angle = 2.0 * np.pi * ((first * second) % modulus) / modulus
    return np.cos(angle), np.sin(angle)


def const_tables():
    i = np.arange
    c, s = _cs(i(16)[:, None], i(128)[None, :], 32)
    gl16 = np.concatenate([c, s], 1)
    gl32 = np.repeat(gl16, 2, axis=0)
    c, s = _cs(i(64)[:, None], i(128)[None, :], 2048)
    twist = np.concatenate([c, s], 0)
    c, s = _cs(i(16)[:, None], i(64)[None, :], 16)
    fwd = np.block([[c, s], [-s, c]])
    inv = np.block([[c.T, -s.T], [s.T, c.T]])
    back = gl16.reshape(16, 2, 128).transpose(1, 0, 2).reshape(32, 128)
    c, s = _cs(i(32)[:, None], i(32)[None, :], 32)
    fold = np.concatenate([c, s], 0)
    blocks = (gl32[:, :128], gl32[:, 128:], twist, fwd, inv, back, fold)
    rows = [np.pad(t, ((0, 0), (0, 128 - t.shape[1]))) for t in blocks]
    return np.concatenate(rows, 0).astype(np.float32)


def _iota(shape, dim):
    return lax.broadcasted_iota(jnp.int32, shape, dim)


def _angle(product, modulus):
    return (product & (modulus - 1)).astype(F32) * (2.0 * math.pi / modulus)


def first_table(zh, n0):
    row = _iota((128, 256), 0)
    col = _iota((128, 256), 1)
    ky = 64 * (row // 4) + row % 4 + 4 * n0
    y = 32 * (col // 16) + col % 16 + 512 * zh
    parts = []
    for h in (0, 1):
        t = _angle(ky * (y + 16 * h), 2048)
        parts += [jnp.cos(t), -jnp.sin(t)]
    return parts


def last_table(zh, n0):
    row = _iota((16, 64), 0)
    col = _iota((16, 64), 1)
    s = 4 * (col % 16) + col // 16
    out = []
    for a in (0, 1):
        t = _angle(s * (32 * row + n0 + 16 * a + 512 * zh), 2048)
        out.append(jnp.concatenate([jnp.cos(t) * TOP_SCALE, jnp.sin(t) * TOP_SCALE], 0))
    return out


def side_table(zh, n0):
    row = _iota((16, 64), 0)
    z = _iota((16, 64), 1)
    own = jnp.where(row < 8, zh, 1 - zh)
    t = _angle((64 * own + 4 * n0 + row % 4) * z, 128)
    return jnp.where(row % 8 < 4, jnp.cos(t), -jnp.sin(t))


def side_last_table(yy):
    row = _iota((16, 128), 0)
    col = _iota((16, 128), 1)
    kz = 64 * (col % 2) + 4 * ((col // 2) % 16) + col // 32
    t = _angle(kz * (row + 16 * yy), 128)
    return jnp.concatenate([jnp.cos(t) * SIDE_SCALE, jnp.sin(t) * SIDE_SCALE], 0)


def first_stage(w, packed, roll):
    p = [_dot(t, packed) for t in w]
    low = _iota((128, 128), 1) < 64
    return jnp.where(low, p[0] + roll(p[2], 64), roll(p[1], 64) + p[3])


def side_first(w, data, roll):
    t = _dot(w, data)
    low = _iota((4, 128), 1) < 64
    own, other = [], []
    for x in range(4):
        for base, out in ((0, own), (8, other)):
            o = t[base : base + 8, 128 * x : 128 * x + 128]
            q = roll(o, 64)
            f0 = jnp.where(low, o[0:4], q[4:8])
            f1 = jnp.where(low, q[0:4], o[4:8])
            out.append(jnp.concatenate([f0, f1], 0))
    return own, other


def line_stage(rows, kernel_at, tabs, roll):
    gl, twist, fwd, inv, back = tabs
    twc, tws = twist[:64], twist[64:]
    p = _dot(jnp.concatenate(rows, 1), gl, 0, 0)
    mid = []
    for r in range(4):
        q = p[128 * r : 128 * r + 128]
        bre = q[:64, :128] + q[64:, 128:]
        bim = q[64:, :128] - q[:64, 128:]
        mid.append(jnp.concatenate([bre * twc + bim * tws, bim * twc - bre * tws], 0))
    spectrum = _dot(fwd, jnp.concatenate(mid, 1))
    weighted = []
    for c in range(2):
        for r in range(4):
            sre = spectrum[:16, 128 * r : 128 * r + 128]
            sim = spectrum[16:, 128 * r : 128 * r + 128]
            kre, kim = kernel_at(c, 0, r), kernel_at(c, 1, r)
            weighted.append(
                jnp.concatenate([kre * sre + kim * sim, kre * sim - kim * sre], 0)
            )
    v = _dot(inv, jnp.concatenate(weighted, 1))
    turned = []
    for cr in range(8):
        vre = v[:64, 128 * cr : 128 * cr + 128]
        vim = v[64:, 128 * cr : 128 * cr + 128]
        turned += [vre * twc - vim * tws, vim * twc + vre * tws]
    u = _dot(back, jnp.concatenate(turned, 0), 1, 1)
    return spread(u, 16, roll)


def spread(u, half, roll):
    sign = jnp.where(_iota((half, 128), 1) < 64, -1.0, 1.0)
    out = []
    for cr in range(8):
        lanes = slice(128 * cr, 128 * cr + 128)
        out.append(u[:half, lanes] + sign * roll(u[half:, lanes], 64))
    return out


def fold_stage(rows, fold, roll):
    return spread(_dot(fold, jnp.concatenate(rows, 1)), 32, roll)


def last_stage(table, rows, roll):
    g = _dot(table, jnp.concatenate(rows, 1))
    low = _iota((16, 128), 1) < 64
    part = [g[:16, 128 * c : 128 * c + 128] - roll(g[16:, 128 * c : 128 * c + 128], 64) for c in (0, 1)]
    return jnp.where(low, part[0], roll(part[1], 64))


def plane_id(zh, n):
    return {"gy": 4 * zh + n // 4, "gz": n % 4}


def ring_place(v):
    z = v // 2
    return 2 * (z % 8) + v % 2, z // 8


def rows8(start, size):
    return pl.ds(pl.multiple_of(start, 8), size)


def body(
    mag, stiff, rtop_in, rside_in, ktop, kside, tables,
    exch, top,
    field, rtop, rside, tabs, kraw, kt, ks,
    send1, recv1, recv1s, send2, recv2, send3, recv3, send4, recv4, send5, recv5,
    hop1, line1, own3, hop2, other3, recvs,
    hx_out_hi, hx_out_lo, hx_lo, hx_hi, hy_out_hi, hy_out_lo, hy_lo, hy_hi,
    local, ssem, rsem, hsend, hrecv,
):
    gx, gy, gz = lax.axis_index("gx"), lax.axis_index("gy"), lax.axis_index("gz")
    zh, xx = gy // 4, gy % 4
    n0 = 4 * xx + gz
    m0 = 2 * gx + zh
    v0 = 2 * (8 * zh + gx // 2) + gx % 2
    crosses = jnp.logical_or(gy == 3, gy == 4)
    far = {"gx": (gx + 8) % 16, "gy": 4 * (1 - zh) + xx}

    def roll(value, shift):
        return pltpu.roll(value, shift, 1)

    def over_plane(action):
        def step(k, carry):
            action((n0 + k) % 16)
            return carry

        lax.fori_loop(1, 16, step, 0)

    def over_column(action):
        def step(k, carry):
            half = (k + 1) // 2
            off = jnp.where(k % 2 == 1, 16 - half, 16 + half)
            px, ph = ring_place((v0 + off) % 32)
            action(2 * px + ph, {"gx": px, "gy": 4 * ph + xx})
            return carry

        lax.fori_loop(0, 31, step, 0)

    def remote(src, dst, sems, target):
        send_sem, recv_sem = sems
        return pltpu.make_async_remote_copy(
            src_ref=src, dst_ref=dst, send_sem=send_sem, recv_sem=recv_sem,
            device_id=target, device_id_type=MESH,
        )

    def wait_bytes(ref, sem):
        pltpu.make_async_copy(ref, ref, sem).wait()

    def pair(i):
        return ssem.at[i], rsem.at[i]

    residuals = [
        pltpu.make_async_copy(rtop_in, rtop, local.at[4]),
        pltpu.make_async_copy(rside_in, rside, local.at[5]),
    ]
    loads = [
        pltpu.make_async_copy(tables, tabs, local.at[6]),
        pltpu.make_async_copy(mag, field.at[0:3, pl.ds(64, 1024)], local.at[0]),
        pltpu.make_async_copy(stiff, field.at[3:4, pl.ds(64, 1024)], local.at[1]),
        pltpu.make_async_copy(ktop, kraw.at[0], local.at[2]),
        pltpu.make_async_copy(kside, kraw.at[1], local.at[3]),
    ]
    for load in residuals + loads:
        load.start()
    barrier = pltpu.get_barrier_semaphore()
    over_plane(
        lambda n: pl.semaphore_signal(barrier, inc=1, device_id=plane_id(zh, n), device_id_type=MESH)
    )
    over_column(
        lambda m, target: pl.semaphore_signal(barrier, inc=1, device_id=target, device_id_type=MESH)
    )

    @pl.when(crosses)
    def _():
        pl.semaphore_signal(barrier, inc=1, device_id={"gy": 7 - gy}, device_id_type=MESH)

    for load in residuals:
        load.wait()
    send1[...] = jnp.concatenate([rtop[0:16, :], rtop[16:32, :]], 1)
    recv1[rows8(16 * n0, 16), :] = send1[...]
    recv1s[rows8(16 * n0, 16), :] = rside[...]
    table1 = first_table(zh, n0)
    table_side = side_table(zh, n0)

    pl.semaphore_wait(barrier, 46 + crosses.astype(jnp.int32))

    over_plane(
        lambda n: remote(send1, recv1.at[rows8(16 * n0, 16)], pair(0), plane_id(zh, n)).start()
    )
    over_plane(
        lambda n: remote(rside, recv1s.at[rows8(16 * n0, 16)], pair(9), plane_id(zh, n)).start()
    )

    for load in loads:
        load.wait()
    zero_face = jnp.zeros((64, 128), F32)
    for c in range(4):
        hx_out_hi[16 * c : 16 * c + 16, :] = field[c, pl.ds(64 + 63, 16, stride=64), :]
        hx_out_lo[16 * c : 16 * c + 16, :] = field[c, pl.ds(64, 16, stride=64), :]
    lane = _iota((64, 128), 1)

    def pack(z, carry):
        hi, lo = carry
        for c in range(4):
            at = 16 * c + z
            turned = pltpu.roll(field[c, rows8(64 + 64 * z, 64), :], at + 1, 1)
            hi = jnp.where(lane == at, turned, hi)
            lo = jnp.where(lane == at + 1, turned, lo)
        return hi, lo

    packed_hi, packed_lo = lax.fori_loop(0, 16, pack, (zero_face, zero_face))
    hy_out_hi[...] = packed_hi
    hy_out_lo[...] = packed_lo

    x_up = (gx < 15, remote(hx_out_hi, hx_lo, (hsend.at[0], hrecv.at[0]), {"gx": (gx + 1) % 16}))
    x_dn = (gx > 0, remote(hx_out_lo, hx_hi, (hsend.at[1], hrecv.at[1]), {"gx": (gx + 15) % 16}))
    y_up = (gy < 7, remote(hy_out_hi, hy_lo, (hsend.at[2], hrecv.at[2]), {"gy": (gy + 1) % 8}))
    y_dn = (gy > 0, remote(hy_out_lo, hy_hi, (hsend.at[3], hrecv.at[3]), {"gy": (gy + 7) % 8}))
    z_up = (
        gz < 3,
        remote(field.at[:, pl.ds(1024, 64)], field.at[:, pl.ds(0, 64)],
               (hsend.at[4], hrecv.at[4]), {"gz": (gz + 1) % 4}),
    )
    z_dn = (
        gz > 0,
        remote(field.at[:, pl.ds(64, 64)], field.at[:, pl.ds(1088, 64)],
               (hsend.at[5], hrecv.at[5]), {"gz": (gz + 3) % 4}),
    )
    faces = (y_up, y_dn, z_up, z_dn, x_up, x_dn)
    for there, copy in faces:

        @pl.when(there)
        def _(copy=copy):
            copy.start()

    for missing, ref in ((gx == 0, hx_lo), (gx == 15, hx_hi), (gy == 0, hy_lo), (gy == 7, hy_hi)):

        @pl.when(missing)
        def _(ref=ref):
            ref[...] = zero_face

    for missing, start in ((gz == 0, 0), (gz == 3, 1088)):

        @pl.when(missing)
        def _(start=start):
            for c in range(4):
                field[c, pl.ds(start, 64), :] = zero_face

    for which, out in ((0, kt), (1, ks)):
        for cp in range(4):
            for j in range(16):
                out[pl.ds(64 * cp + j, 4, stride=16), :] = kraw[
                    which, cp // 2, cp % 2, :, 128 * j : 128 * j + 128
                ]

    wait_bytes(recv1.at[pl.ds(0, 240)], rsem.at[0])
    first = first_stage(table1, recv1[...], roll)
    for m in range(32):
        send2[m] = first[4 * m : 4 * m + 4]
    recv2[m0] = send2[m0]
    over_column(lambda m, target: remote(send2.at[m], recv2.at[m0], pair(1), target).start())

    wait_bytes(recv1s.at[pl.ds(0, 240)], rsem.at[9])
    data = jnp.concatenate([recv1s[64 * x : 64 * x + 64, :] for x in range(4)], 1)
    own, other = side_first(table_side, data, roll)
    for x in range(4):
        line1[rows8(32 * zh + 8 * x, 8), :] = own[x]
        hop1[8 * x : 8 * x + 8, :] = other[x]
    remote(hop1, line1.at[rows8(32 * zh, 32)], pair(5), far).start()

    table_last = last_table(zh, n0)
    table_side_last = side_last_table(gz)

    wait_bytes(recv2.at[pl.ds(0, 31)], rsem.at[1])
    shared = (tabs[64:192, :], tabs[192:224, :], tabs[224:352, :32], tabs[352:384, :])
    lines = line_stage(
        [recv2[:, r, :] for r in range(4)],
        lambda c, p, r: kt[64 * (2 * c + p) + 16 * r : 64 * (2 * c + p) + 16 * r + 16, :],
        (jnp.concatenate([tabs[0:32, :], tabs[32:64, :]], 1),) + shared,
        roll,
    )
    for cr in range(8):
        send3[pl.ds(cr, 16, stride=8), :] = lines[cr]
    recv3[rows8(8 * m0, 8), :] = send3[rows8(8 * gx, 8), :]
    over_column(
        lambda m, target: remote(
            send3.at[rows8(8 * (m // 2), 8)], recv3.at[rows8(8 * m0, 8)], pair(2), target
        ).start()
    )

    wait_bytes(line1.at[pl.ds(0, 32)], rsem.at[5])
    lines = line_stage(
        [line1[pl.ds(r, 16, stride=4), :] for r in range(4)],
        lambda c, p, r: ks[64 * (2 * c + p) + 16 * r : 64 * (2 * c + p) + 16 * r + 16, :],
        (
            jnp.concatenate([tabs[pl.ds(0, 16, stride=2), :], tabs[pl.ds(32, 16, stride=2), :]], 1),
        )
        + shared,
        roll,
    )
    for cr in range(8):
        here, there = lines[cr][:8], lines[cr][8:]
        own3[pl.ds(cr, 8, stride=8), :] = jnp.where(zh == 0, here, there)
        hop2[pl.ds(cr, 8, stride=8), :] = jnp.where(zh == 0, there, here)
    remote(hop2, other3, pair(6), far).start()
    recvs[rows8(32 * n0 + 16 * zh, 16), :] = own3[rows8(16 * xx, 16), :]
    over_plane(
        lambda n: remote(
            own3.at[rows8(16 * (n // 4), 16)],
            recvs.at[rows8(32 * n0 + 16 * zh, 16)], pair(7), plane_id(zh, n),
        ).start()
    )

    arrivals = (
        (gx > 0, hx_lo, 0), (gx < 15, hx_hi, 1), (gy > 0, hy_lo, 2), (gy < 7, hy_hi, 3),
        (gz > 0, field.at[:, pl.ds(0, 64)], 4), (gz < 3, field.at[:, pl.ds(1088, 64)], 5),
    )
    for there, ref, i in arrivals:

        @pl.when(there)
        def _(ref=ref, i=i):
            wait_bytes(ref, hrecv.at[i])

    sub = _iota((64, 128), 0)

    def exchange(z, carry):
        def slab(c, step):
            return field[c, rows8(64 + 64 * (z + step), 64), :]

        def around(c):
            at = 16 * c + z
            center = slab(c, 0)
            below = jnp.where(sub == 0, hx_lo[pl.ds(at, 1), :], pltpu.roll(center, 1, 0))
            above = jnp.where(sub == 63, hx_hi[pl.ds(at, 1), :], pltpu.roll(center, 63, 0))
            left = jnp.where(lane == 0, pltpu.roll(hy_lo[...], 128 - at, 1), pltpu.roll(center, 1, 1))
            right = jnp.where(
                lane == 127, pltpu.roll(hy_hi[...], 126 - at, 1), pltpu.roll(center, 127, 1)
            )
            return center, (slab(c, -1), slab(c, 1), below, above, left, right)

        a, near = around(3)
        weights = [4.0 * a * b / (a + b) for b in near]
        for c in range(3):
            m, beside = around(c)
            total = weights[0] * (m - beside[0])
            for w, b in zip(weights[1:], beside[1:]):
                total = total + w * (m - b)
            exch[c, rows8(64 * z, 64), :] = total
        return carry

    lax.fori_loop(0, 16, exchange, 0)

    wait_bytes(other3, rsem.at[6])
    recvs[rows8(32 * n0 + 16 * (1 - zh), 16), :] = other3[rows8(16 * xx, 16), :]
    over_plane(
        lambda n: remote(
            other3.at[rows8(16 * (n // 4), 16)],
            recvs.at[rows8(32 * n0 + 16 * (1 - zh), 16)], pair(8), plane_id(zh, n),
        ).start()
    )

    wait_bytes(recv3.at[pl.ds(0, 248)], rsem.at[2])
    folded = fold_stage([recv3[pl.ds(cr, 32, stride=8), :] for cr in range(8)], tabs[384:448, :32], roll)
    for cr in range(8):
        send4[pl.ds(cr, 16, stride=16), :] = folded[cr][:16]
        send4[pl.ds(8 + cr, 16, stride=16), :] = folded[cr][16:]
    recv4[rows8(16 * n0, 16), :] = send4[rows8(16 * n0, 16), :]
    over_plane(
        lambda n: remote(
            send4.at[rows8(16 * n, 16)], recv4.at[rows8(16 * n0, 16)], pair(3), plane_id(zh, n)
        ).start()
    )

    wait_bytes(recvs.at[pl.ds(0, 240)], rsem.at[7])
    wait_bytes(recvs.at[pl.ds(0, 240)], rsem.at[8])
    columns = [
        jnp.concatenate([recvs[pl.ds(8 * e + 4 * c + r, 32, stride=16), :] for r in range(4)], 0)
        for c in range(2)
        for e in range(2)
    ]
    g = _dot(table_side_last, jnp.concatenate(columns, 1))
    low = _iota((16, 128), 1) < 64
    for c in range(2):
        halves = [
            g[:16, 128 * q : 128 * q + 128] - roll(g[16:, 128 * q : 128 * q + 128], 64)
            for q in (2 * c, 2 * c + 1)
        ]
        side = jnp.where(low, halves[0], roll(halves[1], 64))
        for z in range(16):
            rows = slice(64 * z, 64 * z + 64)
            exch[c + 1, rows, :] = exch[c + 1, rows, :] + side[z : z + 1, :]

    wait_bytes(recv4.at[pl.ds(0, 240)], rsem.at[3])
    for a in range(2):
        rows = [
            jnp.concatenate(
                [recv4[pl.ds(8 * a + 4 * c + r, 16, stride=16), :] for r in range(4)], 0
            )
            for c in range(2)
        ]
        send5[pl.ds(a, 16, stride=2), :] = last_stage(table_last[a], rows, roll)
    recv5[rows8(8 * n0, 8), :] = send5[rows8(8 * xx, 8), :]
    over_plane(
        lambda n: remote(
            send5.at[rows8(8 * (n // 4), 8)], recv5.at[rows8(8 * n0, 8)], pair(4), plane_id(zh, n)
        ).start()
    )

    wait_bytes(recv1.at[pl.ds(0, 240)], ssem.at[0])
    wait_bytes(recv1s.at[pl.ds(0, 240)], ssem.at[9])
    wait_bytes(send2.at[pl.ds(0, 31)], ssem.at[1])
    wait_bytes(recv3.at[pl.ds(0, 248)], ssem.at[2])
    wait_bytes(recv4.at[pl.ds(0, 240)], ssem.at[3])
    wait_bytes(hop1, ssem.at[5])
    wait_bytes(hop2, ssem.at[6])
    wait_bytes(recvs.at[pl.ds(0, 240)], ssem.at[7])
    wait_bytes(recvs.at[pl.ds(0, 240)], ssem.at[8])
    for there, copy in faces:

        @pl.when(there)
        def _(copy=copy):
            copy.wait_send()

    wait_bytes(recv5.at[pl.ds(0, 120)], rsem.at[4])
    lines_y = jnp.concatenate([recv5[pl.ds(q, 16, stride=8), :] for q in range(8)], 0)
    top[0:128, :] = lines_y.T
    top[128:192, :] = zero_face
    wait_bytes(recv5.at[pl.ds(0, 120)], ssem.at[4])


def on_device(magnetization, stiffness, residual_top, residual_side, top_kernel, side_kernel):
    tables = jnp.asarray(const_tables())
    vmem = pl.BlockSpec(memory_space=pltpu.VMEM)
    hbm = pl.BlockSpec(memory_space=pltpu.HBM)

    def pin(array):
        return pltpu.with_memory_space_constraint(array, pltpu.HBM)

    def buf(*shape):
        return pltpu.VMEM(shape, F32)

    scratch = [
        buf(4, 1152, 128), buf(32, 64), buf(16, 128), buf(448, 128), buf(2, 2, 2, 4, 2048), buf(256, 128), buf(256, 128),
        buf(16, 128), buf(256, 128), buf(256, 128), buf(32, 4, 128), buf(32, 4, 128),
        buf(128, 128), buf(256, 128), buf(256, 128), buf(256, 128), buf(32, 128), buf(128, 128),
        buf(32, 128), buf(64, 128), buf(64, 128), buf(64, 128), buf(64, 128), buf(512, 128),
        buf(64, 128), buf(64, 128), buf(64, 128), buf(64, 128),
        buf(64, 128), buf(64, 128), buf(64, 128), buf(64, 128),
        pltpu.SemaphoreType.DMA((7,)), pltpu.SemaphoreType.DMA((10,)), pltpu.SemaphoreType.DMA((10,)),
        pltpu.SemaphoreType.DMA((6,)), pltpu.SemaphoreType.DMA((6,)),
    ]
    exch, top = pl.pallas_call(
        body,
        out_shape=[
            jax.ShapeDtypeStruct((3, 1024, 128), F32),
            jax.ShapeDtypeStruct((192, 128), F32),
        ],
        in_specs=[hbm] * 7,
        out_specs=[vmem] * 2,
        scratch_shapes=scratch,
        compiler_params=pltpu.CompilerParams(
            collective_id=0, has_side_effects=True, vmem_limit_bytes=40 * 1024 * 1024
        ),
        name="adjoint",
    )(
        pin(magnetization.reshape(3, 1024, 128)),
        pin(stiffness.reshape(1, 1024, 128)),
        pin(residual_top.T),
        pin(residual_side.T),
        pin(top_kernel),
        pin(side_kernel),
        pin(tables),
    )
    return exch.reshape(3, 16, 64, 128) + top.reshape(3, 1, 64, 128)


def solution(mesh):
    placed = (
        P(None, "gz", "gx", "gy"),
        P("gz", "gx", "gy"),
        P("gx", ("gy", "gz")),
        P("gy", "gz"),
        P(None, None, ("gx", "gy", "gz"), None),
        P(None, None, ("gy", "gz"), None),
    )
    return jax.shard_map(
        on_device, mesh=mesh, in_specs=placed, out_specs=P(None, "gz", "gx", "gy"), check_vma=False
    )
```

```python
import math

import jax
import jax.numpy as jnp
import numpy as np
from jax import lax
from jax.experimental import pallas as pl
from jax.experimental.pallas import tpu as pltpu
from jax.sharding import PartitionSpec as P

F32 = jnp.float32
MESH = pl.DeviceIdType.MESH
TOP_SCALE = 1.0 / 2048.0**2
SIDE_SCALE = 1.0 / (2048.0 * 128.0)


BF16 = jnp.bfloat16


def _split(x):
    high = x.astype(BF16)
    return high, (x - high.astype(F32)).astype(BF16)


def _left(table, axis=1):
    high, low = _split(table)
    return jnp.concatenate([high, high, low], axis)


def _right(value, axis=0):
    high, low = _split(value)
    return jnp.concatenate([high, low, high], axis)


def _mul(a, b, ca=1, cb=0):
    return lax.dot_general(a, b, (((ca,), (cb,)), ((), ())), preferred_element_type=F32)


def _cs(first, second, modulus):
    angle = 2.0 * np.pi * ((first * second) % modulus) / modulus
    return np.cos(angle), np.sin(angle)


def const_tables():
    i = np.arange
    c, s = _cs(i(16)[:, None], i(128)[None, :], 32)
    gl16 = np.concatenate([c, s], 1)
    gl32 = np.repeat(gl16, 2, axis=0)
    c, s = _cs(i(64)[:, None], i(128)[None, :], 2048)
    twist = np.concatenate([c, s], 0)
    c, s = _cs(i(16)[:, None], i(64)[None, :], 16)
    fwd = np.block([[c, s], [-s, c]])
    inv = np.block([[c.T, -s.T], [s.T, c.T]])
    back = gl16.reshape(16, 2, 128).transpose(1, 0, 2).reshape(32, 128)
    c, s = _cs(i(32)[:, None], i(32)[None, :], 32)
    fold = np.concatenate([c, s], 0)
    turn = twist.astype(np.float32)
    split = [split3(gl32, 0), split3(gl16, 0), split3(fwd, 1), split3(inv, 1), split3(back, 1), split3(fold, 1)]
    return [turn] + split


def split3(table, axis):
    table = table.astype(np.float32)
    high = table.astype(BF16)
    low = (table - high.astype(np.float32)).astype(BF16)
    return np.concatenate([high, high, low], axis)


def _iota(shape, dim):
    return lax.broadcasted_iota(jnp.int32, shape, dim)


def _angle(product, modulus):
    return (product & (modulus - 1)).astype(F32) * (2.0 * math.pi / modulus)


def first_table(zh, n0):
    row = _iota((128, 256), 0)
    col = _iota((128, 256), 1)
    ky = 64 * (row // 4) + row % 4 + 4 * n0
    y = 32 * (col // 16) + col % 16 + 512 * zh
    parts = []
    for h in (0, 1):
        t = _angle(ky * (y + 16 * h), 2048)
        parts += [_left(jnp.cos(t)), _left(-jnp.sin(t))]
    return parts


def last_table(zh, n0):
    row = _iota((16, 64), 0)
    col = _iota((16, 64), 1)
    s = 4 * (col % 16) + col // 16
    out = []
    for a in (0, 1):
        t = _angle(s * (32 * row + n0 + 16 * a + 512 * zh), 2048)
        out.append(_left(jnp.concatenate([jnp.cos(t) * TOP_SCALE, jnp.sin(t) * TOP_SCALE], 0)))
    return out


def side_table(zh, n0):
    row = _iota((16, 64), 0)
    z = _iota((16, 64), 1)
    own = jnp.where(row < 8, zh, 1 - zh)
    t = _angle((64 * own + 4 * n0 + row % 4) * z, 128)
    return _left(jnp.where(row % 8 < 4, jnp.cos(t), -jnp.sin(t)))


def side_last_table(yy):
    row = _iota((16, 128), 0)
    col = _iota((16, 128), 1)
    kz = 64 * (col % 2) + 4 * ((col // 2) % 16) + col // 32
    t = _angle(kz * (row + 16 * yy), 128)
    return _left(jnp.concatenate([jnp.cos(t) * SIDE_SCALE, jnp.sin(t) * SIDE_SCALE], 0))


def first_stage(w, packed, roll):
    packed = _right(packed)
    p = [_mul(t, packed) for t in w]
    low = _iota((128, 128), 1) < 64
    return jnp.where(low, p[0] + roll(p[2], 64), roll(p[1], 64) + p[3])


def side_first(w, data, roll):
    t = _mul(w, _right(data))
    low = _iota((4, 128), 1) < 64
    own, other = [], []
    for x in range(4):
        for base, out in ((0, own), (8, other)):
            o = t[base : base + 8, 128 * x : 128 * x + 128]
            q = roll(o, 64)
            f0 = jnp.where(low, o[0:4], q[4:8])
            f1 = jnp.where(low, q[0:4], o[4:8])
            out.append(jnp.concatenate([f0, f1], 0))
    return own, other


def line_stage(rows, kernel_at, tabs, roll):
    gl, twist, fwd, inv, back = tabs
    twc, tws = twist[:64], twist[64:]
    p = _mul(_right(jnp.concatenate(rows, 1)), gl, 0, 0)
    mid = []
    for r in range(4):
        q = p[128 * r : 128 * r + 128]
        bre = q[:64, :128] + q[64:, 128:]
        bim = q[64:, :128] - q[:64, 128:]
        mid.append(jnp.concatenate([bre * twc + bim * tws, bim * twc - bre * tws], 0))
    spectrum = _mul(fwd, _right(jnp.concatenate(mid, 1)))
    weighted = []
    for c in range(2):
        for r in range(4):
            sre = spectrum[:16, 128 * r : 128 * r + 128]
            sim = spectrum[16:, 128 * r : 128 * r + 128]
            kre, kim = kernel_at(c, 0, r), kernel_at(c, 1, r)
            weighted.append(
                jnp.concatenate([kre * sre + kim * sim, kre * sim - kim * sre], 0)
            )
    v = _mul(inv, _right(jnp.concatenate(weighted, 1)))
    turned = []
    for cr in range(8):
        vre = v[:64, 128 * cr : 128 * cr + 128]
        vim = v[64:, 128 * cr : 128 * cr + 128]
        turned += [vre * twc - vim * tws, vim * twc + vre * tws]
    u = _mul(back, _right(jnp.concatenate(turned, 0), 1), 1, 1)
    return spread(u, 16, roll)


def spread(u, half, roll):
    sign = jnp.where(_iota((half, 128), 1) < 64, -1.0, 1.0)
    out = []
    for cr in range(8):
        lanes = slice(128 * cr, 128 * cr + 128)
        out.append(u[:half, lanes] + sign * roll(u[half:, lanes], 64))
    return out


def fold_stage(rows, fold, roll):
    return spread(_mul(fold, _right(jnp.concatenate(rows, 1))), 32, roll)


def last_stage(table, rows, roll):
    g = _mul(table, _right(jnp.concatenate(rows, 1)))
    low = _iota((16, 128), 1) < 64
    part = [g[:16, 128 * c : 128 * c + 128] - roll(g[16:, 128 * c : 128 * c + 128], 64) for c in (0, 1)]
    return jnp.where(low, part[0], roll(part[1], 64))


def plane_id(zh, n):
    return {"gy": 4 * zh + n // 4, "gz": n % 4}


def ring_place(v):
    z = v // 2
    return 2 * (z % 8) + v % 2, z // 8


def rows8(start, size):
    return pl.ds(pl.multiple_of(start, 8), size)


def body(
    mag, stiff, rtop_in, rside_in, ktop, kside, c_turn, c_gl32, c_gl16, c_fwd, c_inv, c_back, c_fold,
    exch, top,
    field, rtop, rside, twist, gl32, gl16, fwd, inv, back, fold, kraw, kt, ks,
    send1, recv1, recv1s, send2, recv2, send3, recv3, send4, recv4, send5, recv5,
    hop1, line1, own3, hop2, other3, recvs,
    hx_out_hi, hx_out_lo, hx_lo, hx_hi, hy_out_hi, hy_out_lo, hy_lo, hy_hi,
    local, ssem, rsem, hsend, hrecv,
):
    gx, gy, gz = lax.axis_index("gx"), lax.axis_index("gy"), lax.axis_index("gz")
    zh, xx = gy // 4, gy % 4
    n0 = 4 * xx + gz
    m0 = 2 * gx + zh
    v0 = 2 * (8 * zh + gx // 2) + gx % 2
    crosses = jnp.logical_or(gy == 3, gy == 4)
    far = {"gx": (gx + 8) % 16, "gy": 4 * (1 - zh) + xx}

    def roll(value, shift):
        return pltpu.roll(value, shift, 1)

    def over_plane(action):
        def step(k, carry):
            action((n0 + k) % 16)
            return carry

        lax.fori_loop(1, 16, step, 0)

    def over_column(action):
        def step(k, carry):
            half = (k + 1) // 2
            off = jnp.where(k % 2 == 1, 16 - half, 16 + half)
            px, ph = ring_place((v0 + off) % 32)
            action(2 * px + ph, {"gx": px, "gy": 4 * ph + xx})
            return carry

        lax.fori_loop(0, 31, step, 0)

    def remote(src, dst, sems, target):
        send_sem, recv_sem = sems
        return pltpu.make_async_remote_copy(
            src_ref=src, dst_ref=dst, send_sem=send_sem, recv_sem=recv_sem,
            device_id=target, device_id_type=MESH,
        )

    def wait_bytes(ref, sem):
        pltpu.make_async_copy(ref, ref, sem).wait()

    def pair(i):
        return ssem.at[i], rsem.at[i]

    residuals = [
        pltpu.make_async_copy(rtop_in, rtop, local.at[4]),
        pltpu.make_async_copy(rside_in, rside, local.at[5]),
    ]
    loads = [
        pltpu.make_async_copy(src, dst, local.at[6 + i])
        for i, (src, dst) in enumerate(
            [(c_turn, twist), (c_gl32, gl32), (c_gl16, gl16), (c_fwd, fwd), (c_inv, inv), (c_back, back), (c_fold, fold)]
        )
    ] + [
        pltpu.make_async_copy(mag, field.at[0:3, pl.ds(64, 1024)], local.at[0]),
        pltpu.make_async_copy(stiff, field.at[3:4, pl.ds(64, 1024)], local.at[1]),
        pltpu.make_async_copy(ktop, kraw.at[0], local.at[2]),
        pltpu.make_async_copy(kside, kraw.at[1], local.at[3]),
    ]
    for load in residuals + loads:
        load.start()
    barrier = pltpu.get_barrier_semaphore()
    over_plane(
        lambda n: pl.semaphore_signal(barrier, inc=1, device_id=plane_id(zh, n), device_id_type=MESH)
    )
    over_column(
        lambda m, target: pl.semaphore_signal(barrier, inc=1, device_id=target, device_id_type=MESH)
    )

    @pl.when(crosses)
    def _():
        pl.semaphore_signal(barrier, inc=1, device_id={"gy": 7 - gy}, device_id_type=MESH)

    for load in residuals:
        load.wait()
    send1[...] = jnp.concatenate([rtop[0:16, :], rtop[16:32, :]], 1)
    recv1[rows8(16 * n0, 16), :] = send1[...]
    recv1s[rows8(16 * n0, 16), :] = rside[...]

    pl.semaphore_wait(barrier, 46 + crosses.astype(jnp.int32))

    over_plane(
        lambda n: remote(send1, recv1.at[rows8(16 * n0, 16)], pair(0), plane_id(zh, n)).start()
    )
    over_plane(
        lambda n: remote(rside, recv1s.at[rows8(16 * n0, 16)], pair(9), plane_id(zh, n)).start()
    )

    for load in loads:
        load.wait()
    zero_face = jnp.zeros((64, 128), F32)
    for c in range(4):
        hx_out_hi[16 * c : 16 * c + 16, :] = field[c, pl.ds(64 + 63, 16, stride=64), :]
        hx_out_lo[16 * c : 16 * c + 16, :] = field[c, pl.ds(64, 16, stride=64), :]
    lane = _iota((64, 128), 1)

    def pack(z, carry):
        hi, lo = carry
        for c in range(4):
            at = 16 * c + z
            turned = pltpu.roll(field[c, rows8(64 + 64 * z, 64), :], at + 1, 1)
            hi = jnp.where(lane == at, turned, hi)
            lo = jnp.where(lane == at + 1, turned, lo)
        return hi, lo

    packed_hi, packed_lo = lax.fori_loop(0, 16, pack, (zero_face, zero_face))
    hy_out_hi[...] = packed_hi
    hy_out_lo[...] = packed_lo

    x_up = (gx < 15, remote(hx_out_hi, hx_lo, (hsend.at[0], hrecv.at[0]), {"gx": (gx + 1) % 16}))
    x_dn = (gx > 0, remote(hx_out_lo, hx_hi, (hsend.at[1], hrecv.at[1]), {"gx": (gx + 15) % 16}))
    y_up = (gy < 7, remote(hy_out_hi, hy_lo, (hsend.at[2], hrecv.at[2]), {"gy": (gy + 1) % 8}))
    y_dn = (gy > 0, remote(hy_out_lo, hy_hi, (hsend.at[3], hrecv.at[3]), {"gy": (gy + 7) % 8}))
    z_up = (
        gz < 3,
        remote(field.at[:, pl.ds(1024, 64)], field.at[:, pl.ds(0, 64)],
               (hsend.at[4], hrecv.at[4]), {"gz": (gz + 1) % 4}),
    )
    z_dn = (
        gz > 0,
        remote(field.at[:, pl.ds(64, 64)], field.at[:, pl.ds(1088, 64)],
               (hsend.at[5], hrecv.at[5]), {"gz": (gz + 3) % 4}),
    )
    faces = (y_up, y_dn, z_up, z_dn, x_up, x_dn)
    for there, copy in faces:

        @pl.when(there)
        def _(copy=copy):
            copy.start()

    for missing, ref in ((gx == 0, hx_lo), (gx == 15, hx_hi), (gy == 0, hy_lo), (gy == 7, hy_hi)):

        @pl.when(missing)
        def _(ref=ref):
            ref[...] = zero_face

    for missing, start in ((gz == 0, 0), (gz == 3, 1088)):

        @pl.when(missing)
        def _(start=start):
            for c in range(4):
                field[c, pl.ds(start, 64), :] = zero_face

    for which, out in ((0, kt), (1, ks)):
        for cp in range(4):
            for j in range(16):
                out[pl.ds(64 * cp + j, 4, stride=16), :] = kraw[
                    which, cp // 2, cp % 2, :, 128 * j : 128 * j + 128
                ]

    table1 = first_table(zh, n0)
    table_side = side_table(zh, n0)
    table_last = last_table(zh, n0)
    table_side_last = side_last_table(gz)

    wait_bytes(recv1.at[pl.ds(0, 240)], rsem.at[0])
    first = first_stage(table1, recv1[...], roll)
    for m in range(32):
        send2[m] = first[4 * m : 4 * m + 4]
    recv2[m0] = send2[m0]
    over_column(lambda m, target: remote(send2.at[m], recv2.at[m0], pair(1), target).start())

    wait_bytes(recv1s.at[pl.ds(0, 240)], rsem.at[9])
    data = jnp.concatenate([recv1s[64 * x : 64 * x + 64, :] for x in range(4)], 1)
    own, other = side_first(table_side, data, roll)
    for x in range(4):
        line1[rows8(32 * zh + 8 * x, 8), :] = own[x]
        hop1[8 * x : 8 * x + 8, :] = other[x]
    remote(hop1, line1.at[rows8(32 * zh, 32)], pair(5), far).start()

    wait_bytes(recv2.at[pl.ds(0, 31)], rsem.at[1])
    shared = (twist[...], fwd[...], inv[...], back[...])
    lines = line_stage(
        [recv2[:, r, :] for r in range(4)],
        lambda c, p, r: kt[64 * (2 * c + p) + 16 * r : 64 * (2 * c + p) + 16 * r + 16, :],
        (gl32[...],) + shared,
        roll,
    )
    for cr in range(8):
        send3[pl.ds(cr, 16, stride=8), :] = lines[cr]
    recv3[rows8(8 * m0, 8), :] = send3[rows8(8 * gx, 8), :]
    over_column(
        lambda m, target: remote(
            send3.at[rows8(8 * (m // 2), 8)], recv3.at[rows8(8 * m0, 8)], pair(2), target
        ).start()
    )

    wait_bytes(line1.at[pl.ds(0, 32)], rsem.at[5])
    lines = line_stage(
        [line1[pl.ds(r, 16, stride=4), :] for r in range(4)],
        lambda c, p, r: ks[64 * (2 * c + p) + 16 * r : 64 * (2 * c + p) + 16 * r + 16, :],
        (gl16[...],) + shared,
        roll,
    )
    for cr in range(8):
        here, there = lines[cr][:8], lines[cr][8:]
        own3[pl.ds(cr, 8, stride=8), :] = jnp.where(zh == 0, here, there)
        hop2[pl.ds(cr, 8, stride=8), :] = jnp.where(zh == 0, there, here)
    remote(hop2, other3, pair(6), far).start()
    recvs[rows8(32 * n0 + 16 * zh, 16), :] = own3[rows8(16 * xx, 16), :]
    over_plane(
        lambda n: remote(
            own3.at[rows8(16 * (n // 4), 16)],
            recvs.at[rows8(32 * n0 + 16 * zh, 16)], pair(7), plane_id(zh, n),
        ).start()
    )

    arrivals = (
        (gx > 0, hx_lo, 0), (gx < 15, hx_hi, 1), (gy > 0, hy_lo, 2), (gy < 7, hy_hi, 3),
        (gz > 0, field.at[:, pl.ds(0, 64)], 4), (gz < 3, field.at[:, pl.ds(1088, 64)], 5),
    )
    for there, ref, i in arrivals:

        @pl.when(there)
        def _(ref=ref, i=i):
            wait_bytes(ref, hrecv.at[i])

    sub = _iota((64, 128), 0)

    def exchange(z, carry):
        def slab(c, step):
            return field[c, rows8(64 + 64 * (z + step), 64), :]

        def around(c):
            at = 16 * c + z
            center = slab(c, 0)
            below = jnp.where(sub == 0, hx_lo[pl.ds(at, 1), :], pltpu.roll(center, 1, 0))
            above = jnp.where(sub == 63, hx_hi[pl.ds(at, 1), :], pltpu.roll(center, 63, 0))
            left = jnp.where(lane == 0, pltpu.roll(hy_lo[...], 128 - at, 1), pltpu.roll(center, 1, 1))
            right = jnp.where(
                lane == 127, pltpu.roll(hy_hi[...], 126 - at, 1), pltpu.roll(center, 127, 1)
            )
            return center, (slab(c, -1), slab(c, 1), below, above, left, right)

        a, near = around(3)
        weights = [4.0 * a * b / (a + b) for b in near]
        for c in range(3):
            m, beside = around(c)
            total = weights[0] * (m - beside[0])
            for w, b in zip(weights[1:], beside[1:]):
                total = total + w * (m - b)
            exch[c, rows8(64 * z, 64), :] = total
        return carry

    lax.fori_loop(0, 16, exchange, 0)

    wait_bytes(other3, rsem.at[6])
    recvs[rows8(32 * n0 + 16 * (1 - zh), 16), :] = other3[rows8(16 * xx, 16), :]
    over_plane(
        lambda n: remote(
            other3.at[rows8(16 * (n // 4), 16)],
            recvs.at[rows8(32 * n0 + 16 * (1 - zh), 16)], pair(8), plane_id(zh, n),
        ).start()
    )

    wait_bytes(recv3.at[pl.ds(0, 248)], rsem.at[2])
    folded = fold_stage([recv3[pl.ds(cr, 32, stride=8), :] for cr in range(8)], fold[...], roll)
    for cr in range(8):
        send4[pl.ds(cr, 16, stride=16), :] = folded[cr][:16]
        send4[pl.ds(8 + cr, 16, stride=16), :] = folded[cr][16:]
    recv4[rows8(16 * n0, 16), :] = send4[rows8(16 * n0, 16), :]
    over_plane(
        lambda n: remote(
            send4.at[rows8(16 * n, 16)], recv4.at[rows8(16 * n0, 16)], pair(3), plane_id(zh, n)
        ).start()
    )

    wait_bytes(recvs.at[pl.ds(0, 240)], rsem.at[7])
    wait_bytes(recvs.at[pl.ds(0, 240)], rsem.at[8])
    columns = [
        jnp.concatenate([recvs[pl.ds(8 * e + 4 * c + r, 32, stride=16), :] for r in range(4)], 0)
        for c in range(2)
        for e in range(2)
    ]
    g = _mul(table_side_last, _right(jnp.concatenate(columns, 1)))
    low = _iota((16, 128), 1) < 64
    for c in range(2):
        halves = [
            g[:16, 128 * q : 128 * q + 128] - roll(g[16:, 128 * q : 128 * q + 128], 64)
            for q in (2 * c, 2 * c + 1)
        ]
        side = jnp.where(low, halves[0], roll(halves[1], 64))
        for z in range(16):
            rows = slice(64 * z, 64 * z + 64)
            exch[c + 1, rows, :] = exch[c + 1, rows, :] + side[z : z + 1, :]

    wait_bytes(recv4.at[pl.ds(0, 240)], rsem.at[3])
    for a in range(2):
        rows = [
            jnp.concatenate(
                [recv4[pl.ds(8 * a + 4 * c + r, 16, stride=16), :] for r in range(4)], 0
            )
            for c in range(2)
        ]
        send5[pl.ds(a, 16, stride=2), :] = last_stage(table_last[a], rows, roll)
    recv5[rows8(8 * n0, 8), :] = send5[rows8(8 * xx, 8), :]
    over_plane(
        lambda n: remote(
            send5.at[rows8(8 * (n // 4), 8)], recv5.at[rows8(8 * n0, 8)], pair(4), plane_id(zh, n)
        ).start()
    )

    wait_bytes(recv1.at[pl.ds(0, 240)], ssem.at[0])
    wait_bytes(recv1s.at[pl.ds(0, 240)], ssem.at[9])
    wait_bytes(send2.at[pl.ds(0, 31)], ssem.at[1])
    wait_bytes(recv3.at[pl.ds(0, 248)], ssem.at[2])
    wait_bytes(recv4.at[pl.ds(0, 240)], ssem.at[3])
    wait_bytes(hop1, ssem.at[5])
    wait_bytes(hop2, ssem.at[6])
    wait_bytes(recvs.at[pl.ds(0, 240)], ssem.at[7])
    wait_bytes(recvs.at[pl.ds(0, 240)], ssem.at[8])
    for there, copy in faces:

        @pl.when(there)
        def _(copy=copy):
            copy.wait_send()

    wait_bytes(recv5.at[pl.ds(0, 120)], rsem.at[4])
    lines_y = jnp.concatenate([recv5[pl.ds(q, 16, stride=8), :] for q in range(8)], 0)
    top[0:128, :] = lines_y.T
    top[128:192, :] = zero_face
    wait_bytes(recv5.at[pl.ds(0, 120)], ssem.at[4])


def on_device(magnetization, stiffness, residual_top, residual_side, top_kernel, side_kernel):
    tables = [jnp.asarray(t) for t in const_tables()]
    vmem = pl.BlockSpec(memory_space=pltpu.VMEM)
    hbm = pl.BlockSpec(memory_space=pltpu.HBM)

    def pin(array):
        return pltpu.with_memory_space_constraint(array, pltpu.HBM)

    def buf(*shape):
        return pltpu.VMEM(shape, F32)

    scratch = [
        buf(4, 1152, 128), buf(32, 64), buf(16, 128), *[pltpu.VMEM(t.shape, t.dtype) for t in tables], buf(2, 2, 2, 4, 2048), buf(256, 128), buf(256, 128),
        buf(16, 128), buf(256, 128), buf(256, 128), buf(32, 4, 128), buf(32, 4, 128),
        buf(128, 128), buf(256, 128), buf(256, 128), buf(256, 128), buf(32, 128), buf(128, 128),
        buf(32, 128), buf(64, 128), buf(64, 128), buf(64, 128), buf(64, 128), buf(512, 128),
        buf(64, 128), buf(64, 128), buf(64, 128), buf(64, 128),
        buf(64, 128), buf(64, 128), buf(64, 128), buf(64, 128),
        pltpu.SemaphoreType.DMA((13,)), pltpu.SemaphoreType.DMA((10,)), pltpu.SemaphoreType.DMA((10,)),
        pltpu.SemaphoreType.DMA((6,)), pltpu.SemaphoreType.DMA((6,)),
    ]
    exch, top = pl.pallas_call(
        body,
        out_shape=[
            jax.ShapeDtypeStruct((3, 1024, 128), F32),
            jax.ShapeDtypeStruct((192, 128), F32),
        ],
        in_specs=[hbm] * (6 + len(tables)),
        out_specs=[vmem] * 2,
        scratch_shapes=scratch,
        compiler_params=pltpu.CompilerParams(
            collective_id=0, has_side_effects=True, vmem_limit_bytes=40 * 1024 * 1024
        ),
        name="adjoint",
    )(
        pin(magnetization.reshape(3, 1024, 128)),
        pin(stiffness.reshape(1, 1024, 128)),
        pin(residual_top.T),
        pin(residual_side.T),
        pin(top_kernel),
        pin(side_kernel),
        *[pin(t) for t in tables],
    )
    return exch.reshape(3, 16, 64, 128) + top.reshape(3, 1, 64, 128)


def solution(mesh):
    placed = (
        P(None, "gz", "gx", "gy"),
        P("gz", "gx", "gy"),
        P("gx", ("gy", "gz")),
        P("gy", "gz"),
        P(None, None, ("gx", "gy", "gz"), None),
        P(None, None, ("gy", "gz"), None),
    )
    return jax.shard_map(
        on_device, mesh=mesh, in_specs=placed, out_specs=P(None, "gz", "gx", "gy"), check_vma=False
    )
```

```python
import math

import jax
import jax.numpy as jnp
import numpy as np
from jax import lax
from jax.experimental import pallas as pl
from jax.experimental.pallas import tpu as pltpu
from jax.sharding import PartitionSpec as P

F32 = jnp.float32
MESH = pl.DeviceIdType.MESH
TOP_SCALE = 1.0 / 2048.0**2
SIDE_SCALE = 1.0 / (2048.0 * 128.0)


BF16 = jnp.bfloat16


def _split(x):
    high = x.astype(BF16)
    return high, (x - high.astype(F32)).astype(BF16)


def _left(table, axis=1):
    high, low = _split(table)
    return jnp.concatenate([high, high, low], axis)


def _right(value, axis=0):
    high, low = _split(value)
    return jnp.concatenate([high, low, high], axis)


def _mul(a, b, ca=1, cb=0):
    return lax.dot_general(a, b, (((ca,), (cb,)), ((), ())), preferred_element_type=F32)


def _cs(first, second, modulus):
    angle = 2.0 * np.pi * ((first * second) % modulus) / modulus
    return np.cos(angle), np.sin(angle)


def const_tables():
    i = np.arange
    c, s = _cs(i(16)[:, None], i(128)[None, :], 32)
    gl16 = np.concatenate([c, s], 1)
    gl32 = np.repeat(gl16, 2, axis=0)
    c, s = _cs(i(64)[:, None], i(128)[None, :], 2048)
    twist = np.concatenate([c, s], 0)
    c, s = _cs(i(16)[:, None], i(64)[None, :], 16)
    fwd = np.block([[c, s], [-s, c]])
    inv = np.block([[c.T, -s.T], [s.T, c.T]])
    back = gl16.reshape(16, 2, 128).transpose(1, 0, 2).reshape(32, 128)
    c, s = _cs(i(32)[:, None], i(32)[None, :], 32)
    fold = np.concatenate([c, s], 0)
    turn = twist.astype(np.float32)
    split = [split3(gl32, 0), split3(gl16, 0), split3(fwd, 1), split3(inv, 1), split3(back, 1), split3(fold, 1)]
    return [turn] + split


def split3(table, axis):
    table = table.astype(np.float32)
    high = table.astype(BF16)
    low = (table - high.astype(np.float32)).astype(BF16)
    return np.concatenate([high, high, low], axis)


def _iota(shape, dim):
    return lax.broadcasted_iota(jnp.int32, shape, dim)


def _angle(product, modulus):
    return (product & (modulus - 1)).astype(F32) * (2.0 * math.pi / modulus)


def first_table(zh, n0):
    row = _iota((128, 256), 0)
    col = _iota((128, 256), 1)
    ky = 64 * (row // 4) + row % 4 + 4 * n0
    y = 32 * (col // 16) + col % 16 + 512 * zh
    parts = []
    for h in (0, 1):
        t = _angle(ky * (y + 16 * h), 2048)
        parts += [_left(jnp.cos(t)), _left(-jnp.sin(t))]
    return parts


def last_table(zh, n0):
    row = _iota((16, 64), 0)
    col = _iota((16, 64), 1)
    s = 4 * (col % 16) + col // 16
    out = []
    for a in (0, 1):
        t = _angle(s * (32 * row + n0 + 16 * a + 512 * zh), 2048)
        out.append(_left(jnp.concatenate([jnp.cos(t) * TOP_SCALE, jnp.sin(t) * TOP_SCALE], 0)))
    return out


def side_table(zh, n0):
    row = _iota((16, 64), 0)
    z = _iota((16, 64), 1)
    own = jnp.where(row < 8, zh, 1 - zh)
    t = _angle((64 * own + 4 * n0 + row % 4) * z, 128)
    return _left(jnp.where(row % 8 < 4, jnp.cos(t), -jnp.sin(t)))


def side_last_table(yy):
    row = _iota((16, 128), 0)
    col = _iota((16, 128), 1)
    kz = 64 * (col % 2) + 4 * ((col // 2) % 16) + col // 32
    t = _angle(kz * (row + 16 * yy), 128)
    return _left(jnp.concatenate([jnp.cos(t) * SIDE_SCALE, jnp.sin(t) * SIDE_SCALE], 0))


def first_stage(w, packed, roll):
    packed = _right(packed)
    p = [_mul(t, packed) for t in w]
    low = _iota((128, 128), 1) < 64
    return jnp.where(low, p[0] + roll(p[2], 64), roll(p[1], 64) + p[3])


def side_first(w, data, roll):
    t = _mul(w, _right(data))
    low = _iota((4, 128), 1) < 64
    own, other = [], []
    for x in range(4):
        for base, out in ((0, own), (8, other)):
            o = t[base : base + 8, 128 * x : 128 * x + 128]
            q = roll(o, 64)
            f0 = jnp.where(low, o[0:4], q[4:8])
            f1 = jnp.where(low, q[0:4], o[4:8])
            out.append(jnp.concatenate([f0, f1], 0))
    return own, other


def line_stage(rows, kernel_at, tabs, roll):
    gl, twist, fwd, inv, back = tabs
    twc, tws = twist[:64], twist[64:]
    p = _mul(_right(jnp.concatenate(rows, 1)), gl, 0, 0)
    mid = []
    for r in range(4):
        q = p[128 * r : 128 * r + 128]
        bre = q[:64, :128] + q[64:, 128:]
        bim = q[64:, :128] - q[:64, 128:]
        mid.append(jnp.concatenate([bre * twc + bim * tws, bim * twc - bre * tws], 0))
    spectrum = _mul(fwd, _right(jnp.concatenate(mid, 1)))
    weighted = []
    for c in range(2):
        for r in range(4):
            sre = spectrum[:16, 128 * r : 128 * r + 128]
            sim = spectrum[16:, 128 * r : 128 * r + 128]
            kre, kim = kernel_at(c, 0, r), kernel_at(c, 1, r)
            weighted.append(
                jnp.concatenate([kre * sre + kim * sim, kre * sim - kim * sre], 0)
            )
    v = _mul(inv, _right(jnp.concatenate(weighted, 1)))
    turned = []
    for cr in range(8):
        vre = v[:64, 128 * cr : 128 * cr + 128]
        vim = v[64:, 128 * cr : 128 * cr + 128]
        turned += [vre * twc - vim * tws, vim * twc + vre * tws]
    u = _mul(back, _right(jnp.concatenate(turned, 0), 1), 1, 1)
    return spread(u, 16, roll)


def spread(u, half, roll):
    sign = jnp.where(_iota((half, 128), 1) < 64, -1.0, 1.0)
    out = []
    for cr in range(8):
        lanes = slice(128 * cr, 128 * cr + 128)
        out.append(u[:half, lanes] + sign * roll(u[half:, lanes], 64))
    return out


def fold_stage(rows, fold, roll):
    return spread(_mul(fold, _right(jnp.concatenate(rows, 1))), 32, roll)


def last_stage(table, rows, roll):
    g = _mul(table, _right(jnp.concatenate(rows, 1)))
    low = _iota((16, 128), 1) < 64
    part = [g[:16, 128 * c : 128 * c + 128] - roll(g[16:, 128 * c : 128 * c + 128], 64) for c in (0, 1)]
    return jnp.where(low, part[0], roll(part[1], 64))


def plane_id(zh, n):
    return {"gy": 4 * zh + n // 4, "gz": n % 4}


def ring_place(v):
    z = v // 2
    return 2 * (z % 8) + v % 2, z // 8


def rows8(start, size):
    return pl.ds(pl.multiple_of(start, 8), size)


def body(
    mag, stiff, rtop_in, rside_in, ktop, kside, c_turn, c_gl32, c_gl16, c_fwd, c_inv, c_back, c_fold,
    exch, top,
    field, rtop, rside, twist, gl32, gl16, fwd, inv, back, fold, kraw, kt, ks,
    send1, recv1, recv1s, send2, recv2, send3, recv3, send4, recv4, send5, recv5,
    hop1, line1, own3, hop2, other3, recvs,
    hx_out_hi, hx_out_lo, hx_lo, hx_hi, hy_out_hi, hy_out_lo, hy_lo, hy_hi,
    local, ssem, rsem, hsend, hrecv, near, cross,
):
    gx, gy, gz = lax.axis_index("gx"), lax.axis_index("gy"), lax.axis_index("gz")
    zh, xx = gy // 4, gy % 4
    n0 = 4 * xx + gz
    m0 = 2 * gx + zh
    v0 = 2 * (8 * zh + gx // 2) + gx % 2
    z, core = 8 * zh + gx // 2, gx % 2
    far = {"gx": (gx + 8) % 16, "gy": 4 * (1 - zh) + xx}

    def roll(value, shift):
        return pltpu.roll(value, shift, 1)

    def over_plane(action):
        def step(k, carry):
            action((n0 + k) % 16)
            return carry

        lax.fori_loop(1, 16, step, 0)

    def over_column(action):
        def step(k, carry):
            half = (k + 1) // 2
            off = jnp.where(k % 2 == 1, 16 - half, 16 + half)
            px, ph = ring_place((v0 + off) % 32)
            action(2 * px + ph, {"gx": px, "gy": 4 * ph + xx})
            return carry

        lax.fori_loop(0, 31, step, 0)

    def in_column(at, which):
        at = (at + 16) % 16
        return {"gx": 2 * (at % 8) + which, "gy": 4 * (at // 8) + xx}

    def signal(sem, target):
        pl.semaphore_signal(sem, inc=1, device_id=target, device_id_type=MESH)

    def remote(src, dst, sems, target):
        send_sem, recv_sem = sems
        return pltpu.make_async_remote_copy(
            src_ref=src, dst_ref=dst, send_sem=send_sem, recv_sem=recv_sem,
            device_id=target, device_id_type=MESH,
        )

    def wait_bytes(ref, sem):
        pltpu.make_async_copy(ref, ref, sem).wait()

    def pair(i):
        return ssem.at[i], rsem.at[i]

    residuals = [
        pltpu.make_async_copy(rtop_in, rtop, local.at[4]),
        pltpu.make_async_copy(rside_in, rside, local.at[5]),
    ]
    loads = [
        pltpu.make_async_copy(src, dst, local.at[6 + i])
        for i, (src, dst) in enumerate(
            [(c_turn, twist), (c_gl32, gl32), (c_gl16, gl16), (c_fwd, fwd), (c_inv, inv), (c_back, back), (c_fold, fold)]
        )
    ] + [
        pltpu.make_async_copy(mag, field.at[0:3, pl.ds(64, 1024)], local.at[0]),
        pltpu.make_async_copy(stiff, field.at[3:4, pl.ds(64, 1024)], local.at[1]),
        pltpu.make_async_copy(ktop, kraw.at[0], local.at[2]),
        pltpu.make_async_copy(kside, kraw.at[1], local.at[3]),
    ]
    for load in residuals + loads:
        load.start()
    barrier = pltpu.get_barrier_semaphore()
    over_plane(lambda n: signal(barrier, plane_id(zh, n)))

    def greet(k, carry):
        k = jnp.where(k < 8, k, k + 1)
        signal(barrier, in_column(z + k // 2 - 4, (core + k % 2) % 2))
        return carry

    lax.fori_loop(0, 17, greet, 0)

    for load in residuals:
        load.wait()
    send1[...] = jnp.concatenate([rtop[0:16, :], rtop[16:32, :]], 1)
    recv1[rows8(16 * n0, 16), :] = send1[...]
    recv1s[rows8(16 * n0, 16), :] = rside[...]

    pl.semaphore_wait(barrier, 32)

    over_plane(
        lambda n: remote(send1, recv1.at[rows8(16 * n0, 16)], pair(0), plane_id(zh, n)).start()
    )
    over_plane(
        lambda n: remote(rside, recv1s.at[rows8(16 * n0, 16)], pair(9), plane_id(zh, n)).start()
    )

    signal(near, in_column(z + 4, core))
    signal(near, in_column(z - 4, core))

    for load in loads:
        load.wait()
    zero_face = jnp.zeros((64, 128), F32)
    for c in range(4):
        hx_out_hi[16 * c : 16 * c + 16, :] = field[c, pl.ds(64 + 63, 16, stride=64), :]
        hx_out_lo[16 * c : 16 * c + 16, :] = field[c, pl.ds(64, 16, stride=64), :]
    lane = _iota((64, 128), 1)

    def pack(z, carry):
        hi, lo = carry
        for c in range(4):
            at = 16 * c + z
            turned = pltpu.roll(field[c, rows8(64 + 64 * z, 64), :], at + 1, 1)
            hi = jnp.where(lane == at, turned, hi)
            lo = jnp.where(lane == at + 1, turned, lo)
        return hi, lo

    packed_hi, packed_lo = lax.fori_loop(0, 16, pack, (zero_face, zero_face))
    hy_out_hi[...] = packed_hi
    hy_out_lo[...] = packed_lo

    x_up = (gx < 15, remote(hx_out_hi, hx_lo, (hsend.at[0], hrecv.at[0]), {"gx": (gx + 1) % 16}))
    x_dn = (gx > 0, remote(hx_out_lo, hx_hi, (hsend.at[1], hrecv.at[1]), {"gx": (gx + 15) % 16}))
    y_up = (gy < 7, remote(hy_out_hi, hy_lo, (hsend.at[2], hrecv.at[2]), {"gy": (gy + 1) % 8}))
    y_dn = (gy > 0, remote(hy_out_lo, hy_hi, (hsend.at[3], hrecv.at[3]), {"gy": (gy + 7) % 8}))
    z_up = (
        gz < 3,
        remote(field.at[:, pl.ds(1024, 64)], field.at[:, pl.ds(0, 64)],
               (hsend.at[4], hrecv.at[4]), {"gz": (gz + 1) % 4}),
    )
    z_dn = (
        gz > 0,
        remote(field.at[:, pl.ds(64, 64)], field.at[:, pl.ds(1088, 64)],
               (hsend.at[5], hrecv.at[5]), {"gz": (gz + 3) % 4}),
    )
    faces = (y_up, y_dn, z_up, z_dn, x_up, x_dn)
    inside = (
        (jnp.logical_and(gy < 7, gy != 3), y_up[1]),
        (jnp.logical_and(gy > 0, gy != 4), y_dn[1]),
    ) + faces[2:]
    for there, copy in inside:

        @pl.when(there)
        def _(copy=copy):
            copy.start()

    for missing, ref in ((gx == 0, hx_lo), (gx == 15, hx_hi), (gy == 0, hy_lo), (gy == 7, hy_hi)):

        @pl.when(missing)
        def _(ref=ref):
            ref[...] = zero_face

    for missing, start in ((gz == 0, 0), (gz == 3, 1088)):

        @pl.when(missing)
        def _(start=start):
            for c in range(4):
                field[c, pl.ds(start, 64), :] = zero_face

    for which, out in ((0, kt), (1, ks)):
        for cp in range(4):
            for j in range(16):
                out[pl.ds(64 * cp + j, 4, stride=16), :] = kraw[
                    which, cp // 2, cp % 2, :, 128 * j : 128 * j + 128
                ]

    table1 = first_table(zh, n0)
    table_side = side_table(zh, n0)
    table_last = last_table(zh, n0)
    table_side_last = side_last_table(gz)

    pl.semaphore_wait(near, 2)

    for at in (0, 7):

        @pl.when(gy == at)
        def _(at=at):
            signal(cross, {"gy": 3 if at == 0 else 4})

    wait_bytes(recv1.at[pl.ds(0, 240)], rsem.at[0])
    first = first_stage(table1, recv1[...], roll)
    for m in range(32):
        send2[m] = first[4 * m : 4 * m + 4]
    recv2[m0] = send2[m0]
    over_column(lambda m, target: remote(send2.at[m], recv2.at[m0], pair(1), target).start())

    for at, copy in ((3, y_up[1]), (4, y_dn[1])):

        @pl.when(gy == at)
        def _(copy=copy):
            pl.semaphore_wait(cross, 1)
            copy.start()

    wait_bytes(recv1s.at[pl.ds(0, 240)], rsem.at[9])
    data = jnp.concatenate([recv1s[64 * x : 64 * x + 64, :] for x in range(4)], 1)
    own, other = side_first(table_side, data, roll)
    for x in range(4):
        line1[rows8(32 * zh + 8 * x, 8), :] = own[x]
        hop1[8 * x : 8 * x + 8, :] = other[x]
    remote(hop1, line1.at[rows8(32 * zh, 32)], pair(5), far).start()

    wait_bytes(recv2.at[pl.ds(0, 31)], rsem.at[1])
    shared = (twist[...], fwd[...], inv[...], back[...])
    lines = line_stage(
        [recv2[:, r, :] for r in range(4)],
        lambda c, p, r: kt[64 * (2 * c + p) + 16 * r : 64 * (2 * c + p) + 16 * r + 16, :],
        (gl32[...],) + shared,
        roll,
    )
    for cr in range(8):
        send3[pl.ds(cr, 16, stride=8), :] = lines[cr]
    recv3[rows8(8 * m0, 8), :] = send3[rows8(8 * gx, 8), :]
    over_column(
        lambda m, target: remote(
            send3.at[rows8(8 * (m // 2), 8)], recv3.at[rows8(8 * m0, 8)], pair(2), target
        ).start()
    )

    wait_bytes(line1.at[pl.ds(0, 32)], rsem.at[5])
    lines = line_stage(
        [line1[pl.ds(r, 16, stride=4), :] for r in range(4)],
        lambda c, p, r: ks[64 * (2 * c + p) + 16 * r : 64 * (2 * c + p) + 16 * r + 16, :],
        (gl16[...],) + shared,
        roll,
    )
    for cr in range(8):
        here, there = lines[cr][:8], lines[cr][8:]
        own3[pl.ds(cr, 8, stride=8), :] = jnp.where(zh == 0, here, there)
        hop2[pl.ds(cr, 8, stride=8), :] = jnp.where(zh == 0, there, here)
    remote(hop2, other3, pair(6), far).start()
    recvs[rows8(32 * n0 + 16 * zh, 16), :] = own3[rows8(16 * xx, 16), :]
    over_plane(
        lambda n: remote(
            own3.at[rows8(16 * (n // 4), 16)],
            recvs.at[rows8(32 * n0 + 16 * zh, 16)], pair(7), plane_id(zh, n),
        ).start()
    )

    arrivals = (
        (gx > 0, hx_lo, 0), (gx < 15, hx_hi, 1), (gy > 0, hy_lo, 2), (gy < 7, hy_hi, 3),
        (gz > 0, field.at[:, pl.ds(0, 64)], 4), (gz < 3, field.at[:, pl.ds(1088, 64)], 5),
    )
    for there, ref, i in arrivals:

        @pl.when(there)
        def _(ref=ref, i=i):
            wait_bytes(ref, hrecv.at[i])

    sub = _iota((64, 128), 0)

    def exchange(z, carry):
        def slab(c, step):
            return field[c, rows8(64 + 64 * (z + step), 64), :]

        def around(c):
            at = 16 * c + z
            center = slab(c, 0)
            below = jnp.where(sub == 0, hx_lo[pl.ds(at, 1), :], pltpu.roll(center, 1, 0))
            above = jnp.where(sub == 63, hx_hi[pl.ds(at, 1), :], pltpu.roll(center, 63, 0))
            left = jnp.where(lane == 0, pltpu.roll(hy_lo[...], 128 - at, 1), pltpu.roll(center, 1, 1))
            right = jnp.where(
                lane == 127, pltpu.roll(hy_hi[...], 126 - at, 1), pltpu.roll(center, 127, 1)
            )
            return center, (slab(c, -1), slab(c, 1), below, above, left, right)

        a, near = around(3)
        weights = [4.0 * a * b / (a + b) for b in near]
        for c in range(3):
            m, beside = around(c)
            total = weights[0] * (m - beside[0])
            for w, b in zip(weights[1:], beside[1:]):
                total = total + w * (m - b)
            exch[c, rows8(64 * z, 64), :] = total
        return carry

    lax.fori_loop(0, 16, exchange, 0)

    wait_bytes(other3, rsem.at[6])
    recvs[rows8(32 * n0 + 16 * (1 - zh), 16), :] = other3[rows8(16 * xx, 16), :]
    over_plane(
        lambda n: remote(
            other3.at[rows8(16 * (n // 4), 16)],
            recvs.at[rows8(32 * n0 + 16 * (1 - zh), 16)], pair(8), plane_id(zh, n),
        ).start()
    )

    wait_bytes(recv3.at[pl.ds(0, 248)], rsem.at[2])
    folded = fold_stage([recv3[pl.ds(cr, 32, stride=8), :] for cr in range(8)], fold[...], roll)
    for cr in range(8):
        send4[pl.ds(cr, 16, stride=16), :] = folded[cr][:16]
        send4[pl.ds(8 + cr, 16, stride=16), :] = folded[cr][16:]
    recv4[rows8(16 * n0, 16), :] = send4[rows8(16 * n0, 16), :]
    over_plane(
        lambda n: remote(
            send4.at[rows8(16 * n, 16)], recv4.at[rows8(16 * n0, 16)], pair(3), plane_id(zh, n)
        ).start()
    )

    wait_bytes(recvs.at[pl.ds(0, 240)], rsem.at[7])
    wait_bytes(recvs.at[pl.ds(0, 240)], rsem.at[8])
    columns = [
        jnp.concatenate([recvs[pl.ds(8 * e + 4 * c + r, 32, stride=16), :] for r in range(4)], 0)
        for c in range(2)
        for e in range(2)
    ]
    g = _mul(table_side_last, _right(jnp.concatenate(columns, 1)))
    low = _iota((16, 128), 1) < 64
    for c in range(2):
        halves = [
            g[:16, 128 * q : 128 * q + 128] - roll(g[16:, 128 * q : 128 * q + 128], 64)
            for q in (2 * c, 2 * c + 1)
        ]
        side = jnp.where(low, halves[0], roll(halves[1], 64))
        for z in range(16):
            rows = slice(64 * z, 64 * z + 64)
            exch[c + 1, rows, :] = exch[c + 1, rows, :] + side[z : z + 1, :]

    wait_bytes(recv4.at[pl.ds(0, 240)], rsem.at[3])
    for a in range(2):
        rows = [
            jnp.concatenate(
                [recv4[pl.ds(8 * a + 4 * c + r, 16, stride=16), :] for r in range(4)], 0
            )
            for c in range(2)
        ]
        send5[pl.ds(a, 16, stride=2), :] = last_stage(table_last[a], rows, roll)
    recv5[rows8(8 * n0, 8), :] = send5[rows8(8 * xx, 8), :]
    over_plane(
        lambda n: remote(
            send5.at[rows8(8 * (n // 4), 8)], recv5.at[rows8(8 * n0, 8)], pair(4), plane_id(zh, n)
        ).start()
    )

    wait_bytes(recv1.at[pl.ds(0, 240)], ssem.at[0])
    wait_bytes(recv1s.at[pl.ds(0, 240)], ssem.at[9])
    wait_bytes(send2.at[pl.ds(0, 31)], ssem.at[1])
    wait_bytes(recv3.at[pl.ds(0, 248)], ssem.at[2])
    wait_bytes(recv4.at[pl.ds(0, 240)], ssem.at[3])
    wait_bytes(hop1, ssem.at[5])
    wait_bytes(hop2, ssem.at[6])
    wait_bytes(recvs.at[pl.ds(0, 240)], ssem.at[7])
    wait_bytes(recvs.at[pl.ds(0, 240)], ssem.at[8])
    for there, copy in faces:

        @pl.when(there)
        def _(copy=copy):
            copy.wait_send()

    wait_bytes(recv5.at[pl.ds(0, 120)], rsem.at[4])
    lines_y = jnp.concatenate([recv5[pl.ds(q, 16, stride=8), :] for q in range(8)], 0)
    top[0:128, :] = lines_y.T
    top[128:192, :] = zero_face
    wait_bytes(recv5.at[pl.ds(0, 120)], ssem.at[4])


def on_device(magnetization, stiffness, residual_top, residual_side, top_kernel, side_kernel):
    tables = [jnp.asarray(t) for t in const_tables()]
    vmem = pl.BlockSpec(memory_space=pltpu.VMEM)
    hbm = pl.BlockSpec(memory_space=pltpu.HBM)

    def pin(array):
        return pltpu.with_memory_space_constraint(array, pltpu.HBM)

    def buf(*shape):
        return pltpu.VMEM(shape, F32)

    scratch = [
        buf(4, 1152, 128), buf(32, 64), buf(16, 128), *[pltpu.VMEM(t.shape, t.dtype) for t in tables], buf(2, 2, 2, 4, 2048), buf(256, 128), buf(256, 128),
        buf(16, 128), buf(256, 128), buf(256, 128), buf(32, 4, 128), buf(32, 4, 128),
        buf(128, 128), buf(256, 128), buf(256, 128), buf(256, 128), buf(32, 128), buf(128, 128),
        buf(32, 128), buf(64, 128), buf(64, 128), buf(64, 128), buf(64, 128), buf(512, 128),
        buf(64, 128), buf(64, 128), buf(64, 128), buf(64, 128),
        buf(64, 128), buf(64, 128), buf(64, 128), buf(64, 128),
        pltpu.SemaphoreType.DMA((13,)), pltpu.SemaphoreType.DMA((10,)), pltpu.SemaphoreType.DMA((10,)),
        pltpu.SemaphoreType.DMA((6,)), pltpu.SemaphoreType.DMA((6,)),
        pltpu.SemaphoreType.REGULAR, pltpu.SemaphoreType.REGULAR,
    ]
    exch, top = pl.pallas_call(
        body,
        out_shape=[
            jax.ShapeDtypeStruct((3, 1024, 128), F32),
            jax.ShapeDtypeStruct((192, 128), F32),
        ],
        in_specs=[hbm] * (6 + len(tables)),
        out_specs=[vmem] * 2,
        scratch_shapes=scratch,
        compiler_params=pltpu.CompilerParams(
            collective_id=0, has_side_effects=True, vmem_limit_bytes=40 * 1024 * 1024
        ),
        name="adjoint",
    )(
        pin(magnetization.reshape(3, 1024, 128)),
        pin(stiffness.reshape(1, 1024, 128)),
        pin(residual_top.T),
        pin(residual_side.T),
        pin(top_kernel),
        pin(side_kernel),
        *[pin(t) for t in tables],
    )
    return exch.reshape(3, 16, 64, 128) + top.reshape(3, 1, 64, 128)


def solution(mesh):
    placed = (
        P(None, "gz", "gx", "gy"),
        P("gz", "gx", "gy"),
        P("gx", ("gy", "gz")),
        P("gy", "gz"),
        P(None, None, ("gx", "gy", "gz"), None),
        P(None, None, ("gy", "gz"), None),
    )
    return jax.shard_map(
        on_device, mesh=mesh, in_specs=placed, out_specs=P(None, "gz", "gx", "gy"), check_vma=False
    )
```

```python
import math

import jax
import jax.numpy as jnp
import numpy as np
from jax import lax
from jax.experimental import pallas as pl
from jax.experimental.pallas import tpu as pltpu
from jax.sharding import PartitionSpec as P

F32 = jnp.float32
LOGICAL = pl.DeviceIdType.LOGICAL
PLANE_ORDER = sorted(
    [(dx, dy) for dx in range(4) for dy in range(4) if dx or dy],
    key=lambda d: -(min(d[0], 4 - d[0]) + min(d[1], 4 - d[1])),
)
TOP_SCALE = 1.0 / 2048.0**2
SIDE_SCALE = 1.0 / (2048.0 * 128.0)


BF16 = jnp.bfloat16


def _split(x):
    high = x.astype(BF16)
    return high, (x - high.astype(F32)).astype(BF16)


def _left(table, axis=1):
    high, low = _split(table)
    return jnp.concatenate([high, high, low], axis)


def _right(value, axis=0):
    high, low = _split(value)
    return jnp.concatenate([high, low, high], axis)


def _mul(a, b, ca=1, cb=0):
    return lax.dot_general(a, b, (((ca,), (cb,)), ((), ())), preferred_element_type=F32)


def _cs(first, second, modulus):
    angle = 2.0 * np.pi * ((first * second) % modulus) / modulus
    return np.cos(angle), np.sin(angle)


def const_tables():
    i = np.arange
    c, s = _cs(i(16)[:, None], i(128)[None, :], 32)
    gl16 = np.concatenate([c, s], 1)
    gl32 = np.repeat(gl16, 2, axis=0)
    c, s = _cs(i(64)[:, None], i(128)[None, :], 2048)
    twist = np.concatenate([c, s], 0)
    c, s = _cs(i(16)[:, None], i(64)[None, :], 16)
    fwd = np.block([[c, s], [-s, c]])
    inv = np.block([[c.T, -s.T], [s.T, c.T]])
    back = gl16.reshape(16, 2, 128).transpose(1, 0, 2).reshape(32, 128)
    c, s = _cs(i(32)[:, None], i(32)[None, :], 32)
    fold = np.concatenate([c, s], 0)
    turn = twist.astype(np.float32)
    split = [split3(gl32, 0), split3(gl16, 0), split3(fwd, 1), split3(inv, 1), split3(back, 1), split3(fold, 1)]
    return [turn] + split


def split3(table, axis):
    table = table.astype(np.float32)
    high = table.astype(BF16)
    low = (table - high.astype(np.float32)).astype(BF16)
    return np.concatenate([high, high, low], axis)


def _iota(shape, dim):
    return lax.broadcasted_iota(jnp.int32, shape, dim)


def _angle(product, modulus):
    return (product & (modulus - 1)).astype(F32) * (2.0 * math.pi / modulus)


def first_table(zh, n0):
    row = _iota((128, 256), 0)
    col = _iota((128, 256), 1)
    ky = 64 * (row // 4) + row % 4 + 4 * n0
    y = 32 * (col // 16) + col % 16 + 512 * zh
    parts = []
    for h in (0, 1):
        t = _angle(ky * (y + 16 * h), 2048)
        parts += [_left(jnp.cos(t)), _left(-jnp.sin(t))]
    return parts


def last_table(zh, n0):
    row = _iota((16, 64), 0)
    col = _iota((16, 64), 1)
    s = 4 * (col % 16) + col // 16
    out = []
    for a in (0, 1):
        t = _angle(s * (32 * row + n0 + 16 * a + 512 * zh), 2048)
        out.append(_left(jnp.concatenate([jnp.cos(t) * TOP_SCALE, jnp.sin(t) * TOP_SCALE], 0)))
    return out


def side_table(zh, n0):
    row = _iota((16, 64), 0)
    z = _iota((16, 64), 1)
    own = jnp.where(row < 8, zh, 1 - zh)
    t = _angle((64 * own + 4 * n0 + row % 4) * z, 128)
    return _left(jnp.where(row % 8 < 4, jnp.cos(t), -jnp.sin(t)))


def side_last_table(yy):
    row = _iota((16, 128), 0)
    col = _iota((16, 128), 1)
    kz = 64 * (col % 2) + 4 * ((col // 2) % 16) + col // 32
    t = _angle(kz * (row + 16 * yy), 128)
    return _left(jnp.concatenate([jnp.cos(t) * SIDE_SCALE, jnp.sin(t) * SIDE_SCALE], 0))


def first_stage(w, packed, roll):
    packed = _right(packed)
    p = [_mul(t, packed) for t in w]
    low = _iota((128, 128), 1) < 64
    return jnp.where(low, p[0] + roll(p[2], 64), roll(p[1], 64) + p[3])


def side_first(w, data, roll):
    t = _mul(w, _right(data))
    low = _iota((4, 128), 1) < 64
    own, other = [], []
    for x in range(4):
        for base, out in ((0, own), (8, other)):
            o = t[base : base + 8, 128 * x : 128 * x + 128]
            q = roll(o, 64)
            f0 = jnp.where(low, o[0:4], q[4:8])
            f1 = jnp.where(low, q[0:4], o[4:8])
            out.append(jnp.concatenate([f0, f1], 0))
    return own, other


def line_stage(rows, kernel_at, tabs, roll):
    gl, twist, fwd, inv, back = tabs
    twc, tws = twist[:64], twist[64:]
    p = _mul(_right(jnp.concatenate(rows, 1)), gl, 0, 0)
    mid = []
    for r in range(4):
        q = p[128 * r : 128 * r + 128]
        bre = q[:64, :128] + q[64:, 128:]
        bim = q[64:, :128] - q[:64, 128:]
        mid.append(jnp.concatenate([bre * twc + bim * tws, bim * twc - bre * tws], 0))
    spectrum = _mul(fwd, _right(jnp.concatenate(mid, 1)))
    weighted = []
    for c in range(2):
        for r in range(4):
            sre = spectrum[:16, 128 * r : 128 * r + 128]
            sim = spectrum[16:, 128 * r : 128 * r + 128]
            kre, kim = kernel_at(c, 0, r), kernel_at(c, 1, r)
            weighted.append(
                jnp.concatenate([kre * sre + kim * sim, kre * sim - kim * sre], 0)
            )
    v = _mul(inv, _right(jnp.concatenate(weighted, 1)))
    turned = []
    for cr in range(8):
        vre = v[:64, 128 * cr : 128 * cr + 128]
        vim = v[64:, 128 * cr : 128 * cr + 128]
        turned += [vre * twc - vim * tws, vim * twc + vre * tws]
    u = _mul(back, _right(jnp.concatenate(turned, 0), 1), 1, 1)
    return spread(u, 16, roll)


def spread(u, half, roll):
    sign = jnp.where(_iota((half, 128), 1) < 64, -1.0, 1.0)
    out = []
    for cr in range(8):
        lanes = slice(128 * cr, 128 * cr + 128)
        out.append(u[:half, lanes] + sign * roll(u[half:, lanes], 64))
    return out


def fold_stage(rows, fold, roll):
    return spread(_mul(fold, _right(jnp.concatenate(rows, 1))), 32, roll)


def last_stage(table, rows, roll):
    g = _mul(table, _right(jnp.concatenate(rows, 1)))
    low = _iota((16, 128), 1) < 64
    part = [g[:16, 128 * c : 128 * c + 128] - roll(g[16:, 128 * c : 128 * c + 128], 64) for c in (0, 1)]
    return jnp.where(low, part[0], roll(part[1], 64))


def rows8(start, size):
    return pl.ds(pl.multiple_of(start, 8), size)


def body(
    mag, stiff, rtop_in, rside_in, ktop, kside, c_turn, c_gl32, c_gl16, c_fwd, c_inv, c_back, c_fold,
    exch, top,
    field, rtop, rside, twist, gl32, gl16, fwd, inv, back, fold, kraw, kt, ks,
    send1, recv1, recv1s, send2, recv2, send3, recv3, send4, recv4, send5, recv5,
    hop1, line1, own3, hop2, other3, recvs,
    hx_out_hi, hx_out_lo, hx_lo, hx_hi, hy_out_hi, hy_out_lo, hy_lo, hy_hi,
    local, ssem, rsem, hsend, hrecv, near, cross,
):
    gx, gy, gz = lax.axis_index("gx"), lax.axis_index("gy"), lax.axis_index("gz")
    zh, xx = lax.div(gy, 4), lax.rem(gy, 4)
    n0 = 4 * xx + gz
    m0 = 2 * gx + zh
    z, core = 8 * zh + lax.div(gx, 2), lax.rem(gx, 2)
    device = 16 * m0 + n0

    def column_index(z_plus, which):
        at = lax.rem(z_plus, 16)
        return 4 * lax.rem(at, 8) + 2 * which + lax.div(at, 8)

    def plane_id(n):
        return 16 * m0 + n

    def column_id(m):
        return 16 * m + n0

    far = jnp.where(lax.rem(gx, 16) < 8, column_id(2 * (gx + 8) + 1 - zh), column_id(2 * (gx - 8) + 1 - zh))

    def roll(value, shift):
        return pltpu.roll(value, shift, 1)

    def over_plane(action):
        for dx, dy in PLANE_ORDER:
            x = lax.rem(xx + dx, 4)
            action(4 * x + lax.rem(gz + dy, 4), x)

    def over_column(action):
        for which in (0, 1):
            action(column_index(z + 8, which))

        def step(k, carry):
            for which in (0, 1):
                action(column_index(z + 8 - k, which))
                action(column_index(z + 8 + k, which))
            return carry

        lax.fori_loop(1, 8, step, 0)
        action(column_index(z, 1 - core))

    def signal(sem, target):
        pl.semaphore_signal(sem, inc=1, device_id=target, device_id_type=LOGICAL)

    def remote(src, dst, sems, target):
        send_sem, recv_sem = sems
        return pltpu.make_async_remote_copy(
            src_ref=src, dst_ref=dst, send_sem=send_sem, recv_sem=recv_sem,
            device_id=target, device_id_type=LOGICAL,
        )

    def wait_bytes(ref, sem):
        pltpu.make_async_copy(ref, ref, sem).wait()

    def pair(i):
        return ssem.at[i], rsem.at[i]

    residuals = [
        pltpu.make_async_copy(rtop_in, rtop, local.at[4]),
        pltpu.make_async_copy(rside_in, rside, local.at[5]),
    ]
    loads = [
        pltpu.make_async_copy(src, dst, local.at[6 + i])
        for i, (src, dst) in enumerate(
            [(c_turn, twist), (c_gl32, gl32), (c_gl16, gl16), (c_fwd, fwd), (c_inv, inv), (c_back, back), (c_fold, fold)]
        )
    ] + [
        pltpu.make_async_copy(mag, field.at[0:3, pl.ds(64, 1024)], local.at[0]),
        pltpu.make_async_copy(stiff, field.at[3:4, pl.ds(64, 1024)], local.at[1]),
        pltpu.make_async_copy(ktop, kraw.at[0], local.at[2]),
        pltpu.make_async_copy(kside, kraw.at[1], local.at[3]),
    ]
    for load in residuals + loads:
        load.start()
    barrier = pltpu.get_barrier_semaphore()
    over_plane(lambda n, x: signal(barrier, plane_id(n)))

    def greet(k, carry):
        for which in (0, 1):
            signal(barrier, column_id(column_index(z + k, which)))
            signal(barrier, column_id(column_index(z + 16 - k, which)))
        return carry

    lax.fori_loop(1, 5, greet, 0)
    signal(barrier, column_id(column_index(z, 1 - core)))

    for load in residuals:
        load.wait()
    send1[...] = jnp.concatenate([rtop[0:16, :], rtop[16:32, :]], 1)
    recv1[rows8(16 * n0, 16), :] = send1[...]
    recv1s[rows8(16 * n0, 16), :] = rside[...]

    pl.semaphore_wait(barrier, 32)

    over_plane(
        lambda n, x: remote(send1, recv1.at[rows8(16 * n0, 16)], pair(0), plane_id(n)).start()
    )
    over_plane(
        lambda n, x: remote(rside, recv1s.at[rows8(16 * n0, 16)], pair(9), plane_id(n)).start()
    )

    signal(near, column_id(column_index(z + 4, core)))
    signal(near, column_id(column_index(z + 12, core)))

    for load in loads:
        load.wait()
    zero_face = jnp.zeros((64, 128), F32)
    for c in range(4):
        hx_out_hi[16 * c : 16 * c + 16, :] = field[c, pl.ds(64 + 63, 16, stride=64), :]
        hx_out_lo[16 * c : 16 * c + 16, :] = field[c, pl.ds(64, 16, stride=64), :]
    lane = _iota((64, 128), 1)

    def pack(z, carry):
        hi, lo = carry
        for c in range(4):
            at = 16 * c + z
            turned = pltpu.roll(field[c, rows8(64 + 64 * z, 64), :], at + 1, 1)
            hi = jnp.where(lane == at, turned, hi)
            lo = jnp.where(lane == at + 1, turned, lo)
        return hi, lo

    packed_hi, packed_lo = lax.fori_loop(0, 16, pack, (zero_face, zero_face))
    hy_out_hi[...] = packed_hi
    hy_out_lo[...] = packed_lo

    x_up = (gx < 15, remote(hx_out_hi, hx_lo, (hsend.at[0], hrecv.at[0]), device + 32))
    x_dn = (gx > 0, remote(hx_out_lo, hx_hi, (hsend.at[1], hrecv.at[1]), device - 32))
    y_up = (gy < 7, remote(hy_out_hi, hy_lo, (hsend.at[2], hrecv.at[2]), device + 4))
    y_dn = (gy > 0, remote(hy_out_lo, hy_hi, (hsend.at[3], hrecv.at[3]), device - 4))
    z_up = (
        gz < 3,
        remote(field.at[:, pl.ds(1024, 64)], field.at[:, pl.ds(0, 64)],
               (hsend.at[4], hrecv.at[4]), device + 1),
    )
    z_dn = (
        gz > 0,
        remote(field.at[:, pl.ds(64, 64)], field.at[:, pl.ds(1088, 64)],
               (hsend.at[5], hrecv.at[5]), device - 1),
    )
    faces = (y_up, y_dn, z_up, z_dn, x_up, x_dn)
    for there, copy in faces[4:]:

        @pl.when(there)
        def _(copy=copy):
            copy.start()

    for missing, ref in ((gx == 0, hx_lo), (gx == 15, hx_hi), (gy == 0, hy_lo), (gy == 7, hy_hi)):

        @pl.when(missing)
        def _(ref=ref):
            ref[...] = zero_face

    for missing, start in ((gz == 0, 0), (gz == 3, 1088)):

        @pl.when(missing)
        def _(start=start):
            for c in range(4):
                field[c, pl.ds(start, 64), :] = zero_face

    for which, out in ((0, kt), (1, ks)):
        for cp in range(4):
            for j in range(16):
                out[pl.ds(64 * cp + j, 4, stride=16), :] = kraw[
                    which, cp // 2, cp % 2, :, 128 * j : 128 * j + 128
                ]

    table1 = first_table(zh, n0)
    table_side = side_table(zh, n0)
    table_last = last_table(zh, n0)
    table_side_last = side_last_table(gz)

    pl.semaphore_wait(near, 2)

    for at in (0, 7):

        @pl.when(gy == at)
        def _(at=at):
            signal(cross, device + (12 if at == 0 else -12))

    wait_bytes(recv1.at[pl.ds(0, 240)], rsem.at[0])
    first = first_stage(table1, recv1[...], roll)
    for m in range(32):
        send2[m] = first[4 * m : 4 * m + 4]
    recv2[m0] = send2[m0]
    over_column(lambda m: remote(send2.at[m], recv2.at[m0], pair(1), column_id(m)).start())

    @pl.when(jnp.logical_or(gy == 3, gy == 4))
    def _():
        pl.semaphore_wait(cross, 1)

    for there, copy in faces[:4]:

        @pl.when(there)
        def _(copy=copy):
            copy.start()

    wait_bytes(recv1s.at[pl.ds(0, 240)], rsem.at[9])
    data = jnp.concatenate([recv1s[64 * x : 64 * x + 64, :] for x in range(4)], 1)
    own, other = side_first(table_side, data, roll)
    for x in range(4):
        line1[rows8(32 * zh + 8 * x, 8), :] = own[x]
        hop1[8 * x : 8 * x + 8, :] = other[x]
    remote(hop1, line1.at[rows8(32 * zh, 32)], pair(5), far).start()

    wait_bytes(recv2.at[pl.ds(0, 31)], rsem.at[1])
    shared = (twist[...], fwd[...], inv[...], back[...])
    lines = line_stage(
        [recv2[:, r, :] for r in range(4)],
        lambda c, p, r: kt[64 * (2 * c + p) + 16 * r : 64 * (2 * c + p) + 16 * r + 16, :],
        (gl32[...],) + shared,
        roll,
    )
    for cr in range(8):
        send3[pl.ds(cr, 16, stride=8), :] = lines[cr]
    recv3[rows8(8 * m0, 8), :] = send3[rows8(8 * gx, 8), :]
    over_column(
        lambda m: remote(
            send3.at[rows8(8 * lax.div(m, 2), 8)], recv3.at[rows8(8 * m0, 8)], pair(2), column_id(m)
        ).start()
    )

    wait_bytes(line1.at[pl.ds(0, 32)], rsem.at[5])
    lines = line_stage(
        [line1[pl.ds(r, 16, stride=4), :] for r in range(4)],
        lambda c, p, r: ks[64 * (2 * c + p) + 16 * r : 64 * (2 * c + p) + 16 * r + 16, :],
        (gl16[...],) + shared,
        roll,
    )
    for cr in range(8):
        here, there = lines[cr][:8], lines[cr][8:]
        own3[pl.ds(cr, 8, stride=8), :] = jnp.where(zh == 0, here, there)
        hop2[pl.ds(cr, 8, stride=8), :] = jnp.where(zh == 0, there, here)
    remote(hop2, other3, pair(6), far).start()
    recvs[rows8(32 * n0 + 16 * zh, 16), :] = own3[rows8(16 * xx, 16), :]
    over_plane(
        lambda n, x: remote(
            own3.at[rows8(16 * x, 16)],
            recvs.at[rows8(32 * n0 + 16 * zh, 16)], pair(7), plane_id(n),
        ).start()
    )

    arrivals = (
        (gx > 0, hx_lo, 0), (gx < 15, hx_hi, 1), (gy > 0, hy_lo, 2), (gy < 7, hy_hi, 3),
        (gz > 0, field.at[:, pl.ds(0, 64)], 4), (gz < 3, field.at[:, pl.ds(1088, 64)], 5),
    )
    for there, ref, i in arrivals:

        @pl.when(there)
        def _(ref=ref, i=i):
            wait_bytes(ref, hrecv.at[i])

    sub = _iota((64, 128), 0)

    def exchange(z, carry):
        def slab(c, step):
            return field[c, rows8(64 + 64 * (z + step), 64), :]

        def around(c):
            at = 16 * c + z
            center = slab(c, 0)
            below = jnp.where(sub == 0, hx_lo[pl.ds(at, 1), :], pltpu.roll(center, 1, 0))
            above = jnp.where(sub == 63, hx_hi[pl.ds(at, 1), :], pltpu.roll(center, 63, 0))
            left = jnp.where(lane == 0, pltpu.roll(hy_lo[...], 128 - at, 1), pltpu.roll(center, 1, 1))
            right = jnp.where(
                lane == 127, pltpu.roll(hy_hi[...], 126 - at, 1), pltpu.roll(center, 127, 1)
            )
            return center, (slab(c, -1), slab(c, 1), below, above, left, right)

        a, near = around(3)
        weights = [4.0 * a * b / (a + b) for b in near]
        for c in range(3):
            m, beside = around(c)
            total = weights[0] * (m - beside[0])
            for w, b in zip(weights[1:], beside[1:]):
                total = total + w * (m - b)
            exch[c, rows8(64 * z, 64), :] = total
        return carry

    lax.fori_loop(0, 16, exchange, 0)

    wait_bytes(other3, rsem.at[6])
    recvs[rows8(32 * n0 + 16 * (1 - zh), 16), :] = other3[rows8(16 * xx, 16), :]
    over_plane(
        lambda n, x: remote(
            other3.at[rows8(16 * x, 16)],
            recvs.at[rows8(32 * n0 + 16 * (1 - zh), 16)], pair(8), plane_id(n),
        ).start()
    )

    wait_bytes(recv3.at[pl.ds(0, 248)], rsem.at[2])
    folded = fold_stage([recv3[pl.ds(cr, 32, stride=8), :] for cr in range(8)], fold[...], roll)
    for cr in range(8):
        send4[pl.ds(cr, 16, stride=16), :] = folded[cr][:16]
        send4[pl.ds(8 + cr, 16, stride=16), :] = folded[cr][16:]
    recv4[rows8(16 * n0, 16), :] = send4[rows8(16 * n0, 16), :]
    over_plane(
        lambda n, x: remote(
            send4.at[rows8(16 * n, 16)], recv4.at[rows8(16 * n0, 16)], pair(3), plane_id(n)
        ).start()
    )

    wait_bytes(recvs.at[pl.ds(0, 240)], rsem.at[7])
    wait_bytes(recvs.at[pl.ds(0, 240)], rsem.at[8])
    columns = [
        jnp.concatenate([recvs[pl.ds(8 * e + 4 * c + r, 32, stride=16), :] for r in range(4)], 0)
        for c in range(2)
        for e in range(2)
    ]
    g = _mul(table_side_last, _right(jnp.concatenate(columns, 1)))
    low = _iota((16, 128), 1) < 64
    for c in range(2):
        halves = [
            g[:16, 128 * q : 128 * q + 128] - roll(g[16:, 128 * q : 128 * q + 128], 64)
            for q in (2 * c, 2 * c + 1)
        ]
        side = jnp.where(low, halves[0], roll(halves[1], 64))
        for z in range(16):
            rows = slice(64 * z, 64 * z + 64)
            exch[c + 1, rows, :] = exch[c + 1, rows, :] + side[z : z + 1, :]

    wait_bytes(recv4.at[pl.ds(0, 240)], rsem.at[3])
    for a in range(2):
        rows = [
            jnp.concatenate(
                [recv4[pl.ds(8 * a + 4 * c + r, 16, stride=16), :] for r in range(4)], 0
            )
            for c in range(2)
        ]
        send5[pl.ds(a, 16, stride=2), :] = last_stage(table_last[a], rows, roll)
    recv5[rows8(8 * n0, 8), :] = send5[rows8(8 * xx, 8), :]
    over_plane(
        lambda n, x: remote(
            send5.at[rows8(8 * x, 8)], recv5.at[rows8(8 * n0, 8)], pair(4), plane_id(n)
        ).start()
    )

    wait_bytes(recv1.at[pl.ds(0, 240)], ssem.at[0])
    wait_bytes(recv1s.at[pl.ds(0, 240)], ssem.at[9])
    wait_bytes(send2.at[pl.ds(0, 31)], ssem.at[1])
    wait_bytes(recv3.at[pl.ds(0, 248)], ssem.at[2])
    wait_bytes(recv4.at[pl.ds(0, 240)], ssem.at[3])
    wait_bytes(hop1, ssem.at[5])
    wait_bytes(hop2, ssem.at[6])
    wait_bytes(recvs.at[pl.ds(0, 240)], ssem.at[7])
    wait_bytes(recvs.at[pl.ds(0, 240)], ssem.at[8])
    for there, copy in faces:

        @pl.when(there)
        def _(copy=copy):
            copy.wait_send()

    wait_bytes(recv5.at[pl.ds(0, 120)], rsem.at[4])
    lines_y = jnp.concatenate([recv5[pl.ds(q, 16, stride=8), :] for q in range(8)], 0)
    top[0:128, :] = lines_y.T
    top[128:192, :] = zero_face
    wait_bytes(recv5.at[pl.ds(0, 120)], ssem.at[4])


def on_device(magnetization, stiffness, residual_top, residual_side, top_kernel, side_kernel):
    tables = [jnp.asarray(t) for t in const_tables()]
    vmem = pl.BlockSpec(memory_space=pltpu.VMEM)
    hbm = pl.BlockSpec(memory_space=pltpu.HBM)

    def pin(array):
        return pltpu.with_memory_space_constraint(array, pltpu.HBM)

    def buf(*shape):
        return pltpu.VMEM(shape, F32)

    scratch = [
        buf(4, 1152, 128), buf(32, 64), buf(16, 128), *[pltpu.VMEM(t.shape, t.dtype) for t in tables], buf(2, 2, 2, 4, 2048), buf(256, 128), buf(256, 128),
        buf(16, 128), buf(256, 128), buf(256, 128), buf(32, 4, 128), buf(32, 4, 128),
        buf(128, 128), buf(256, 128), buf(256, 128), buf(256, 128), buf(32, 128), buf(128, 128),
        buf(32, 128), buf(64, 128), buf(64, 128), buf(64, 128), buf(64, 128), buf(512, 128),
        buf(64, 128), buf(64, 128), buf(64, 128), buf(64, 128),
        buf(64, 128), buf(64, 128), buf(64, 128), buf(64, 128),
        pltpu.SemaphoreType.DMA((13,)), pltpu.SemaphoreType.DMA((10,)), pltpu.SemaphoreType.DMA((10,)),
        pltpu.SemaphoreType.DMA((6,)), pltpu.SemaphoreType.DMA((6,)),
        pltpu.SemaphoreType.REGULAR, pltpu.SemaphoreType.REGULAR,
    ]
    exch, top = pl.pallas_call(
        body,
        out_shape=[
            jax.ShapeDtypeStruct((3, 1024, 128), F32),
            jax.ShapeDtypeStruct((192, 128), F32),
        ],
        in_specs=[hbm] * (6 + len(tables)),
        out_specs=[vmem] * 2,
        scratch_shapes=scratch,
        compiler_params=pltpu.CompilerParams(
            collective_id=0, has_side_effects=True, vmem_limit_bytes=40 * 1024 * 1024
        ),
        name="adjoint",
    )(
        pin(magnetization.reshape(3, 1024, 128)),
        pin(stiffness.reshape(1, 1024, 128)),
        pin(residual_top.T),
        pin(residual_side.T),
        pin(top_kernel),
        pin(side_kernel),
        *[pin(t) for t in tables],
    )
    return exch.reshape(3, 16, 64, 128) + top.reshape(3, 1, 64, 128)


def solution(mesh):
    placed = (
        P(None, "gz", "gx", "gy"),
        P("gz", "gx", "gy"),
        P("gx", ("gy", "gz")),
        P("gy", "gz"),
        P(None, None, ("gx", "gy", "gz"), None),
        P(None, None, ("gy", "gz"), None),
    )
    return jax.shard_map(
        on_device, mesh=mesh, in_specs=placed, out_specs=P(None, "gz", "gx", "gy"), check_vma=False
    )
```

```python
import math

import jax
import jax.numpy as jnp
import numpy as np
from jax import lax
from jax.experimental import pallas as pl
from jax.experimental.pallas import tpu as pltpu
from jax.sharding import PartitionSpec as P

F32 = jnp.float32
LOGICAL = pl.DeviceIdType.LOGICAL
PLANE_ORDER = sorted(
    [(dx, dy) for dx in range(4) for dy in range(4) if dx or dy],
    key=lambda d: -(min(d[0], 4 - d[0]) + min(d[1], 4 - d[1])),
)
TOP_SCALE = 1.0 / 2048.0**2
SIDE_SCALE = 1.0 / (2048.0 * 128.0)


BF16 = jnp.bfloat16


def _split(x):
    high = x.astype(BF16)
    return high, (x - high.astype(F32)).astype(BF16)


def _left(table, axis=1):
    high, low = _split(table)
    return jnp.concatenate([high, high, low], axis)


def _right(value, axis=0):
    high, low = _split(value)
    return jnp.concatenate([high, low, high], axis)


def _mul(a, b, ca=1, cb=0):
    return lax.dot_general(a, b, (((ca,), (cb,)), ((), ())), preferred_element_type=F32)


def _cs(first, second, modulus):
    angle = 2.0 * np.pi * ((first * second) % modulus) / modulus
    return np.cos(angle), np.sin(angle)


def const_tables():
    i = np.arange
    c, s = _cs(i(16)[:, None], i(128)[None, :], 32)
    gl16 = np.concatenate([c, s], 1)
    gl32 = np.repeat(gl16, 2, axis=0)
    c, s = _cs(i(64)[:, None], i(128)[None, :], 2048)
    twist = np.concatenate([c, s], 0)
    c, s = _cs(i(16)[:, None], i(64)[None, :], 16)
    fwd = np.block([[c, s], [-s, c]])
    inv = np.block([[c.T, -s.T], [s.T, c.T]])
    back = gl16.reshape(16, 2, 128).transpose(1, 0, 2).reshape(32, 128)
    c, s = _cs(i(32)[:, None], i(32)[None, :], 32)
    fold = np.concatenate([c, s], 0)
    turn = twist.astype(np.float32)
    split = [split3(gl32, 0), split3(gl16, 0), split3(fwd, 1), split3(inv, 1), split3(back, 1), split3(fold, 1)]
    return [turn] + split


def split3(table, axis):
    table = table.astype(np.float32)
    high = table.astype(BF16)
    low = (table - high.astype(np.float32)).astype(BF16)
    return np.concatenate([high, high, low], axis)


def _iota(shape, dim):
    return lax.broadcasted_iota(jnp.int32, shape, dim)


def _angle(product, modulus):
    return (product & (modulus - 1)).astype(F32) * (2.0 * math.pi / modulus)


def first_table(zh, n0):
    row = _iota((128, 256), 0)
    col = _iota((128, 256), 1)
    ky = 64 * (row // 4) + row % 4 + 4 * n0
    y = 32 * (col // 16) + col % 16 + 512 * zh
    parts = []
    for h in (0, 1):
        t = _angle(ky * (y + 16 * h), 2048)
        parts += [_left(jnp.cos(t)), _left(-jnp.sin(t))]
    return parts


def last_table(zh, n0):
    row = _iota((16, 64), 0)
    col = _iota((16, 64), 1)
    s = 4 * (col % 16) + col // 16
    out = []
    for a in (0, 1):
        t = _angle(s * (32 * row + n0 + 16 * a + 512 * zh), 2048)
        out.append(_left(jnp.concatenate([jnp.cos(t) * TOP_SCALE, jnp.sin(t) * TOP_SCALE], 0)))
    return out


def side_table(zh, n0):
    row = _iota((16, 64), 0)
    z = _iota((16, 64), 1)
    own = jnp.where(row < 8, zh, 1 - zh)
    t = _angle((64 * own + 4 * n0 + row % 4) * z, 128)
    return _left(jnp.where(row % 8 < 4, jnp.cos(t), -jnp.sin(t)))


def side_last_table(zh, yy):
    row = _iota((16, 64), 0)
    col = _iota((16, 64), 1)
    kz = 64 * zh + 4 * (col % 16) + col // 16
    t = _angle(kz * (row + 16 * yy), 128)
    return _left(jnp.concatenate([jnp.cos(t) * SIDE_SCALE, jnp.sin(t) * SIDE_SCALE], 0))


def first_stage(w, packed, roll):
    packed = _right(packed)
    p = [_mul(t, packed) for t in w]
    low = _iota((128, 128), 1) < 64
    return jnp.where(low, p[0] + roll(p[2], 64), roll(p[1], 64) + p[3])


def side_first(w, data, roll):
    t = _mul(w, _right(data))
    low = _iota((4, 128), 1) < 64
    own, other = [], []
    for x in range(4):
        for base, out in ((0, own), (8, other)):
            o = t[base : base + 8, 128 * x : 128 * x + 128]
            q = roll(o, 64)
            f0 = jnp.where(low, o[0:4], q[4:8])
            f1 = jnp.where(low, q[0:4], o[4:8])
            out.append(jnp.concatenate([f0, f1], 0))
    return own, other


def line_stage(rows, kernel_at, tabs, roll):
    gl, twist, fwd, inv, back = tabs
    twc, tws = twist[:64], twist[64:]
    p = _mul(_right(jnp.concatenate(rows, 1)), gl, 0, 0)
    mid = []
    for r in range(4):
        q = p[128 * r : 128 * r + 128]
        bre = q[:64, :128] + q[64:, 128:]
        bim = q[64:, :128] - q[:64, 128:]
        mid.append(jnp.concatenate([bre * twc + bim * tws, bim * twc - bre * tws], 0))
    spectrum = _mul(fwd, _right(jnp.concatenate(mid, 1)))
    weighted = []
    for c in range(2):
        for r in range(4):
            sre = spectrum[:16, 128 * r : 128 * r + 128]
            sim = spectrum[16:, 128 * r : 128 * r + 128]
            kre, kim = kernel_at(c, 0, r), kernel_at(c, 1, r)
            weighted.append(
                jnp.concatenate([kre * sre + kim * sim, kre * sim - kim * sre], 0)
            )
    v = _mul(inv, _right(jnp.concatenate(weighted, 1)))
    turned = []
    for cr in range(8):
        vre = v[:64, 128 * cr : 128 * cr + 128]
        vim = v[64:, 128 * cr : 128 * cr + 128]
        turned += [vre * twc - vim * tws, vim * twc + vre * tws]
    u = _mul(back, _right(jnp.concatenate(turned, 0), 1), 1, 1)
    return spread(u, 16, roll)


def spread(u, half, roll):
    sign = jnp.where(_iota((half, 128), 1) < 64, -1.0, 1.0)
    out = []
    for cr in range(8):
        lanes = slice(128 * cr, 128 * cr + 128)
        out.append(u[:half, lanes] + sign * roll(u[half:, lanes], 64))
    return out


def fold_stage(rows, fold, roll):
    return spread(_mul(fold, _right(jnp.concatenate(rows, 1))), 32, roll)


def last_stage(table, rows, roll):
    g = _mul(table, _right(jnp.concatenate(rows, 1)))
    low = _iota((16, 128), 1) < 64
    part = [g[:16, 128 * c : 128 * c + 128] - roll(g[16:, 128 * c : 128 * c + 128], 64) for c in (0, 1)]
    return jnp.where(low, part[0], roll(part[1], 64))


def rows8(start, size):
    return pl.ds(pl.multiple_of(start, 8), size)


def body(
    mag, stiff, rtop_in, rside_in, ktop, kside, c_turn, c_gl32, c_gl16, c_fwd, c_inv, c_back, c_fold,
    exch, top,
    field, rtop, rside, twist, gl32, gl16, fwd, inv, back, fold, kraw, kt, ks,
    send1, recv1, recv1s, send2, recv2, send3, recv3, send4, recv4, send5, recv5,
    hop1, line1, send6, recv6, hop2, other2,
    hx_out_hi, hx_out_lo, hx_lo, hx_hi, hy_out_hi, hy_out_lo, hy_lo, hy_hi, col_lo, col_hi,
    local, ssem, rsem, hsend, hrecv, near, cross,
):
    gx, gy, gz = lax.axis_index("gx"), lax.axis_index("gy"), lax.axis_index("gz")
    zh, xx = lax.div(gy, 4), lax.rem(gy, 4)
    n0 = 4 * xx + gz
    m0 = 2 * gx + zh
    z, core = 8 * zh + lax.div(gx, 2), lax.rem(gx, 2)
    device = 16 * m0 + n0

    def column_index(z_plus, which):
        at = lax.rem(z_plus, 16)
        return 4 * lax.rem(at, 8) + 2 * which + lax.div(at, 8)

    def plane_id(n):
        return 16 * m0 + n

    def column_id(m):
        return 16 * m + n0

    far = jnp.where(lax.rem(gx, 16) < 8, column_id(2 * (gx + 8) + 1 - zh), column_id(2 * (gx - 8) + 1 - zh))

    def roll(value, shift):
        return pltpu.roll(value, shift, 1)

    def over_plane(action):
        for dx, dy in PLANE_ORDER:
            x = lax.rem(xx + dx, 4)
            action(4 * x + lax.rem(gz + dy, 4), x)

    def over_column(action):
        for which in (0, 1):
            action(column_index(z + 8, which))

        def step(k, carry):
            for which in (0, 1):
                action(column_index(z + 8 - k, which))
                action(column_index(z + 8 + k, which))
            return carry

        lax.fori_loop(1, 8, step, 0)
        action(column_index(z, 1 - core))

    def signal(sem, target):
        pl.semaphore_signal(sem, inc=1, device_id=target, device_id_type=LOGICAL)

    def remote(src, dst, sems, target):
        send_sem, recv_sem = sems
        return pltpu.make_async_remote_copy(
            src_ref=src, dst_ref=dst, send_sem=send_sem, recv_sem=recv_sem,
            device_id=target, device_id_type=LOGICAL,
        )

    def wait_bytes(ref, sem):
        pltpu.make_async_copy(ref, ref, sem).wait()

    def pair(i):
        return ssem.at[i], rsem.at[i]

    residuals = [
        pltpu.make_async_copy(rtop_in, rtop, local.at[4]),
        pltpu.make_async_copy(rside_in, rside, local.at[5]),
    ]
    loads = [
        pltpu.make_async_copy(src, dst, local.at[6 + i])
        for i, (src, dst) in enumerate(
            [(c_turn, twist), (c_gl32, gl32), (c_gl16, gl16), (c_fwd, fwd), (c_inv, inv), (c_back, back), (c_fold, fold)]
        )
    ] + [
        pltpu.make_async_copy(mag, field.at[0:3, pl.ds(64, 1024)], local.at[0]),
        pltpu.make_async_copy(stiff, field.at[3:4, pl.ds(64, 1024)], local.at[1]),
        pltpu.make_async_copy(ktop, kraw.at[0], local.at[2]),
        pltpu.make_async_copy(kside, kraw.at[1], local.at[3]),
    ]
    for load in residuals + loads:
        load.start()
    barrier = pltpu.get_barrier_semaphore()
    over_plane(lambda n, x: signal(barrier, plane_id(n)))

    def greet(k, carry):
        for which in (0, 1):
            signal(barrier, column_id(column_index(z + k, which)))
            signal(barrier, column_id(column_index(z + 16 - k, which)))
        return carry

    lax.fori_loop(1, 5, greet, 0)
    signal(barrier, column_id(column_index(z, 1 - core)))

    for load in residuals:
        load.wait()
    send1[...] = jnp.concatenate([rtop[0:16, :], rtop[16:32, :]], 1)
    recv1[rows8(16 * n0, 16), :] = send1[...]
    recv1s[rows8(16 * n0, 16), :] = rside[...]

    pl.semaphore_wait(barrier, 32)

    over_plane(
        lambda n, x: remote(send1, recv1.at[rows8(16 * n0, 16)], pair(0), plane_id(n)).start()
    )
    over_plane(
        lambda n, x: remote(rside, recv1s.at[rows8(16 * n0, 16)], pair(8), plane_id(n)).start()
    )

    signal(near, column_id(column_index(z + 4, core)))
    signal(near, column_id(column_index(z + 12, core)))

    for load in loads:
        load.wait()
    zero_face = jnp.zeros((64, 128), F32)
    for c in range(4):
        hx_out_hi[16 * c : 16 * c + 16, :] = field[c, pl.ds(64 + 63, 16, stride=64), :]
        hx_out_lo[16 * c : 16 * c + 16, :] = field[c, pl.ds(64, 16, stride=64), :]
    lane = _iota((64, 128), 1)

    def pack(z, carry):
        hi, lo = carry
        for c in range(4):
            at = 16 * c + z
            turned = pltpu.roll(field[c, rows8(64 + 64 * z, 64), :], at + 1, 1)
            hi = jnp.where(lane == at, turned, hi)
            lo = jnp.where(lane == at + 1, turned, lo)
        return hi, lo

    packed_hi, packed_lo = lax.fori_loop(0, 16, pack, (zero_face, zero_face))
    low = _iota((32, 128), 1) < 64
    hy_out_hi[...] = jnp.where(low, packed_hi[:32], roll(packed_hi[32:], 64))
    hy_out_lo[...] = jnp.where(low, roll(packed_lo[:32], 127), roll(packed_lo[32:], 63))

    x_up = (gx < 15, remote(hx_out_hi, hx_lo, (hsend.at[0], hrecv.at[0]), device + 32))
    x_dn = (gx > 0, remote(hx_out_lo, hx_hi, (hsend.at[1], hrecv.at[1]), device - 32))
    y_up = (gy < 7, remote(hy_out_hi, hy_lo, (hsend.at[2], hrecv.at[2]), device + 4))
    y_dn = (gy > 0, remote(hy_out_lo, hy_hi, (hsend.at[3], hrecv.at[3]), device - 4))
    z_up = (
        gz < 3,
        remote(field.at[:, pl.ds(1024, 64)], field.at[:, pl.ds(0, 64)],
               (hsend.at[4], hrecv.at[4]), device + 1),
    )
    z_dn = (
        gz > 0,
        remote(field.at[:, pl.ds(64, 64)], field.at[:, pl.ds(1088, 64)],
               (hsend.at[5], hrecv.at[5]), device - 1),
    )
    faces = (y_up, y_dn, z_up, z_dn, x_up, x_dn)
    for there, copy in faces[4:]:

        @pl.when(there)
        def _(copy=copy):
            copy.start()

    pl.semaphore_wait(near, 2)
    for at in (0, 7):

        @pl.when(gy == at)
        def _(at=at):
            signal(cross, device + (12 if at == 0 else -12))

    for missing, ref in ((gx == 0, hx_lo), (gx == 15, hx_hi), (gy == 0, hy_lo), (gy == 7, hy_hi)):

        @pl.when(missing)
        def _(ref=ref):
            ref[...] = zero_face[: ref.shape[0]]

    for missing, start in ((gz == 0, 0), (gz == 3, 1088)):

        @pl.when(missing)
        def _(start=start):
            for c in range(4):
                field[c, pl.ds(start, 64), :] = zero_face

    for which, out in ((0, kt), (1, ks)):
        for cp in range(4):
            for j in range(16):
                out[pl.ds(64 * cp + j, 4, stride=16), :] = kraw[
                    which, cp // 2, cp % 2, :, 128 * j : 128 * j + 128
                ]

    table1 = first_table(zh, n0)
    table_side = side_table(zh, n0)
    table_last = last_table(zh, n0)
    table_side_last = side_last_table(zh, gz)

    for at, copy in ((3, y_up[1]), (4, y_dn[1])):

        @pl.when(gy == at)
        def _(copy=copy):
            pl.semaphore_wait(cross, 1)
            copy.start()

    wait_bytes(recv1.at[pl.ds(0, 240)], rsem.at[0])
    first = first_stage(table1, recv1[...], roll)
    for m in range(32):
        send2[m] = first[4 * m : 4 * m + 4]
    recv2[m0] = send2[m0]
    over_column(lambda m: remote(send2.at[m], recv2.at[m0], pair(1), column_id(m)).start())

    inside = (
        (jnp.logical_and(gy < 7, gy != 3), y_up[1]),
        (jnp.logical_and(gy > 0, gy != 4), y_dn[1]),
    ) + faces[2:4]
    for there, copy in inside:

        @pl.when(there)
        def _(copy=copy):
            copy.start()

    wait_bytes(recv1s.at[pl.ds(0, 240)], rsem.at[8])
    data = jnp.concatenate([recv1s[64 * x : 64 * x + 64, :] for x in range(4)], 1)
    own, other = side_first(table_side, data, roll)
    for x in range(4):
        line1[rows8(32 * zh + 8 * x, 8), :] = own[x]
        hop1[8 * x : 8 * x + 8, :] = other[x]
    remote(hop1, line1.at[rows8(32 * zh, 32)], pair(5), far).start()

    wait_bytes(recv2.at[pl.ds(0, 31)], rsem.at[1])
    shared = (twist[...], fwd[...], inv[...], back[...])
    lines = line_stage(
        [recv2[:, r, :] for r in range(4)],
        lambda c, p, r: kt[64 * (2 * c + p) + 16 * r : 64 * (2 * c + p) + 16 * r + 16, :],
        (gl32[...],) + shared,
        roll,
    )
    for cr in range(8):
        send3[pl.ds(cr, 16, stride=8), :] = lines[cr]
    recv3[rows8(8 * m0, 8), :] = send3[rows8(8 * gx, 8), :]
    over_column(
        lambda m: remote(
            send3.at[rows8(8 * lax.div(m, 2), 8)], recv3.at[rows8(8 * m0, 8)], pair(2), column_id(m)
        ).start()
    )

    wait_bytes(line1.at[pl.ds(0, 32)], rsem.at[5])
    lines = line_stage(
        [line1[pl.ds(r, 16, stride=4), :] for r in range(4)],
        lambda c, p, r: ks[64 * (2 * c + p) + 16 * r : 64 * (2 * c + p) + 16 * r + 16, :],
        (gl16[...],) + shared,
        roll,
    )
    for cr in range(8):
        for h in range(2):
            send6[h, pl.ds(cr, 8, stride=8), :] = lines[cr][8 * h : 8 * h + 8]
    recv6[:, rows8(16 * n0, 16), :] = send6[:, rows8(16 * xx, 16), :]
    over_plane(
        lambda n, x: remote(
            send6.at[:, rows8(16 * x, 16)], recv6.at[:, rows8(16 * n0, 16)], pair(6), plane_id(n)
        ).start()
    )

    arrivals = (
        (gx > 0, hx_lo, 0), (gx < 15, hx_hi, 1), (gy > 0, hy_lo, 2), (gy < 7, hy_hi, 3),
        (gz > 0, field.at[:, pl.ds(0, 64)], 4), (gz < 3, field.at[:, pl.ds(1088, 64)], 5),
    )
    for there, ref, i in arrivals:

        @pl.when(there)
        def _(ref=ref, i=i):
            wait_bytes(ref, hrecv.at[i])

    for ref, out in ((hy_lo, col_lo), (hy_hi, col_hi)):
        out[0:32, :] = ref[...]
        out[32:64, :] = roll(ref[...], 64)
    sub = _iota((64, 128), 0)

    def exchange(z, carry):
        def slab(c, step):
            return field[c, rows8(64 + 64 * (z + step), 64), :]

        def around(c):
            at = 16 * c + z
            center = slab(c, 0)
            below = jnp.where(sub == 0, hx_lo[pl.ds(at, 1), :], pltpu.roll(center, 1, 0))
            above = jnp.where(sub == 63, hx_hi[pl.ds(at, 1), :], pltpu.roll(center, 63, 0))
            left = jnp.where(lane == 0, pltpu.roll(col_lo[...], 128 - at, 1), pltpu.roll(center, 1, 1))
            right = jnp.where(
                lane == 127, pltpu.roll(col_hi[...], 127 - at, 1), pltpu.roll(center, 127, 1)
            )
            return center, (slab(c, -1), slab(c, 1), below, above, left, right)

        a, near = around(3)
        weights = [4.0 * a * b / (a + b) for b in near]
        for c in range(3):
            m, beside = around(c)
            total = weights[0] * (m - beside[0])
            for w, b in zip(weights[1:], beside[1:]):
                total = total + w * (m - b)
            exch[c, rows8(64 * z, 64), :] = total
        return carry

    lax.fori_loop(0, 16, exchange, 0)

    wait_bytes(recv3.at[pl.ds(0, 248)], rsem.at[2])
    folded = fold_stage([recv3[pl.ds(cr, 32, stride=8), :] for cr in range(8)], fold[...], roll)
    for cr in range(8):
        send4[pl.ds(cr, 16, stride=16), :] = folded[cr][:16]
        send4[pl.ds(8 + cr, 16, stride=16), :] = folded[cr][16:]
    recv4[rows8(16 * n0, 16), :] = send4[rows8(16 * n0, 16), :]
    over_plane(
        lambda n, x: remote(
            send4.at[rows8(16 * n, 16)], recv4.at[rows8(16 * n0, 16)], pair(3), plane_id(n)
        ).start()
    )

    wait_bytes(recv6.at[:, pl.ds(0, 240)], rsem.at[6])
    columns = [
        jnp.concatenate([recv6[h, pl.ds(8 * e + 4 * c + r, 16, stride=16), :] for r in range(4)], 0)
        for h in (zh, 1 - zh)
        for c in range(2)
        for e in range(2)
    ]
    g = _mul(table_side_last, _right(jnp.concatenate(columns, 1)))
    low = _iota((16, 128), 1) < 64
    halves = [
        g[:16, 128 * q : 128 * q + 128] - roll(g[16:, 128 * q : 128 * q + 128], 64) for q in range(8)
    ]
    sums = [jnp.where(low, halves[q], roll(halves[q + 1], 64)) for q in (0, 2, 4, 6)]
    hop2[0:16, :], hop2[16:32, :] = sums[2], sums[3]
    remote(hop2, other2, pair(7), far).start()

    wait_bytes(recv4.at[pl.ds(0, 240)], rsem.at[3])
    for a in range(2):
        rows = [
            jnp.concatenate(
                [recv4[pl.ds(8 * a + 4 * c + r, 16, stride=16), :] for r in range(4)], 0
            )
            for c in range(2)
        ]
        send5[pl.ds(a, 16, stride=2), :] = last_stage(table_last[a], rows, roll)
    recv5[rows8(8 * n0, 8), :] = send5[rows8(8 * xx, 8), :]
    over_plane(
        lambda n, x: remote(
            send5.at[rows8(8 * x, 8)], recv5.at[rows8(8 * n0, 8)], pair(4), plane_id(n)
        ).start()
    )

    wait_bytes(other2, rsem.at[7])
    for c in range(2):
        side = sums[c] + other2[16 * c : 16 * c + 16, :]
        for at in range(16):
            rows = slice(64 * at, 64 * at + 64)
            exch[c + 1, rows, :] = exch[c + 1, rows, :] + side[at : at + 1, :]

    wait_bytes(recv1.at[pl.ds(0, 240)], ssem.at[0])
    wait_bytes(recv1s.at[pl.ds(0, 240)], ssem.at[8])
    wait_bytes(send2.at[pl.ds(0, 31)], ssem.at[1])
    wait_bytes(recv3.at[pl.ds(0, 248)], ssem.at[2])
    wait_bytes(recv4.at[pl.ds(0, 240)], ssem.at[3])
    wait_bytes(hop1, ssem.at[5])
    wait_bytes(recv6.at[:, pl.ds(0, 240)], ssem.at[6])
    wait_bytes(hop2, ssem.at[7])
    for there, copy in faces:

        @pl.when(there)
        def _(copy=copy):
            copy.wait_send()

    wait_bytes(recv5.at[pl.ds(0, 120)], rsem.at[4])
    lines_y = jnp.concatenate([recv5[pl.ds(q, 16, stride=8), :] for q in range(8)], 0)
    top[0:128, :] = lines_y.T
    top[128:192, :] = zero_face
    wait_bytes(recv5.at[pl.ds(0, 120)], ssem.at[4])


def on_device(magnetization, stiffness, residual_top, residual_side, top_kernel, side_kernel):
    tables = [jnp.asarray(t) for t in const_tables()]
    vmem = pl.BlockSpec(memory_space=pltpu.VMEM)
    hbm = pl.BlockSpec(memory_space=pltpu.HBM)

    def pin(array):
        return pltpu.with_memory_space_constraint(array, pltpu.HBM)

    def buf(*shape):
        return pltpu.VMEM(shape, F32)

    scratch = [
        buf(4, 1152, 128), buf(32, 64), buf(16, 128), *[pltpu.VMEM(t.shape, t.dtype) for t in tables], buf(2, 2, 2, 4, 2048), buf(256, 128), buf(256, 128),
        buf(16, 128), buf(256, 128), buf(256, 128), buf(32, 4, 128), buf(32, 4, 128),
        buf(128, 128), buf(256, 128), buf(256, 128), buf(256, 128), buf(32, 128), buf(128, 128),
        buf(32, 128), buf(64, 128), buf(2, 64, 128), buf(2, 256, 128), buf(32, 128), buf(32, 128),
        buf(64, 128), buf(64, 128), buf(64, 128), buf(64, 128),
        buf(32, 128), buf(32, 128), buf(32, 128), buf(32, 128), buf(64, 128), buf(64, 128),
        pltpu.SemaphoreType.DMA((13,)), pltpu.SemaphoreType.DMA((9,)), pltpu.SemaphoreType.DMA((9,)),
        pltpu.SemaphoreType.DMA((6,)), pltpu.SemaphoreType.DMA((6,)),
        pltpu.SemaphoreType.REGULAR, pltpu.SemaphoreType.REGULAR,
    ]
    exch, top = pl.pallas_call(
        body,
        out_shape=[
            jax.ShapeDtypeStruct((3, 1024, 128), F32),
            jax.ShapeDtypeStruct((192, 128), F32),
        ],
        in_specs=[hbm] * (6 + len(tables)),
        out_specs=[vmem] * 2,
        scratch_shapes=scratch,
        compiler_params=pltpu.CompilerParams(
            collective_id=0, has_side_effects=True, vmem_limit_bytes=40 * 1024 * 1024
        ),
        name="adjoint",
    )(
        pin(magnetization.reshape(3, 1024, 128)),
        pin(stiffness.reshape(1, 1024, 128)),
        pin(residual_top.T),
        pin(residual_side.T),
        pin(top_kernel),
        pin(side_kernel),
        *[pin(t) for t in tables],
    )
    return exch.reshape(3, 16, 64, 128) + top.reshape(3, 1, 64, 128)


def solution(mesh):
    placed = (
        P(None, "gz", "gx", "gy"),
        P("gz", "gx", "gy"),
        P("gx", ("gy", "gz")),
        P("gy", "gz"),
        P(None, None, ("gx", "gy", "gz"), None),
        P(None, None, ("gy", "gz"), None),
    )
    return jax.shard_map(
        on_device, mesh=mesh, in_specs=placed, out_specs=P(None, "gz", "gx", "gy"), check_vma=False
    )
```

```python
import math

import jax
import jax.numpy as jnp
import numpy as np
from jax import lax
from jax.experimental import pallas as pl
from jax.experimental.pallas import tpu as pltpu
from jax.sharding import PartitionSpec as P

F32 = jnp.float32
LOGICAL = pl.DeviceIdType.LOGICAL
PLANE_ORDER = sorted(
    [(dx, dy) for dx in range(4) for dy in range(4) if dx or dy],
    key=lambda d: -(min(d[0], 4 - d[0]) + min(d[1], 4 - d[1])),
)
TOP_SCALE = 1.0 / 2048.0**2
SIDE_SCALE = 1.0 / (2048.0 * 128.0)


BF16 = jnp.bfloat16


def _split(x):
    high = x.astype(BF16)
    return high, (x - high.astype(F32)).astype(BF16)


def _left(table, axis=1):
    high, low = _split(table)
    return jnp.concatenate([high, high, low], axis)


def _right(value, axis=0):
    high, low = _split(value)
    return jnp.concatenate([high, low, high], axis)


def _mul(a, b, ca=1, cb=0):
    return lax.dot_general(a, b, (((ca,), (cb,)), ((), ())), preferred_element_type=F32)


def _cs(first, second, modulus):
    angle = 2.0 * np.pi * ((first * second) % modulus) / modulus
    return np.cos(angle), np.sin(angle)


def const_tables():
    i = np.arange
    c, s = _cs(i(16)[:, None], i(128)[None, :], 32)
    gl16 = np.concatenate([c, s], 1)
    gl32 = np.repeat(gl16, 2, axis=0)
    c, s = _cs(i(64)[:, None], i(128)[None, :], 2048)
    twist = np.concatenate([c, s], 0)
    c, s = _cs(i(16)[:, None], i(64)[None, :], 16)
    fwd = np.block([[c, s], [-s, c]])
    inv = np.block([[c.T, -s.T], [s.T, c.T]])
    back = gl16.reshape(16, 2, 128).transpose(1, 0, 2).reshape(32, 128)
    c, s = _cs(i(32)[:, None], i(32)[None, :], 32)
    fold = np.concatenate([c, s], 0)
    turn = twist.astype(np.float32)
    split = [split3(gl32, 0), split3(gl16, 0), split3(fwd, 1), split3(inv, 1), split3(back, 1), split3(fold, 1)]
    return [turn] + split


def split3(table, axis):
    table = table.astype(np.float32)
    high = table.astype(BF16)
    low = (table - high.astype(np.float32)).astype(BF16)
    return np.concatenate([high, high, low], axis)


def _iota(shape, dim):
    return lax.broadcasted_iota(jnp.int32, shape, dim)


def _angle(product, modulus):
    return (product & (modulus - 1)).astype(F32) * (2.0 * math.pi / modulus)


def first_table(zh, n0):
    row = _iota((128, 256), 0)
    col = _iota((128, 256), 1)
    ky = 64 * (row // 4) + row % 4 + 4 * n0
    y = 32 * (col // 16) + col % 16 + 512 * zh
    parts = []
    for h in (0, 1):
        t = _angle(ky * (y + 16 * h), 2048)
        parts += [_left(jnp.cos(t)), _left(-jnp.sin(t))]
    return parts


def last_table(zh, n0):
    row = _iota((16, 64), 0)
    col = _iota((16, 64), 1)
    s = 4 * (col % 16) + col // 16
    out = []
    for a in (0, 1):
        t = _angle(s * (32 * row + n0 + 16 * a + 512 * zh), 2048)
        out.append(_left(jnp.concatenate([jnp.cos(t) * TOP_SCALE, jnp.sin(t) * TOP_SCALE], 0)))
    return out


def side_table(zh, n0):
    row = _iota((16, 64), 0)
    z = _iota((16, 64), 1)
    own = jnp.where(row < 8, zh, 1 - zh)
    t = _angle((64 * own + 4 * n0 + row % 4) * z, 128)
    return _left(jnp.where(row % 8 < 4, jnp.cos(t), -jnp.sin(t)))


def side_last_table(zh, yy):
    row = _iota((16, 64), 0)
    col = _iota((16, 64), 1)
    kz = 64 * zh + 4 * (col % 16) + col // 16
    t = _angle(kz * (row + 16 * yy), 128)
    return _left(jnp.concatenate([jnp.cos(t) * SIDE_SCALE, jnp.sin(t) * SIDE_SCALE], 0))


def first_stage(w, packed, roll):
    packed = _right(packed)
    p = [_mul(t, packed) for t in w]
    low = _iota((128, 128), 1) < 64
    return jnp.where(low, p[0] + roll(p[2], 64), roll(p[1], 64) + p[3])


def side_first(w, data, roll):
    t = _mul(w, _right(data))
    low = _iota((4, 128), 1) < 64
    own, other = [], []
    for x in range(4):
        for base, out in ((0, own), (8, other)):
            o = t[base : base + 8, 128 * x : 128 * x + 128]
            q = roll(o, 64)
            f0 = jnp.where(low, o[0:4], q[4:8])
            f1 = jnp.where(low, q[0:4], o[4:8])
            out.append(jnp.concatenate([f0, f1], 0))
    return own, other


def line_stage(rows, kernel_at, tabs, roll):
    gl, twist, fwd, inv, back = tabs
    twc, tws = twist[:64], twist[64:]
    p = _mul(_right(jnp.concatenate(rows, 1)), gl, 0, 0)
    mid = []
    for r in range(4):
        q = p[128 * r : 128 * r + 128]
        bre = q[:64, :128] + q[64:, 128:]
        bim = q[64:, :128] - q[:64, 128:]
        mid.append(jnp.concatenate([bre * twc + bim * tws, bim * twc - bre * tws], 0))
    spectrum = _mul(fwd, _right(jnp.concatenate(mid, 1)))
    weighted = []
    for c in range(2):
        for r in range(4):
            sre = spectrum[:16, 128 * r : 128 * r + 128]
            sim = spectrum[16:, 128 * r : 128 * r + 128]
            kre, kim = kernel_at(c, 0, r), kernel_at(c, 1, r)
            weighted.append(
                jnp.concatenate([kre * sre + kim * sim, kre * sim - kim * sre], 0)
            )
    v = _mul(inv, _right(jnp.concatenate(weighted, 1)))
    turned = []
    for cr in range(8):
        vre = v[:64, 128 * cr : 128 * cr + 128]
        vim = v[64:, 128 * cr : 128 * cr + 128]
        turned += [vre * twc - vim * tws, vim * twc + vre * tws]
    u = _mul(back, _right(jnp.concatenate(turned, 0), 1), 1, 1)
    return spread(u, 16, roll)


def spread(u, half, roll):
    sign = jnp.where(_iota((half, 128), 1) < 64, -1.0, 1.0)
    out = []
    for cr in range(8):
        lanes = slice(128 * cr, 128 * cr + 128)
        out.append(u[:half, lanes] + sign * roll(u[half:, lanes], 64))
    return out


def fold_stage(rows, fold, roll):
    return spread(_mul(fold, _right(jnp.concatenate(rows, 1))), 32, roll)


def last_stage(table, rows, roll):
    g = _mul(table, _right(jnp.concatenate(rows, 1)))
    low = _iota((16, 128), 1) < 64
    part = [g[:16, 128 * c : 128 * c + 128] - roll(g[16:, 128 * c : 128 * c + 128], 64) for c in (0, 1)]
    return jnp.where(low, part[0], roll(part[1], 64))


def rows8(start, size):
    return pl.ds(pl.multiple_of(start, 8), size)


def body(
    mag, stiff, rtop_in, rside_in, ktop, kside, c_turn, c_gl32, c_gl16, c_fwd, c_inv, c_back, c_fold,
    exch, top,
    field, rtop, rside, twist, gl32, gl16, fwd, inv, back, fold, kraw, kt, ks,
    send1, recv1, recv1s, send2, recv2, send3, recv3, send4, recv4, send5, recv5,
    hop1, line1, send6, recv6, hop2, other2,
    hx_out_hi, hx_out_lo, hx_lo, hx_hi, hy_out_hi, hy_out_lo, hy_lo, hy_hi, col_lo, col_hi,
    local, ssem, rsem, hsend, hrecv, near, cross,
):
    gx, gy, gz = lax.axis_index("gx"), lax.axis_index("gy"), lax.axis_index("gz")
    zh, xx = lax.div(gy, 4), lax.rem(gy, 4)
    n0 = 4 * xx + gz
    m0 = 2 * gx + zh
    z, core = 8 * zh + lax.div(gx, 2), lax.rem(gx, 2)
    device = 16 * m0 + n0

    def column_index(z_plus, which):
        at = lax.rem(z_plus, 16)
        return 4 * lax.rem(at, 8) + 2 * which + lax.div(at, 8)

    def plane_id(n):
        return 16 * m0 + n

    def column_id(m):
        return 16 * m + n0

    far = jnp.where(lax.rem(gx, 16) < 8, column_id(2 * (gx + 8) + 1 - zh), column_id(2 * (gx - 8) + 1 - zh))

    def roll(value, shift):
        return pltpu.roll(value, shift, 1)

    def over_plane(action):
        for dx, dy in PLANE_ORDER:
            x = lax.rem(xx + dx, 4)
            action(4 * x + lax.rem(gz + dy, 4), x)

    def over_column(action):
        for which in (0, 1):
            action(column_index(z + 8, which))

        def step(k, carry):
            for which in (0, 1):
                action(column_index(z + 8 - k, which))
                action(column_index(z + 8 + k, which))
            return carry

        lax.fori_loop(1, 8, step, 0)
        action(column_index(z, 1 - core))

    def signal(sem, target):
        pl.semaphore_signal(sem, inc=1, device_id=target, device_id_type=LOGICAL)

    def remote(src, dst, sems, target):
        send_sem, recv_sem = sems
        return pltpu.make_async_remote_copy(
            src_ref=src, dst_ref=dst, send_sem=send_sem, recv_sem=recv_sem,
            device_id=target, device_id_type=LOGICAL,
        )

    def wait_bytes(ref, sem):
        pltpu.make_async_copy(ref, ref, sem).wait()

    def pair(i):
        return ssem.at[i], rsem.at[i]

    residuals = [
        pltpu.make_async_copy(rtop_in, rtop, local.at[4]),
        pltpu.make_async_copy(rside_in, rside, local.at[5]),
    ]
    loads = [
        pltpu.make_async_copy(src, dst, local.at[6 + i])
        for i, (src, dst) in enumerate(
            [(c_turn, twist), (c_gl32, gl32), (c_gl16, gl16), (c_fwd, fwd), (c_inv, inv), (c_back, back), (c_fold, fold)]
        )
    ] + [
        pltpu.make_async_copy(mag, field.at[0:3, pl.ds(64, 1024)], local.at[0]),
        pltpu.make_async_copy(stiff, field.at[3:4, pl.ds(64, 1024)], local.at[1]),
        pltpu.make_async_copy(ktop, kraw.at[0], local.at[2]),
        pltpu.make_async_copy(kside, kraw.at[1], local.at[3]),
    ]
    for load in residuals + loads:
        load.start()
    barrier = pltpu.get_barrier_semaphore()
    over_plane(lambda n, x: signal(barrier, plane_id(n)))

    def greet(k, carry):
        for which in (0, 1):
            signal(barrier, column_id(column_index(z + k, which)))
            signal(barrier, column_id(column_index(z + 16 - k, which)))
        return carry

    lax.fori_loop(1, 5, greet, 0)
    signal(barrier, column_id(column_index(z, 1 - core)))

    for load in residuals:
        load.wait()
    send1[...] = jnp.concatenate([rtop[0:16, :], rtop[16:32, :]], 1)
    recv1[rows8(16 * n0, 16), :] = send1[...]
    recv1s[rows8(16 * n0, 16), :] = rside[...]

    pl.semaphore_wait(barrier, 32)

    over_plane(
        lambda n, x: remote(send1, recv1.at[rows8(16 * n0, 16)], pair(0), plane_id(n)).start()
    )
    over_plane(
        lambda n, x: remote(rside, recv1s.at[rows8(16 * n0, 16)], pair(8), plane_id(n)).start()
    )

    signal(near, column_id(column_index(z + 4, core)))
    signal(near, column_id(column_index(z + 12, core)))

    for load in loads:
        load.wait()
    zero_face = jnp.zeros((64, 128), F32)
    for c in range(4):
        hx_out_hi[16 * c : 16 * c + 16, :] = field[c, pl.ds(64 + 63, 16, stride=64), :]
        hx_out_lo[16 * c : 16 * c + 16, :] = field[c, pl.ds(64, 16, stride=64), :]
    lane = _iota((64, 128), 1)

    def pack(z, carry):
        hi, lo = carry
        for c in range(4):
            at = 16 * c + z
            turned = pltpu.roll(field[c, rows8(64 + 64 * z, 64), :], at + 1, 1)
            hi = jnp.where(lane == at, turned, hi)
            lo = jnp.where(lane == at + 1, turned, lo)
        return hi, lo

    packed_hi, packed_lo = lax.fori_loop(0, 16, pack, (zero_face, zero_face))
    low = _iota((32, 128), 1) < 64
    hy_out_hi[...] = jnp.where(low, packed_hi[:32], roll(packed_hi[32:], 64))
    hy_out_lo[...] = jnp.where(low, roll(packed_lo[:32], 127), roll(packed_lo[32:], 63))

    x_up = (gx < 15, remote(hx_out_hi, hx_lo, (hsend.at[0], hrecv.at[0]), device + 32))
    x_dn = (gx > 0, remote(hx_out_lo, hx_hi, (hsend.at[1], hrecv.at[1]), device - 32))
    y_up = (gy < 7, remote(hy_out_hi, hy_lo, (hsend.at[2], hrecv.at[2]), device + 4))
    y_dn = (gy > 0, remote(hy_out_lo, hy_hi, (hsend.at[3], hrecv.at[3]), device - 4))
    z_up = (
        gz < 3,
        remote(field.at[:, pl.ds(1024, 64)], field.at[:, pl.ds(0, 64)],
               (hsend.at[4], hrecv.at[4]), device + 1),
    )
    z_dn = (
        gz > 0,
        remote(field.at[:, pl.ds(64, 64)], field.at[:, pl.ds(1088, 64)],
               (hsend.at[5], hrecv.at[5]), device - 1),
    )
    faces = (y_up, y_dn, z_up, z_dn, x_up, x_dn)
    for there, copy in faces[4:]:

        @pl.when(there)
        def _(copy=copy):
            copy.start()

    pl.semaphore_wait(near, 2)
    for at in (0, 7):

        @pl.when(gy == at)
        def _(at=at):
            signal(cross, device + (12 if at == 0 else -12))

    for missing, ref in ((gx == 0, hx_lo), (gx == 15, hx_hi), (gy == 0, hy_lo), (gy == 7, hy_hi)):

        @pl.when(missing)
        def _(ref=ref):
            ref[...] = zero_face[: ref.shape[0]]

    for missing, start in ((gz == 0, 0), (gz == 3, 1088)):

        @pl.when(missing)
        def _(start=start):
            for c in range(4):
                field[c, pl.ds(start, 64), :] = zero_face

    for which, out in ((0, kt), (1, ks)):
        for cp in range(4):
            for j in range(16):
                out[pl.ds(64 * cp + j, 4, stride=16), :] = kraw[
                    which, cp // 2, cp % 2, :, 128 * j : 128 * j + 128
                ]

    table1 = first_table(zh, n0)
    table_side = side_table(zh, n0)
    table_last = last_table(zh, n0)
    table_side_last = side_last_table(zh, gz)

    for at, copy in ((3, y_up[1]), (4, y_dn[1])):

        @pl.when(gy == at)
        def _(copy=copy):
            pl.semaphore_wait(cross, 1)
            copy.start()

    wait_bytes(recv1.at[pl.ds(0, 240)], rsem.at[0])
    first = first_stage(table1, recv1[...], roll)
    for m in range(32):
        send2[m] = first[4 * m : 4 * m + 4]
    recv2[m0] = send2[m0]
    over_column(lambda m: remote(send2.at[m], recv2.at[m0], pair(1), column_id(m)).start())

    inside = (
        (jnp.logical_and(gy < 7, gy != 3), y_up[1]),
        (jnp.logical_and(gy > 0, gy != 4), y_dn[1]),
    ) + faces[2:4]
    for there, copy in inside:

        @pl.when(there)
        def _(copy=copy):
            copy.start()

    wait_bytes(recv1s.at[pl.ds(0, 240)], rsem.at[8])
    data = jnp.concatenate([recv1s[64 * x : 64 * x + 64, :] for x in range(4)], 1)
    own, other = side_first(table_side, data, roll)
    for x in range(4):
        line1[rows8(32 * zh + 8 * x, 8), :] = own[x]
        hop1[8 * x : 8 * x + 8, :] = other[x]
    remote(hop1, line1.at[rows8(32 * zh, 32)], pair(5), far).start()

    wait_bytes(recv2.at[pl.ds(0, 31)], rsem.at[1])
    shared = (twist[...], fwd[...], inv[...], back[...])
    lines = line_stage(
        [recv2[:, r, :] for r in range(4)],
        lambda c, p, r: kt[64 * (2 * c + p) + 16 * r : 64 * (2 * c + p) + 16 * r + 16, :],
        (gl32[...],) + shared,
        roll,
    )
    for cr in range(8):
        send3[pl.ds(cr, 16, stride=8), :] = lines[cr]
    recv3[rows8(8 * m0, 8), :] = send3[rows8(8 * gx, 8), :]
    over_column(
        lambda m: remote(
            send3.at[rows8(8 * lax.div(m, 2), 8)], recv3.at[rows8(8 * m0, 8)], pair(2), column_id(m)
        ).start()
    )

    wait_bytes(line1.at[pl.ds(0, 32)], rsem.at[5])
    lines = line_stage(
        [line1[pl.ds(r, 16, stride=4), :] for r in range(4)],
        lambda c, p, r: ks[64 * (2 * c + p) + 16 * r : 64 * (2 * c + p) + 16 * r + 16, :],
        (gl16[...],) + shared,
        roll,
    )
    for cr in range(8):
        for h in range(2):
            send6[h, pl.ds(cr, 8, stride=8), :] = lines[cr][8 * h : 8 * h + 8]
    recv6[:, rows8(16 * n0, 16), :] = send6[:, rows8(16 * xx, 16), :]
    over_plane(
        lambda n, x: remote(
            send6.at[:, rows8(16 * x, 16)], recv6.at[:, rows8(16 * n0, 16)], pair(6), plane_id(n)
        ).start()
    )

    wait_bytes(recv3.at[pl.ds(0, 248)], rsem.at[2])
    folded = fold_stage([recv3[pl.ds(cr, 32, stride=8), :] for cr in range(8)], fold[...], roll)
    for cr in range(8):
        send4[pl.ds(cr, 16, stride=16), :] = folded[cr][:16]
        send4[pl.ds(8 + cr, 16, stride=16), :] = folded[cr][16:]
    recv4[rows8(16 * n0, 16), :] = send4[rows8(16 * n0, 16), :]
    over_plane(
        lambda n, x: remote(
            send4.at[rows8(16 * n, 16)], recv4.at[rows8(16 * n0, 16)], pair(3), plane_id(n)
        ).start()
    )

    wait_bytes(recv6.at[:, pl.ds(0, 240)], rsem.at[6])
    columns = [
        jnp.concatenate([recv6[h, pl.ds(8 * e + 4 * c + r, 16, stride=16), :] for r in range(4)], 0)
        for h in (zh, 1 - zh)
        for c in range(2)
        for e in range(2)
    ]
    g = _mul(table_side_last, _right(jnp.concatenate(columns, 1)))
    low = _iota((16, 128), 1) < 64
    halves = [
        g[:16, 128 * q : 128 * q + 128] - roll(g[16:, 128 * q : 128 * q + 128], 64) for q in range(8)
    ]
    sums = [jnp.where(low, halves[q], roll(halves[q + 1], 64)) for q in (0, 2, 4, 6)]
    hop2[0:16, :], hop2[16:32, :] = sums[2], sums[3]
    remote(hop2, other2, pair(7), far).start()

    arrivals = (
        (gx > 0, hx_lo, 0), (gx < 15, hx_hi, 1), (gy > 0, hy_lo, 2), (gy < 7, hy_hi, 3),
        (gz > 0, field.at[:, pl.ds(0, 64)], 4), (gz < 3, field.at[:, pl.ds(1088, 64)], 5),
    )
    for there, ref, i in arrivals:

        @pl.when(there)
        def _(ref=ref, i=i):
            wait_bytes(ref, hrecv.at[i])

    for ref, out in ((hy_lo, col_lo), (hy_hi, col_hi)):
        out[0:32, :] = ref[...]
        out[32:64, :] = roll(ref[...], 64)
    sub = _iota((64, 128), 0)

    def exchange(z, carry):
        def slab(c, step):
            return field[c, rows8(64 + 64 * (z + step), 64), :]

        def around(c):
            at = 16 * c + z
            center = slab(c, 0)
            below = jnp.where(sub == 0, hx_lo[pl.ds(at, 1), :], pltpu.roll(center, 1, 0))
            above = jnp.where(sub == 63, hx_hi[pl.ds(at, 1), :], pltpu.roll(center, 63, 0))
            left = jnp.where(lane == 0, pltpu.roll(col_lo[...], 128 - at, 1), pltpu.roll(center, 1, 1))
            right = jnp.where(
                lane == 127, pltpu.roll(col_hi[...], 127 - at, 1), pltpu.roll(center, 127, 1)
            )
            return center, (slab(c, -1), slab(c, 1), below, above, left, right)

        a, near = around(3)
        weights = [4.0 * a * b / (a + b) for b in near]
        for c in range(3):
            m, beside = around(c)
            total = weights[0] * (m - beside[0])
            for w, b in zip(weights[1:], beside[1:]):
                total = total + w * (m - b)
            exch[c, rows8(64 * z, 64), :] = total
        return carry

    lax.fori_loop(0, 16, exchange, 0)

    wait_bytes(recv4.at[pl.ds(0, 240)], rsem.at[3])
    for a in range(2):
        rows = [
            jnp.concatenate(
                [recv4[pl.ds(8 * a + 4 * c + r, 16, stride=16), :] for r in range(4)], 0
            )
            for c in range(2)
        ]
        send5[pl.ds(a, 16, stride=2), :] = last_stage(table_last[a], rows, roll)
    recv5[rows8(8 * n0, 8), :] = send5[rows8(8 * xx, 8), :]
    over_plane(
        lambda n, x: remote(
            send5.at[rows8(8 * x, 8)], recv5.at[rows8(8 * n0, 8)], pair(4), plane_id(n)
        ).start()
    )

    wait_bytes(other2, rsem.at[7])
    for c in range(2):
        side = sums[c] + other2[16 * c : 16 * c + 16, :]
        for at in range(16):
            rows = slice(64 * at, 64 * at + 64)
            exch[c + 1, rows, :] = exch[c + 1, rows, :] + side[at : at + 1, :]

    wait_bytes(recv1.at[pl.ds(0, 240)], ssem.at[0])
    wait_bytes(recv1s.at[pl.ds(0, 240)], ssem.at[8])
    wait_bytes(send2.at[pl.ds(0, 31)], ssem.at[1])
    wait_bytes(recv3.at[pl.ds(0, 248)], ssem.at[2])
    wait_bytes(recv4.at[pl.ds(0, 240)], ssem.at[3])
    wait_bytes(hop1, ssem.at[5])
    wait_bytes(recv6.at[:, pl.ds(0, 240)], ssem.at[6])
    wait_bytes(hop2, ssem.at[7])
    for there, copy in faces:

        @pl.when(there)
        def _(copy=copy):
            copy.wait_send()

    wait_bytes(recv5.at[pl.ds(0, 120)], rsem.at[4])
    lines_y = jnp.concatenate([recv5[pl.ds(q, 16, stride=8), :] for q in range(8)], 0)
    top[0:128, :] = lines_y.T
    top[128:192, :] = zero_face
    wait_bytes(recv5.at[pl.ds(0, 120)], ssem.at[4])


def on_device(magnetization, stiffness, residual_top, residual_side, top_kernel, side_kernel):
    tables = [jnp.asarray(t) for t in const_tables()]
    vmem = pl.BlockSpec(memory_space=pltpu.VMEM)
    hbm = pl.BlockSpec(memory_space=pltpu.HBM)

    def pin(array):
        return pltpu.with_memory_space_constraint(array, pltpu.HBM)

    def buf(*shape):
        return pltpu.VMEM(shape, F32)

    scratch = [
        buf(4, 1152, 128), buf(32, 64), buf(16, 128), *[pltpu.VMEM(t.shape, t.dtype) for t in tables], buf(2, 2, 2, 4, 2048), buf(256, 128), buf(256, 128),
        buf(16, 128), buf(256, 128), buf(256, 128), buf(32, 4, 128), buf(32, 4, 128),
        buf(128, 128), buf(256, 128), buf(256, 128), buf(256, 128), buf(32, 128), buf(128, 128),
        buf(32, 128), buf(64, 128), buf(2, 64, 128), buf(2, 256, 128), buf(32, 128), buf(32, 128),
        buf(64, 128), buf(64, 128), buf(64, 128), buf(64, 128),
        buf(32, 128), buf(32, 128), buf(32, 128), buf(32, 128), buf(64, 128), buf(64, 128),
        pltpu.SemaphoreType.DMA((13,)), pltpu.SemaphoreType.DMA((9,)), pltpu.SemaphoreType.DMA((9,)),
        pltpu.SemaphoreType.DMA((6,)), pltpu.SemaphoreType.DMA((6,)),
        pltpu.SemaphoreType.REGULAR, pltpu.SemaphoreType.REGULAR,
    ]
    exch, top = pl.pallas_call(
        body,
        out_shape=[
            jax.ShapeDtypeStruct((3, 1024, 128), F32),
            jax.ShapeDtypeStruct((192, 128), F32),
        ],
        in_specs=[hbm] * (6 + len(tables)),
        out_specs=[vmem] * 2,
        scratch_shapes=scratch,
        compiler_params=pltpu.CompilerParams(
            collective_id=0, has_side_effects=True, vmem_limit_bytes=40 * 1024 * 1024
        ),
        name="adjoint",
    )(
        pin(magnetization.reshape(3, 1024, 128)),
        pin(stiffness.reshape(1, 1024, 128)),
        pin(residual_top.T),
        pin(residual_side.T),
        pin(top_kernel),
        pin(side_kernel),
        *[pin(t) for t in tables],
    )
    return exch.reshape(3, 16, 64, 128) + top.reshape(3, 1, 64, 128)


def solution(mesh):
    placed = (
        P(None, "gz", "gx", "gy"),
        P("gz", "gx", "gy"),
        P("gx", ("gy", "gz")),
        P("gy", "gz"),
        P(None, None, ("gx", "gy", "gz"), None),
        P(None, None, ("gy", "gz"), None),
    )
    return jax.shard_map(
        on_device, mesh=mesh, in_specs=placed, out_specs=P(None, "gz", "gx", "gy"), check_vma=False
    )
```

```python
import math

import jax
import jax.numpy as jnp
import numpy as np
from jax import lax
from jax.experimental import pallas as pl
from jax.experimental.pallas import tpu as pltpu
from jax.sharding import PartitionSpec as P

F32 = jnp.float32
LOGICAL = pl.DeviceIdType.LOGICAL
PLANE_ORDER = sorted(
    [(dx, dy) for dx in range(4) for dy in range(4) if dx or dy],
    key=lambda d: -(min(d[0], 4 - d[0]) + min(d[1], 4 - d[1])),
)
TOP_SCALE = 1.0 / 2048.0**2
SIDE_SCALE = 1.0 / (2048.0 * 128.0)


BF16 = jnp.bfloat16


def _split(x):
    high = x.astype(BF16)
    return high, (x - high.astype(F32)).astype(BF16)


def _left(table, axis=1):
    high, low = _split(table)
    return jnp.concatenate([high, high, low], axis)


def _right(value, axis=0):
    high, low = _split(value)
    return jnp.concatenate([high, low, high], axis)


def _mul(a, b, ca=1, cb=0):
    return lax.dot_general(a, b, (((ca,), (cb,)), ((), ())), preferred_element_type=F32)


def _cs(first, second, modulus):
    angle = 2.0 * np.pi * ((first * second) % modulus) / modulus
    return np.cos(angle), np.sin(angle)


def const_tables():
    i = np.arange
    c, s = _cs(i(16)[:, None], i(128)[None, :], 32)
    gl16 = np.concatenate([c, s], 1)
    gl32 = np.repeat(gl16, 2, axis=0)
    c, s = _cs(i(64)[:, None], i(128)[None, :], 2048)
    twist = np.concatenate([c, s], 0)
    c, s = _cs(i(16)[:, None], i(64)[None, :], 16)
    fwd = np.block([[c, s], [-s, c]])
    inv = np.block([[c.T, -s.T], [s.T, c.T]])
    back = gl16.reshape(16, 2, 128).transpose(1, 0, 2).reshape(32, 128)
    c, s = _cs(i(32)[:, None], i(32)[None, :], 32)
    fold = np.concatenate([c, s], 0)
    turn = twist.astype(np.float32)
    split = [split3(gl32, 0), split3(gl16, 0), split3(fwd, 1), split3(inv, 1), split3(back, 1), split3(fold, 1)]
    return [turn] + split


def split3(table, axis):
    table = table.astype(np.float32)
    high = table.astype(BF16)
    low = (table - high.astype(np.float32)).astype(BF16)
    return np.concatenate([high, high, low], axis)


def _iota(shape, dim):
    return lax.broadcasted_iota(jnp.int32, shape, dim)


def _angle(product, modulus):
    return (product & (modulus - 1)).astype(F32) * (2.0 * math.pi / modulus)


def first_table(zh, n0):
    row = _iota((128, 256), 0)
    col = _iota((128, 256), 1)
    ky = 64 * (row // 4) + row % 4 + 4 * n0
    y = 32 * (col // 16) + col % 16 + 512 * zh
    parts = []
    for h in (0, 1):
        t = _angle(ky * (y + 16 * h), 2048)
        parts += [_left(jnp.cos(t)), _left(-jnp.sin(t))]
    return parts


def last_table(zh, n0):
    row = _iota((16, 64), 0)
    col = _iota((16, 64), 1)
    s = 4 * (col % 16) + col // 16
    out = []
    for a in (0, 1):
        t = _angle(s * (32 * row + n0 + 16 * a + 512 * zh), 2048)
        out.append(_left(jnp.concatenate([jnp.cos(t) * TOP_SCALE, jnp.sin(t) * TOP_SCALE], 0)))
    return out


def side_table(zh, n0):
    row = _iota((16, 64), 0)
    z = _iota((16, 64), 1)
    own = jnp.where(row < 8, zh, 1 - zh)
    t = _angle((64 * own + 4 * n0 + row % 4) * z, 128)
    return _left(jnp.where(row % 8 < 4, jnp.cos(t), -jnp.sin(t)))


def side_last_table(zh, yy):
    row = _iota((16, 64), 0)
    col = _iota((16, 64), 1)
    kz = 64 * zh + 4 * (col % 16) + col // 16
    t = _angle(kz * (row + 16 * yy), 128)
    return _left(jnp.concatenate([jnp.cos(t) * SIDE_SCALE, jnp.sin(t) * SIDE_SCALE], 0))


def first_stage(w, packed, roll):
    packed = _right(packed)
    p = [_mul(t, packed) for t in w]
    low = _iota((128, 128), 1) < 64
    return jnp.where(low, p[0] + roll(p[2], 64), roll(p[1], 64) + p[3])


def side_first(w, data, roll):
    t = _mul(w, _right(data))
    low = _iota((4, 128), 1) < 64
    own, other = [], []
    for x in range(4):
        for base, out in ((0, own), (8, other)):
            o = t[base : base + 8, 128 * x : 128 * x + 128]
            q = roll(o, 64)
            f0 = jnp.where(low, o[0:4], q[4:8])
            f1 = jnp.where(low, q[0:4], o[4:8])
            out.append(jnp.concatenate([f0, f1], 0))
    return own, other


def line_stage(rows, kernel_at, tabs, roll):
    gl, twist, fwd, inv, back = tabs
    twc, tws = twist[:64], twist[64:]
    p = _mul(_right(jnp.concatenate(rows, 1)), gl, 0, 0)
    mid = []
    for r in range(4):
        q = p[128 * r : 128 * r + 128]
        bre = q[:64, :128] + q[64:, 128:]
        bim = q[64:, :128] - q[:64, 128:]
        mid.append(jnp.concatenate([bre * twc + bim * tws, bim * twc - bre * tws], 0))
    spectrum = _mul(fwd, _right(jnp.concatenate(mid, 1)))
    weighted = []
    for c in range(2):
        for r in range(4):
            sre = spectrum[:16, 128 * r : 128 * r + 128]
            sim = spectrum[16:, 128 * r : 128 * r + 128]
            kre, kim = kernel_at(c, 0, r), kernel_at(c, 1, r)
            weighted.append(
                jnp.concatenate([kre * sre + kim * sim, kre * sim - kim * sre], 0)
            )
    v = _mul(inv, _right(jnp.concatenate(weighted, 1)))
    turned = []
    for cr in range(8):
        vre = v[:64, 128 * cr : 128 * cr + 128]
        vim = v[64:, 128 * cr : 128 * cr + 128]
        turned += [vre * twc - vim * tws, vim * twc + vre * tws]
    u = _mul(back, _right(jnp.concatenate(turned, 0), 1), 1, 1)
    return spread(u, 16, roll)


def spread(u, half, roll):
    sign = jnp.where(_iota((half, 128), 1) < 64, -1.0, 1.0)
    out = []
    for cr in range(8):
        lanes = slice(128 * cr, 128 * cr + 128)
        out.append(u[:half, lanes] + sign * roll(u[half:, lanes], 64))
    return out


def fold_stage(rows, fold, roll):
    return spread(_mul(fold, _right(jnp.concatenate(rows, 1))), 32, roll)


def last_stage(table, rows, roll):
    g = _mul(table, _right(jnp.concatenate(rows, 1)))
    low = _iota((16, 128), 1) < 64
    part = [g[:16, 128 * c : 128 * c + 128] - roll(g[16:, 128 * c : 128 * c + 128], 64) for c in (0, 1)]
    return jnp.where(low, part[0], roll(part[1], 64))


def rows8(start, size):
    return pl.ds(pl.multiple_of(start, 8), size)


def body(
    mag, stiff, rtop_in, rside_in, ktop, kside, c_turn, c_gl32, c_gl16, c_fwd, c_inv, c_back, c_fold,
    exch, top,
    field, rtop, rside, twist, gl32, gl16, fwd, inv, back, fold, kraw, kt, ks,
    send1, recv1, recv1s, send2, recv2, send3, recv3, send4, recv4, send5, recv5,
    hop1, line1, send6, recv6, hop2, other2,
    hx_out_hi, hx_out_lo, hx_lo, hx_hi, hy_out_hi, hy_out_lo, hy_lo, hy_hi, col_lo, col_hi,
    local, ssem, rsem, hsend, hrecv, near, cross,
):
    gx, gy, gz = lax.axis_index("gx"), lax.axis_index("gy"), lax.axis_index("gz")
    zh, xx = lax.div(gy, 4), lax.rem(gy, 4)
    n0 = 4 * xx + gz
    m0 = 2 * gx + zh
    z, core = 8 * zh + lax.div(gx, 2), lax.rem(gx, 2)
    device = 16 * m0 + n0

    def column_index(z_plus, which):
        at = lax.rem(z_plus, 16)
        return 4 * lax.rem(at, 8) + 2 * which + lax.div(at, 8)

    def plane_id(n):
        return 16 * m0 + n

    def column_id(m):
        return 16 * m + n0

    far = jnp.where(lax.rem(gx, 16) < 8, column_id(2 * (gx + 8) + 1 - zh), column_id(2 * (gx - 8) + 1 - zh))

    def roll(value, shift):
        return pltpu.roll(value, shift, 1)

    def over_plane(action):
        for dx, dy in PLANE_ORDER:
            x = lax.rem(xx + dx, 4)
            action(4 * x + lax.rem(gz + dy, 4), x)

    def over_column(action):
        for which in (0, 1):
            action(column_index(z + 8, which))

        def step(k, carry):
            for which in (0, 1):
                action(column_index(z + 8 - k, which))
                action(column_index(z + 8 + k, which))
            return carry

        lax.fori_loop(1, 8, step, 0)
        action(column_index(z, 1 - core))

    def signal(sem, target):
        pl.semaphore_signal(sem, inc=1, device_id=target, device_id_type=LOGICAL)

    def remote(src, dst, sems, target):
        send_sem, recv_sem = sems
        return pltpu.make_async_remote_copy(
            src_ref=src, dst_ref=dst, send_sem=send_sem, recv_sem=recv_sem,
            device_id=target, device_id_type=LOGICAL,
        )

    def wait_bytes(ref, sem):
        pltpu.make_async_copy(ref, ref, sem).wait()

    def pair(i):
        return ssem.at[i], rsem.at[i]

    residuals = [
        pltpu.make_async_copy(rtop_in, rtop, local.at[4]),
        pltpu.make_async_copy(rside_in, rside, local.at[5]),
    ]
    loads = [
        pltpu.make_async_copy(src, dst, local.at[6 + i])
        for i, (src, dst) in enumerate(
            [(c_turn, twist), (c_gl32, gl32), (c_gl16, gl16), (c_fwd, fwd), (c_inv, inv), (c_back, back), (c_fold, fold)]
        )
    ] + [
        pltpu.make_async_copy(mag, field.at[0:3, pl.ds(64, 1024)], local.at[0]),
        pltpu.make_async_copy(stiff, field.at[3:4, pl.ds(64, 1024)], local.at[1]),
        pltpu.make_async_copy(ktop, kraw.at[0], local.at[2]),
        pltpu.make_async_copy(kside, kraw.at[1], local.at[3]),
    ]
    for load in residuals + loads:
        load.start()
    barrier = pltpu.get_barrier_semaphore()
    over_plane(lambda n, x: signal(barrier, plane_id(n)))

    def greet(k, carry):
        for which in (0, 1):
            signal(barrier, column_id(column_index(z + k, which)))
            signal(barrier, column_id(column_index(z + 16 - k, which)))
        return carry

    lax.fori_loop(1, 5, greet, 0)
    signal(barrier, column_id(column_index(z, 1 - core)))

    for load in residuals:
        load.wait()
    send1[...] = jnp.concatenate([rtop[0:16, :], rtop[16:32, :]], 1)
    recv1[rows8(16 * n0, 16), :] = send1[...]
    recv1s[rows8(16 * n0, 16), :] = rside[...]

    pl.semaphore_wait(barrier, 32)

    over_plane(
        lambda n, x: remote(send1, recv1.at[rows8(16 * n0, 16)], pair(0), plane_id(n)).start()
    )

    signal(near, column_id(column_index(z + 4, core)))
    signal(near, column_id(column_index(z + 12, core)))

    for load in loads:
        load.wait()
    zero_face = jnp.zeros((64, 128), F32)
    for c in range(4):
        hx_out_hi[16 * c : 16 * c + 16, :] = field[c, pl.ds(64 + 63, 16, stride=64), :]
        hx_out_lo[16 * c : 16 * c + 16, :] = field[c, pl.ds(64, 16, stride=64), :]
    lane = _iota((64, 128), 1)

    def pack(z, carry):
        hi, lo = carry
        for c in range(4):
            at = 16 * c + z
            turned = pltpu.roll(field[c, rows8(64 + 64 * z, 64), :], at + 1, 1)
            hi = jnp.where(lane == at, turned, hi)
            lo = jnp.where(lane == at + 1, turned, lo)
        return hi, lo

    packed_hi, packed_lo = lax.fori_loop(0, 16, pack, (zero_face, zero_face))
    low = _iota((32, 128), 1) < 64
    hy_out_hi[...] = jnp.where(low, packed_hi[:32], roll(packed_hi[32:], 64))
    hy_out_lo[...] = jnp.where(low, roll(packed_lo[:32], 127), roll(packed_lo[32:], 63))

    x_up = (gx < 15, remote(hx_out_hi, hx_lo, (hsend.at[0], hrecv.at[0]), device + 32))
    x_dn = (gx > 0, remote(hx_out_lo, hx_hi, (hsend.at[1], hrecv.at[1]), device - 32))
    y_up = (gy < 7, remote(hy_out_hi, hy_lo, (hsend.at[2], hrecv.at[2]), device + 4))
    y_dn = (gy > 0, remote(hy_out_lo, hy_hi, (hsend.at[3], hrecv.at[3]), device - 4))
    z_up = (
        gz < 3,
        remote(field.at[:, pl.ds(1024, 64)], field.at[:, pl.ds(0, 64)],
               (hsend.at[4], hrecv.at[4]), device + 1),
    )
    z_dn = (
        gz > 0,
        remote(field.at[:, pl.ds(64, 64)], field.at[:, pl.ds(1088, 64)],
               (hsend.at[5], hrecv.at[5]), device - 1),
    )
    faces = (y_up, y_dn, z_up, z_dn, x_up, x_dn)
    for there, copy in faces[4:]:

        @pl.when(there)
        def _(copy=copy):
            copy.start()

    over_plane(
        lambda n, x: remote(rside, recv1s.at[rows8(16 * n0, 16)], pair(8), plane_id(n)).start()
    )

    pl.semaphore_wait(near, 2)
    for at in (0, 7):

        @pl.when(gy == at)
        def _(at=at):
            signal(cross, device + (12 if at == 0 else -12))

    for missing, ref in ((gx == 0, hx_lo), (gx == 15, hx_hi), (gy == 0, hy_lo), (gy == 7, hy_hi)):

        @pl.when(missing)
        def _(ref=ref):
            ref[...] = zero_face[: ref.shape[0]]

    for missing, start in ((gz == 0, 0), (gz == 3, 1088)):

        @pl.when(missing)
        def _(start=start):
            for c in range(4):
                field[c, pl.ds(start, 64), :] = zero_face

    for which, out in ((0, kt), (1, ks)):
        for cp in range(4):
            for j in range(16):
                out[pl.ds(64 * cp + j, 4, stride=16), :] = kraw[
                    which, cp // 2, cp % 2, :, 128 * j : 128 * j + 128
                ]

    table1 = first_table(zh, n0)
    table_side = side_table(zh, n0)
    table_last = last_table(zh, n0)
    table_side_last = side_last_table(zh, gz)

    wait_bytes(recv1.at[pl.ds(0, 240)], rsem.at[0])
    first = first_stage(table1, recv1[...], roll)
    for m in range(32):
        send2[m] = first[4 * m : 4 * m + 4]
    recv2[m0] = send2[m0]
    over_column(lambda m: remote(send2.at[m], recv2.at[m0], pair(1), column_id(m)).start())

    inside = (
        (jnp.logical_and(gy < 7, gy != 3), y_up[1]),
        (jnp.logical_and(gy > 0, gy != 4), y_dn[1]),
    ) + faces[2:4]
    for there, copy in inside:

        @pl.when(there)
        def _(copy=copy):
            copy.start()

    wait_bytes(recv1s.at[pl.ds(0, 240)], rsem.at[8])
    data = jnp.concatenate([recv1s[64 * x : 64 * x + 64, :] for x in range(4)], 1)
    own, other = side_first(table_side, data, roll)
    for x in range(4):
        line1[rows8(32 * zh + 8 * x, 8), :] = own[x]
        hop1[8 * x : 8 * x + 8, :] = other[x]
    remote(hop1, line1.at[rows8(32 * zh, 32)], pair(5), far).start()

    for at, copy in ((3, y_up[1]), (4, y_dn[1])):

        @pl.when(gy == at)
        def _(copy=copy):
            pl.semaphore_wait(cross, 1)
            copy.start()

    wait_bytes(recv2.at[pl.ds(0, 31)], rsem.at[1])
    shared = (twist[...], fwd[...], inv[...], back[...])
    lines = line_stage(
        [recv2[:, r, :] for r in range(4)],
        lambda c, p, r: kt[64 * (2 * c + p) + 16 * r : 64 * (2 * c + p) + 16 * r + 16, :],
        (gl32[...],) + shared,
        roll,
    )
    for cr in range(8):
        send3[pl.ds(cr, 16, stride=8), :] = lines[cr]
    recv3[rows8(8 * m0, 8), :] = send3[rows8(8 * gx, 8), :]
    over_column(
        lambda m: remote(
            send3.at[rows8(8 * lax.div(m, 2), 8)], recv3.at[rows8(8 * m0, 8)], pair(2), column_id(m)
        ).start()
    )

    wait_bytes(line1.at[pl.ds(0, 32)], rsem.at[5])
    lines = line_stage(
        [line1[pl.ds(r, 16, stride=4), :] for r in range(4)],
        lambda c, p, r: ks[64 * (2 * c + p) + 16 * r : 64 * (2 * c + p) + 16 * r + 16, :],
        (gl16[...],) + shared,
        roll,
    )
    for cr in range(8):
        for h in range(2):
            send6[h, pl.ds(cr, 8, stride=8), :] = lines[cr][8 * h : 8 * h + 8]
    recv6[:, rows8(16 * n0, 16), :] = send6[:, rows8(16 * xx, 16), :]
    over_plane(
        lambda n, x: remote(
            send6.at[:, rows8(16 * x, 16)], recv6.at[:, rows8(16 * n0, 16)], pair(6), plane_id(n)
        ).start()
    )

    wait_bytes(recv3.at[pl.ds(0, 248)], rsem.at[2])
    folded = fold_stage([recv3[pl.ds(cr, 32, stride=8), :] for cr in range(8)], fold[...], roll)
    for cr in range(8):
        send4[pl.ds(cr, 16, stride=16), :] = folded[cr][:16]
        send4[pl.ds(8 + cr, 16, stride=16), :] = folded[cr][16:]
    recv4[rows8(16 * n0, 16), :] = send4[rows8(16 * n0, 16), :]
    over_plane(
        lambda n, x: remote(
            send4.at[rows8(16 * n, 16)], recv4.at[rows8(16 * n0, 16)], pair(3), plane_id(n)
        ).start()
    )

    wait_bytes(recv6.at[:, pl.ds(0, 240)], rsem.at[6])
    columns = [
        jnp.concatenate([recv6[h, pl.ds(8 * e + 4 * c + r, 16, stride=16), :] for r in range(4)], 0)
        for h in (zh, 1 - zh)
        for c in range(2)
        for e in range(2)
    ]
    g = _mul(table_side_last, _right(jnp.concatenate(columns, 1)))
    low = _iota((16, 128), 1) < 64
    halves = [
        g[:16, 128 * q : 128 * q + 128] - roll(g[16:, 128 * q : 128 * q + 128], 64) for q in range(8)
    ]
    sums = [jnp.where(low, halves[q], roll(halves[q + 1], 64)) for q in (0, 2, 4, 6)]
    hop2[0:16, :], hop2[16:32, :] = sums[2], sums[3]
    remote(hop2, other2, pair(7), far).start()

    arrivals = (
        (gx > 0, hx_lo, 0), (gx < 15, hx_hi, 1), (gy > 0, hy_lo, 2), (gy < 7, hy_hi, 3),
        (gz > 0, field.at[:, pl.ds(0, 64)], 4), (gz < 3, field.at[:, pl.ds(1088, 64)], 5),
    )
    for there, ref, i in arrivals:

        @pl.when(there)
        def _(ref=ref, i=i):
            wait_bytes(ref, hrecv.at[i])

    for ref, out in ((hy_lo, col_lo), (hy_hi, col_hi)):
        out[0:32, :] = ref[...]
        out[32:64, :] = roll(ref[...], 64)
    sub = _iota((64, 128), 0)

    def exchange(z, carry):
        def slab(c, step):
            return field[c, rows8(64 + 64 * (z + step), 64), :]

        def around(c):
            at = 16 * c + z
            center = slab(c, 0)
            below = jnp.where(sub == 0, hx_lo[pl.ds(at, 1), :], pltpu.roll(center, 1, 0))
            above = jnp.where(sub == 63, hx_hi[pl.ds(at, 1), :], pltpu.roll(center, 63, 0))
            left = jnp.where(lane == 0, pltpu.roll(col_lo[...], 128 - at, 1), pltpu.roll(center, 1, 1))
            right = jnp.where(
                lane == 127, pltpu.roll(col_hi[...], 127 - at, 1), pltpu.roll(center, 127, 1)
            )
            return center, (slab(c, -1), slab(c, 1), below, above, left, right)

        a, near = around(3)
        weights = [4.0 * a * b / (a + b) for b in near]
        for c in range(3):
            m, beside = around(c)
            total = weights[0] * (m - beside[0])
            for w, b in zip(weights[1:], beside[1:]):
                total = total + w * (m - b)
            exch[c, rows8(64 * z, 64), :] = total
        return carry

    lax.fori_loop(0, 16, exchange, 0)

    wait_bytes(recv4.at[pl.ds(0, 240)], rsem.at[3])
    for a in range(2):
        rows = [
            jnp.concatenate(
                [recv4[pl.ds(8 * a + 4 * c + r, 16, stride=16), :] for r in range(4)], 0
            )
            for c in range(2)
        ]
        send5[pl.ds(a, 16, stride=2), :] = last_stage(table_last[a], rows, roll)
    recv5[rows8(8 * n0, 8), :] = send5[rows8(8 * xx, 8), :]
    over_plane(
        lambda n, x: remote(
            send5.at[rows8(8 * x, 8)], recv5.at[rows8(8 * n0, 8)], pair(4), plane_id(n)
        ).start()
    )

    wait_bytes(other2, rsem.at[7])
    for c in range(2):
        side = sums[c] + other2[16 * c : 16 * c + 16, :]
        for at in range(16):
            rows = slice(64 * at, 64 * at + 64)
            exch[c + 1, rows, :] = exch[c + 1, rows, :] + side[at : at + 1, :]

    wait_bytes(recv1.at[pl.ds(0, 240)], ssem.at[0])
    wait_bytes(recv1s.at[pl.ds(0, 240)], ssem.at[8])
    wait_bytes(send2.at[pl.ds(0, 31)], ssem.at[1])
    wait_bytes(recv3.at[pl.ds(0, 248)], ssem.at[2])
    wait_bytes(recv4.at[pl.ds(0, 240)], ssem.at[3])
    wait_bytes(hop1, ssem.at[5])
    wait_bytes(recv6.at[:, pl.ds(0, 240)], ssem.at[6])
    wait_bytes(hop2, ssem.at[7])
    for there, copy in faces:

        @pl.when(there)
        def _(copy=copy):
            copy.wait_send()

    wait_bytes(recv5.at[pl.ds(0, 120)], rsem.at[4])
    lines_y = jnp.concatenate([recv5[pl.ds(q, 16, stride=8), :] for q in range(8)], 0)
    top[0:128, :] = lines_y.T
    top[128:192, :] = zero_face
    wait_bytes(recv5.at[pl.ds(0, 120)], ssem.at[4])


def on_device(magnetization, stiffness, residual_top, residual_side, top_kernel, side_kernel):
    tables = [jnp.asarray(t) for t in const_tables()]
    vmem = pl.BlockSpec(memory_space=pltpu.VMEM)
    hbm = pl.BlockSpec(memory_space=pltpu.HBM)

    def pin(array):
        return pltpu.with_memory_space_constraint(array, pltpu.HBM)

    def buf(*shape):
        return pltpu.VMEM(shape, F32)

    scratch = [
        buf(4, 1152, 128), buf(32, 64), buf(16, 128), *[pltpu.VMEM(t.shape, t.dtype) for t in tables], buf(2, 2, 2, 4, 2048), buf(256, 128), buf(256, 128),
        buf(16, 128), buf(256, 128), buf(256, 128), buf(32, 4, 128), buf(32, 4, 128),
        buf(128, 128), buf(256, 128), buf(256, 128), buf(256, 128), buf(32, 128), buf(128, 128),
        buf(32, 128), buf(64, 128), buf(2, 64, 128), buf(2, 256, 128), buf(32, 128), buf(32, 128),
        buf(64, 128), buf(64, 128), buf(64, 128), buf(64, 128),
        buf(32, 128), buf(32, 128), buf(32, 128), buf(32, 128), buf(64, 128), buf(64, 128),
        pltpu.SemaphoreType.DMA((13,)), pltpu.SemaphoreType.DMA((9,)), pltpu.SemaphoreType.DMA((9,)),
        pltpu.SemaphoreType.DMA((6,)), pltpu.SemaphoreType.DMA((6,)),
        pltpu.SemaphoreType.REGULAR, pltpu.SemaphoreType.REGULAR,
    ]
    exch, top = pl.pallas_call(
        body,
        out_shape=[
            jax.ShapeDtypeStruct((3, 1024, 128), F32),
            jax.ShapeDtypeStruct((192, 128), F32),
        ],
        in_specs=[hbm] * (6 + len(tables)),
        out_specs=[vmem] * 2,
        scratch_shapes=scratch,
        compiler_params=pltpu.CompilerParams(
            collective_id=0, has_side_effects=True, vmem_limit_bytes=40 * 1024 * 1024
        ),
        name="adjoint",
    )(
        pin(magnetization.reshape(3, 1024, 128)),
        pin(stiffness.reshape(1, 1024, 128)),
        pin(residual_top.T),
        pin(residual_side.T),
        pin(top_kernel),
        pin(side_kernel),
        *[pin(t) for t in tables],
    )
    return exch.reshape(3, 16, 64, 128) + top.reshape(3, 1, 64, 128)


def solution(mesh):
    placed = (
        P(None, "gz", "gx", "gy"),
        P("gz", "gx", "gy"),
        P("gx", ("gy", "gz")),
        P("gy", "gz"),
        P(None, None, ("gx", "gy", "gz"), None),
        P(None, None, ("gy", "gz"), None),
    )
    return jax.shard_map(
        on_device, mesh=mesh, in_specs=placed, out_specs=P(None, "gz", "gx", "gy"), check_vma=False
    )
```

```python
import math

import jax
import jax.numpy as jnp
import numpy as np
from jax import lax
from jax.experimental import pallas as pl
from jax.experimental.pallas import tpu as pltpu
from jax.sharding import PartitionSpec as P

F32 = jnp.float32
LOGICAL = pl.DeviceIdType.LOGICAL
PLANE_ORDER = sorted(
    [(dx, dy) for dx in range(4) for dy in range(4) if dx or dy],
    key=lambda d: -(min(d[0], 4 - d[0]) + min(d[1], 4 - d[1])),
)
TOP_SCALE = 1.0 / 2048.0**2
SIDE_SCALE = 1.0 / (2048.0 * 128.0)


BF16 = jnp.bfloat16


def _split(x):
    high = x.astype(BF16)
    return high, (x - high.astype(F32)).astype(BF16)


def _left(table, axis=1):
    high, low = _split(table)
    return jnp.concatenate([high, high, low], axis)


def _right(value, axis=0):
    high, low = _split(value)
    return jnp.concatenate([high, low, high], axis)


def _mul(a, b, ca=1, cb=0):
    return lax.dot_general(a, b, (((ca,), (cb,)), ((), ())), preferred_element_type=F32)


def _cs(first, second, modulus):
    angle = 2.0 * np.pi * ((first * second) % modulus) / modulus
    return np.cos(angle), np.sin(angle)


def const_tables():
    i = np.arange
    c, s = _cs(i(16)[:, None], i(128)[None, :], 32)
    gl16 = np.concatenate([c, s], 1)
    gl32 = np.repeat(gl16, 2, axis=0)
    c, s = _cs(i(64)[:, None], i(128)[None, :], 2048)
    twist = np.concatenate([c, s], 0)
    c, s = _cs(i(16)[:, None], i(64)[None, :], 16)
    fwd = np.block([[c, s], [-s, c]])
    inv = np.block([[c.T, -s.T], [s.T, c.T]])
    back = gl16.reshape(16, 2, 128).transpose(1, 0, 2).reshape(32, 128)
    c, s = _cs(i(32)[:, None], i(32)[None, :], 32)
    fold = np.concatenate([c, s], 0)
    turn = twist.astype(np.float32)
    split = [split3(gl32, 0), split3(gl16, 0), split3(fwd, 1), split3(inv, 1), split3(back, 1), split3(fold, 1)]
    return [turn] + split


def split3(table, axis):
    table = table.astype(np.float32)
    high = table.astype(BF16)
    low = (table - high.astype(np.float32)).astype(BF16)
    return np.concatenate([high, high, low], axis)


def _iota(shape, dim):
    return lax.broadcasted_iota(jnp.int32, shape, dim)


def _angle(product, modulus):
    return (product & (modulus - 1)).astype(F32) * (2.0 * math.pi / modulus)


def first_table(zh, n0):
    row = _iota((128, 256), 0)
    col = _iota((128, 256), 1)
    ky = 64 * (row // 4) + row % 4 + 4 * n0
    y = 32 * (col // 16) + col % 16 + 512 * zh
    parts = []
    for h in (0, 1):
        t = _angle(ky * (y + 16 * h), 2048)
        parts += [_left(jnp.cos(t)), _left(-jnp.sin(t))]
    return parts


def last_table(zh, n0):
    row = _iota((16, 64), 0)
    col = _iota((16, 64), 1)
    s = 4 * (col % 16) + col // 16
    out = []
    for a in (0, 1):
        t = _angle(s * (32 * row + n0 + 16 * a + 512 * zh), 2048)
        out.append(_left(jnp.concatenate([jnp.cos(t) * TOP_SCALE, jnp.sin(t) * TOP_SCALE], 0)))
    return out


def side_table(zh, n0):
    row = _iota((16, 64), 0)
    z = _iota((16, 64), 1)
    own = jnp.where(row < 8, zh, 1 - zh)
    t = _angle((64 * own + 4 * n0 + row % 4) * z, 128)
    return _left(jnp.where(row % 8 < 4, jnp.cos(t), -jnp.sin(t)))


def side_last_table(zh, yy):
    row = _iota((16, 64), 0)
    col = _iota((16, 64), 1)
    kz = 64 * zh + 4 * (col % 16) + col // 16
    t = _angle(kz * (row + 16 * yy), 128)
    return _left(jnp.concatenate([jnp.cos(t) * SIDE_SCALE, jnp.sin(t) * SIDE_SCALE], 0))


def first_stage(w, packed, roll):
    packed = _right(packed)
    p = [_mul(t, packed) for t in w]
    low = _iota((128, 128), 1) < 64
    return jnp.where(low, p[0] + roll(p[2], 64), roll(p[1], 64) + p[3])


def side_first(w, data, roll):
    t = _mul(w, _right(data))
    low = _iota((4, 128), 1) < 64
    own, other = [], []
    for x in range(4):
        for base, out in ((0, own), (8, other)):
            o = t[base : base + 8, 128 * x : 128 * x + 128]
            q = roll(o, 64)
            f0 = jnp.where(low, o[0:4], q[4:8])
            f1 = jnp.where(low, q[0:4], o[4:8])
            out.append(jnp.concatenate([f0, f1], 0))
    return own, other


def line_stage(rows, kernel_at, tabs, roll):
    gl, twist, fwd, inv, back = tabs
    twc, tws = twist[:64], twist[64:]
    p = _mul(_right(jnp.concatenate(rows, 1)), gl, 0, 0)
    mid = []
    for r in range(4):
        q = p[128 * r : 128 * r + 128]
        bre = q[:64, :128] + q[64:, 128:]
        bim = q[64:, :128] - q[:64, 128:]
        mid.append(jnp.concatenate([bre * twc + bim * tws, bim * twc - bre * tws], 0))
    spectrum = _mul(fwd, _right(jnp.concatenate(mid, 1)))
    weighted = []
    for c in range(2):
        for r in range(4):
            sre = spectrum[:16, 128 * r : 128 * r + 128]
            sim = spectrum[16:, 128 * r : 128 * r + 128]
            kre, kim = kernel_at(c, 0, r), kernel_at(c, 1, r)
            weighted.append(
                jnp.concatenate([kre * sre + kim * sim, kre * sim - kim * sre], 0)
            )
    v = _mul(inv, _right(jnp.concatenate(weighted, 1)))
    turned = []
    for cr in range(8):
        vre = v[:64, 128 * cr : 128 * cr + 128]
        vim = v[64:, 128 * cr : 128 * cr + 128]
        turned += [vre * twc - vim * tws, vim * twc + vre * tws]
    u = _mul(back, _right(jnp.concatenate(turned, 0), 1), 1, 1)
    return spread(u, 16, roll)


def spread(u, half, roll):
    sign = jnp.where(_iota((half, 128), 1) < 64, -1.0, 1.0)
    out = []
    for cr in range(8):
        lanes = slice(128 * cr, 128 * cr + 128)
        out.append(u[:half, lanes] + sign * roll(u[half:, lanes], 64))
    return out


def fold_stage(rows, fold, roll):
    return spread(_mul(fold, _right(jnp.concatenate(rows, 1))), 32, roll)


def last_stage(table, rows, roll):
    g = _mul(table, _right(jnp.concatenate(rows, 1)))
    low = _iota((16, 128), 1) < 64
    part = [g[:16, 128 * c : 128 * c + 128] - roll(g[16:, 128 * c : 128 * c + 128], 64) for c in (0, 1)]
    return jnp.where(low, part[0], roll(part[1], 64))


def rows8(start, size):
    return pl.ds(pl.multiple_of(start, 8), size)


def body(
    mag, stiff, rtop_in, rside_in, ktop, kside, c_turn, c_gl32, c_gl16, c_fwd, c_inv, c_back, c_fold,
    exch, top,
    field, rtop, rside, twist, gl32, gl16, fwd, inv, back, fold, kraw, kt, ks,
    send1, recv1, recv1s, send2, recv2, send3, recv3, send4, recv4, send5, recv5,
    hop1, line1, send6, recv6, hop2, other2,
    hx_out_hi, hx_out_lo, hx_lo, hx_hi, hy_out_hi, hy_out_lo, hy_lo, hy_hi, col_lo, col_hi,
    local, ssem, rsem, hsend, hrecv, near, cross,
):
    gx, gy, gz = lax.axis_index("gx"), lax.axis_index("gy"), lax.axis_index("gz")
    zh, xx = lax.div(gy, 4), lax.rem(gy, 4)
    n0 = 4 * xx + gz
    m0 = 2 * gx + zh
    z, core = 8 * zh + lax.div(gx, 2), lax.rem(gx, 2)
    device = 16 * m0 + n0

    def column_index(z_plus, which):
        at = lax.rem(z_plus, 16)
        return 4 * lax.rem(at, 8) + 2 * which + lax.div(at, 8)

    def plane_id(n):
        return 16 * m0 + n

    def column_id(m):
        return 16 * m + n0

    far = jnp.where(lax.rem(gx, 16) < 8, column_id(2 * (gx + 8) + 1 - zh), column_id(2 * (gx - 8) + 1 - zh))

    def roll(value, shift):
        return pltpu.roll(value, shift, 1)

    def over_plane(action):
        for dx, dy in PLANE_ORDER:
            x = lax.rem(xx + dx, 4)
            action(4 * x + lax.rem(gz + dy, 4), x)

    def over_column(action):
        for which in (0, 1):
            action(column_index(z + 8, which))

        def step(k, carry):
            for which in (0, 1):
                action(column_index(z + 8 - k, which))
                action(column_index(z + 8 + k, which))
            return carry

        lax.fori_loop(1, 8, step, 0)
        action(column_index(z, 1 - core))

    def signal(sem, target):
        pl.semaphore_signal(sem, inc=1, device_id=target, device_id_type=LOGICAL)

    def remote(src, dst, sems, target):
        send_sem, recv_sem = sems
        return pltpu.make_async_remote_copy(
            src_ref=src, dst_ref=dst, send_sem=send_sem, recv_sem=recv_sem,
            device_id=target, device_id_type=LOGICAL,
        )

    def wait_bytes(ref, sem):
        pltpu.make_async_copy(ref, ref, sem).wait()

    def pair(i):
        return ssem.at[i], rsem.at[i]

    residuals = [
        pltpu.make_async_copy(rtop_in, rtop, local.at[4]),
        pltpu.make_async_copy(rside_in, rside, local.at[5]),
    ]
    loads = [
        pltpu.make_async_copy(src, dst, local.at[6 + i])
        for i, (src, dst) in enumerate(
            [(c_turn, twist), (c_gl32, gl32), (c_gl16, gl16), (c_fwd, fwd), (c_inv, inv), (c_back, back), (c_fold, fold)]
        )
    ] + [
        pltpu.make_async_copy(mag, field.at[0:3, pl.ds(64, 1024)], local.at[0]),
        pltpu.make_async_copy(stiff, field.at[3:4, pl.ds(64, 1024)], local.at[1]),
        pltpu.make_async_copy(ktop, kraw.at[0], local.at[2]),
        pltpu.make_async_copy(kside, kraw.at[1], local.at[3]),
    ]
    for load in residuals + loads:
        load.start()
    barrier = pltpu.get_barrier_semaphore()
    over_plane(lambda n, x: signal(barrier, plane_id(n)))

    def greet(k, carry):
        for which in (0, 1):
            signal(barrier, column_id(column_index(z + k, which)))
            signal(barrier, column_id(column_index(z + 16 - k, which)))
        return carry

    lax.fori_loop(1, 5, greet, 0)
    signal(barrier, column_id(column_index(z, 1 - core)))

    for load in residuals:
        load.wait()
    send1[...] = jnp.concatenate([rtop[0:16, :], rtop[16:32, :]], 1)
    recv1[rows8(16 * n0, 16), :] = send1[...]
    recv1s[rows8(16 * n0, 16), :] = rside[...]

    pl.semaphore_wait(barrier, 32)

    over_plane(
        lambda n, x: remote(send1, recv1.at[rows8(16 * n0, 16)], pair(0), plane_id(n)).start()
    )

    signal(near, column_id(column_index(z + 4, core)))
    signal(near, column_id(column_index(z + 12, core)))

    for load in loads:
        load.wait()
    zero_face = jnp.zeros((64, 128), F32)
    for c in range(4):
        hx_out_hi[16 * c : 16 * c + 16, :] = field[c, pl.ds(64 + 63, 16, stride=64), :]
        hx_out_lo[16 * c : 16 * c + 16, :] = field[c, pl.ds(64, 16, stride=64), :]
    lane = _iota((64, 128), 1)

    def pack(z, carry):
        hi, lo = carry
        for c in range(4):
            at = 16 * c + z
            turned = pltpu.roll(field[c, rows8(64 + 64 * z, 64), :], at + 1, 1)
            hi = jnp.where(lane == at, turned, hi)
            lo = jnp.where(lane == at + 1, turned, lo)
        return hi, lo

    packed_hi, packed_lo = lax.fori_loop(0, 16, pack, (zero_face, zero_face))
    low = _iota((32, 128), 1) < 64
    hy_out_hi[...] = jnp.where(low, packed_hi[:32], roll(packed_hi[32:], 64))
    hy_out_lo[...] = jnp.where(low, roll(packed_lo[:32], 127), roll(packed_lo[32:], 63))

    x_up = (gx < 15, remote(hx_out_hi, hx_lo, (hsend.at[0], hrecv.at[0]), device + 32))
    x_dn = (gx > 0, remote(hx_out_lo, hx_hi, (hsend.at[1], hrecv.at[1]), device - 32))
    y_up = (gy < 7, remote(hy_out_hi, hy_lo, (hsend.at[2], hrecv.at[2]), device + 4))
    y_dn = (gy > 0, remote(hy_out_lo, hy_hi, (hsend.at[3], hrecv.at[3]), device - 4))
    z_up = (
        gz < 3,
        remote(field.at[:, pl.ds(1024, 64)], field.at[:, pl.ds(0, 64)],
               (hsend.at[4], hrecv.at[4]), device + 1),
    )
    z_dn = (
        gz > 0,
        remote(field.at[:, pl.ds(64, 64)], field.at[:, pl.ds(1088, 64)],
               (hsend.at[5], hrecv.at[5]), device - 1),
    )
    faces = (y_up, y_dn, z_up, z_dn, x_up, x_dn)
    for there, copy in faces[4:]:

        @pl.when(there)
        def _(copy=copy):
            copy.start()

    over_plane(
        lambda n, x: remote(rside, recv1s.at[rows8(16 * n0, 16)], pair(8), plane_id(n)).start()
    )

    pl.semaphore_wait(near, 2)
    for at in (0, 7):

        @pl.when(gy == at)
        def _(at=at):
            signal(cross, device + (12 if at == 0 else -12))

    for missing, ref in ((gx == 0, hx_lo), (gx == 15, hx_hi), (gy == 0, hy_lo), (gy == 7, hy_hi)):

        @pl.when(missing)
        def _(ref=ref):
            ref[...] = zero_face[: ref.shape[0]]

    for missing, start in ((gz == 0, 0), (gz == 3, 1088)):

        @pl.when(missing)
        def _(start=start):
            for c in range(4):
                field[c, pl.ds(start, 64), :] = zero_face

    for which, out in ((0, kt), (1, ks)):
        for cp in range(4):
            for j in range(16):
                out[pl.ds(64 * cp + j, 4, stride=16), :] = kraw[
                    which, cp // 2, cp % 2, :, 128 * j : 128 * j + 128
                ]

    table1 = first_table(zh, n0)
    table_side = side_table(zh, n0)
    table_last = last_table(zh, n0)
    table_side_last = side_last_table(zh, gz)

    wait_bytes(recv1.at[pl.ds(0, 240)], rsem.at[0])
    first = first_stage(table1, recv1[...], roll)
    for m in range(32):
        send2[m] = first[4 * m : 4 * m + 4]
    recv2[m0] = send2[m0]
    over_column(lambda m: remote(send2.at[m], recv2.at[m0], pair(1), column_id(m)).start())

    inside = (
        (jnp.logical_and(gy < 7, gy != 3), y_up[1]),
        (jnp.logical_and(gy > 0, gy != 4), y_dn[1]),
    ) + faces[2:4]
    for there, copy in inside:

        @pl.when(there)
        def _(copy=copy):
            copy.start()

    wait_bytes(recv1s.at[pl.ds(0, 240)], rsem.at[8])
    data = jnp.concatenate([recv1s[64 * x : 64 * x + 64, :] for x in range(4)], 1)
    own, other = side_first(table_side, data, roll)
    for x in range(4):
        line1[rows8(32 * zh + 8 * x, 8), :] = own[x]
        hop1[8 * x : 8 * x + 8, :] = other[x]
    remote(hop1, line1.at[rows8(32 * zh, 32)], pair(5), far).start()

    for at, copy in ((3, y_up[1]), (4, y_dn[1])):

        @pl.when(gy == at)
        def _(copy=copy):
            pl.semaphore_wait(cross, 1)
            copy.start()

    wait_bytes(recv2.at[pl.ds(0, 31)], rsem.at[1])
    shared = (twist[...], fwd[...], inv[...], back[...])
    lines = line_stage(
        [recv2[:, r, :] for r in range(4)],
        lambda c, p, r: kt[64 * (2 * c + p) + 16 * r : 64 * (2 * c + p) + 16 * r + 16, :],
        (gl32[...],) + shared,
        roll,
    )
    for cr in range(8):
        send3[pl.ds(cr, 16, stride=8), :] = lines[cr]
    recv3[rows8(8 * m0, 8), :] = send3[rows8(8 * gx, 8), :]
    over_column(
        lambda m: remote(
            send3.at[rows8(8 * lax.div(m, 2), 8)], recv3.at[rows8(8 * m0, 8)], pair(2), column_id(m)
        ).start()
    )

    wait_bytes(line1.at[pl.ds(0, 32)], rsem.at[5])
    lines = line_stage(
        [line1[pl.ds(r, 16, stride=4), :] for r in range(4)],
        lambda c, p, r: ks[64 * (2 * c + p) + 16 * r : 64 * (2 * c + p) + 16 * r + 16, :],
        (gl16[...],) + shared,
        roll,
    )
    for cr in range(8):
        for h in range(2):
            send6[h, pl.ds(cr, 8, stride=8), :] = lines[cr][8 * h : 8 * h + 8]
    recv6[:, rows8(16 * n0, 16), :] = send6[:, rows8(16 * xx, 16), :]
    over_plane(
        lambda n, x: remote(
            send6.at[:, rows8(16 * x, 16)], recv6.at[:, rows8(16 * n0, 16)], pair(6), plane_id(n)
        ).start()
    )

    wait_bytes(recv3.at[pl.ds(0, 248)], rsem.at[2])
    folded = fold_stage([recv3[pl.ds(cr, 32, stride=8), :] for cr in range(8)], fold[...], roll)
    for cr in range(8):
        send4[pl.ds(cr, 16, stride=16), :] = folded[cr][:16]
        send4[pl.ds(8 + cr, 16, stride=16), :] = folded[cr][16:]
    recv4[rows8(16 * n0, 16), :] = send4[rows8(16 * n0, 16), :]
    over_plane(
        lambda n, x: remote(
            send4.at[rows8(16 * n, 16)], recv4.at[rows8(16 * n0, 16)], pair(3), plane_id(n)
        ).start()
    )

    wait_bytes(recv6.at[:, pl.ds(0, 240)], rsem.at[6])
    columns = [
        jnp.concatenate([recv6[h, pl.ds(8 * e + 4 * c + r, 16, stride=16), :] for r in range(4)], 0)
        for h in (zh, 1 - zh)
        for c in range(2)
        for e in range(2)
    ]
    g = _mul(table_side_last, _right(jnp.concatenate(columns, 1)))
    low = _iota((16, 128), 1) < 64
    halves = [
        g[:16, 128 * q : 128 * q + 128] - roll(g[16:, 128 * q : 128 * q + 128], 64) for q in range(8)
    ]
    sums = [jnp.where(low, halves[q], roll(halves[q + 1], 64)) for q in (0, 2, 4, 6)]
    hop2[0:16, :], hop2[16:32, :] = sums[2], sums[3]
    remote(hop2, other2, pair(7), far).start()

    arrivals = (
        (gx > 0, hx_lo, 0), (gx < 15, hx_hi, 1), (gy > 0, hy_lo, 2), (gy < 7, hy_hi, 3),
        (gz > 0, field.at[:, pl.ds(0, 64)], 4), (gz < 3, field.at[:, pl.ds(1088, 64)], 5),
    )
    for there, ref, i in arrivals:

        @pl.when(there)
        def _(ref=ref, i=i):
            wait_bytes(ref, hrecv.at[i])

    for ref, out in ((hy_lo, col_lo), (hy_hi, col_hi)):
        out[0:32, :] = ref[...]
        out[32:64, :] = roll(ref[...], 64)
    sub = _iota((64, 128), 0)

    def exchange(z, carry):
        def slab(c, step):
            return field[c, rows8(64 + 64 * (z + step), 64), :]

        def around(c):
            at = 16 * c + z
            center = slab(c, 0)
            below = jnp.where(sub == 0, hx_lo[pl.ds(at, 1), :], pltpu.roll(center, 1, 0))
            above = jnp.where(sub == 63, hx_hi[pl.ds(at, 1), :], pltpu.roll(center, 63, 0))
            left = jnp.where(lane == 0, pltpu.roll(col_lo[...], 128 - at, 1), pltpu.roll(center, 1, 1))
            right = jnp.where(
                lane == 127, pltpu.roll(col_hi[...], 127 - at, 1), pltpu.roll(center, 127, 1)
            )
            return center, (slab(c, -1), slab(c, 1), below, above, left, right)

        a, near = around(3)
        weights = [4.0 * a * b / (a + b) for b in near]
        for c in range(3):
            m, beside = around(c)
            total = weights[0] * (m - beside[0])
            for w, b in zip(weights[1:], beside[1:]):
                total = total + w * (m - b)
            exch[c, rows8(64 * z, 64), :] = total
        return carry

    lax.fori_loop(0, 16, exchange, 0)

    wait_bytes(recv4.at[pl.ds(0, 240)], rsem.at[3])
    for a in range(2):
        rows = [
            jnp.concatenate(
                [recv4[pl.ds(8 * a + 4 * c + r, 16, stride=16), :] for r in range(4)], 0
            )
            for c in range(2)
        ]
        send5[pl.ds(a, 16, stride=2), :] = last_stage(table_last[a], rows, roll)
    recv5[rows8(8 * n0, 8), :] = send5[rows8(8 * xx, 8), :]
    over_plane(
        lambda n, x: remote(
            send5.at[rows8(8 * x, 8)], recv5.at[rows8(8 * n0, 8)], pair(4), plane_id(n)
        ).start()
    )

    wait_bytes(other2, rsem.at[7])
    for c in range(2):
        side = sums[c] + other2[16 * c : 16 * c + 16, :]
        for at in range(16):
            rows = slice(64 * at, 64 * at + 64)
            exch[c + 1, rows, :] = exch[c + 1, rows, :] + side[at : at + 1, :]

    wait_bytes(recv1.at[pl.ds(0, 240)], ssem.at[0])
    wait_bytes(recv1s.at[pl.ds(0, 240)], ssem.at[8])
    wait_bytes(send2.at[pl.ds(0, 31)], ssem.at[1])
    wait_bytes(recv3.at[pl.ds(0, 248)], ssem.at[2])
    wait_bytes(recv4.at[pl.ds(0, 240)], ssem.at[3])
    wait_bytes(hop1, ssem.at[5])
    wait_bytes(recv6.at[:, pl.ds(0, 240)], ssem.at[6])
    wait_bytes(hop2, ssem.at[7])
    for there, copy in faces:

        @pl.when(there)
        def _(copy=copy):
            copy.wait_send()

    wait_bytes(recv5.at[pl.ds(0, 120)], rsem.at[4])
    lines_y = jnp.concatenate([recv5[pl.ds(q, 16, stride=8), :] for q in range(8)], 0)
    top[...] = lines_y.T
    wait_bytes(recv5.at[pl.ds(0, 120)], ssem.at[4])


CHUNKS = 8


def add_top(exch, top, out, total, sems):
    size = 2048 // CHUNKS
    copies = [pltpu.make_async_copy(exch.at[2], out.at[2], sems.at[CHUNKS])]
    copies[0].start()
    for k in range(CHUNKS):
        c, start = divmod(k * size, 1024)
        image = top[64 * c : 64 * c + 64, :]
        for at in range(start, start + size, 64):
            total[c, at : at + 64, :] = exch[c, at : at + 64, :] + image
        rows = pl.ds(start, size)
        copies.append(pltpu.make_async_copy(total.at[c, rows], out.at[c, rows], sems.at[k]))
        copies[-1].start()
    for copy in copies:
        copy.wait()


def on_device(magnetization, stiffness, residual_top, residual_side, top_kernel, side_kernel):
    tables = [jnp.asarray(t) for t in const_tables()]
    vmem = pl.BlockSpec(memory_space=pltpu.VMEM)
    hbm = pl.BlockSpec(memory_space=pltpu.HBM)

    def pin(array):
        return pltpu.with_memory_space_constraint(array, pltpu.HBM)

    def buf(*shape):
        return pltpu.VMEM(shape, F32)

    scratch = [
        buf(4, 1152, 128), buf(32, 64), buf(16, 128), *[pltpu.VMEM(t.shape, t.dtype) for t in tables], buf(2, 2, 2, 4, 2048), buf(256, 128), buf(256, 128),
        buf(16, 128), buf(256, 128), buf(256, 128), buf(32, 4, 128), buf(32, 4, 128),
        buf(128, 128), buf(256, 128), buf(256, 128), buf(256, 128), buf(32, 128), buf(128, 128),
        buf(32, 128), buf(64, 128), buf(2, 64, 128), buf(2, 256, 128), buf(32, 128), buf(32, 128),
        buf(64, 128), buf(64, 128), buf(64, 128), buf(64, 128),
        buf(32, 128), buf(32, 128), buf(32, 128), buf(32, 128), buf(64, 128), buf(64, 128),
        pltpu.SemaphoreType.DMA((13,)), pltpu.SemaphoreType.DMA((9,)), pltpu.SemaphoreType.DMA((9,)),
        pltpu.SemaphoreType.DMA((6,)), pltpu.SemaphoreType.DMA((6,)),
        pltpu.SemaphoreType.REGULAR, pltpu.SemaphoreType.REGULAR,
    ]
    exch, top = pl.pallas_call(
        body,
        out_shape=[
            jax.ShapeDtypeStruct((3, 1024, 128), F32),
            jax.ShapeDtypeStruct((128, 128), F32),
        ],
        in_specs=[hbm] * (6 + len(tables)),
        out_specs=[vmem] * 2,
        scratch_shapes=scratch,
        compiler_params=pltpu.CompilerParams(
            collective_id=0, has_side_effects=True, vmem_limit_bytes=40 * 1024 * 1024
        ),
        name="adjoint",
    )(
        pin(magnetization.reshape(3, 1024, 128)),
        pin(stiffness.reshape(1, 1024, 128)),
        pin(residual_top.T),
        pin(residual_side.T),
        pin(top_kernel),
        pin(side_kernel),
        *[pin(t) for t in tables],
    )
    out = pl.pallas_call(
        add_top,
        out_shape=jax.ShapeDtypeStruct((3, 1024, 128), F32),
        in_specs=[vmem, vmem],
        out_specs=hbm,
        scratch_shapes=[buf(2, 1024, 128), pltpu.SemaphoreType.DMA((CHUNKS + 1,))],
        compiler_params=pltpu.CompilerParams(vmem_limit_bytes=4 * 1024 * 1024),
        name="add_top",
    )(exch, top)
    return out.reshape(3, 16, 64, 128)


def solution(mesh):
    placed = (
        P(None, "gz", "gx", "gy"),
        P("gz", "gx", "gy"),
        P("gx", ("gy", "gz")),
        P("gy", "gz"),
        P(None, None, ("gx", "gy", "gz"), None),
        P(None, None, ("gy", "gz"), None),
    )
    return jax.shard_map(
        on_device, mesh=mesh, in_specs=placed, out_specs=P(None, "gz", "gx", "gy"), check_vma=False
    )
```

```python
import math

import jax
import jax.numpy as jnp
import numpy as np
from jax import lax
from jax.experimental import pallas as pl
from jax.experimental.pallas import tpu as pltpu
from jax.sharding import PartitionSpec as P

F32 = jnp.float32
LOGICAL = pl.DeviceIdType.LOGICAL
PLANE_ORDER = sorted(
    [(dx, dy) for dx in range(4) for dy in range(4) if dx or dy],
    key=lambda d: -(min(d[0], 4 - d[0]) + min(d[1], 4 - d[1])),
)
TOP_SCALE = 1.0 / 2048.0**2
SIDE_SCALE = 1.0 / (2048.0 * 128.0)


BF16 = jnp.bfloat16


def _split(x):
    high = x.astype(BF16)
    return high, (x - high.astype(F32)).astype(BF16)


def _left(table, axis=1):
    high, low = _split(table)
    return jnp.concatenate([high, high, low], axis)


def _right(value, axis=0):
    high, low = _split(value)
    return jnp.concatenate([high, low, high], axis)


def _mul(a, b, ca=1, cb=0):
    return lax.dot_general(a, b, (((ca,), (cb,)), ((), ())), preferred_element_type=F32)


def _cs(first, second, modulus):
    angle = 2.0 * np.pi * ((first * second) % modulus) / modulus
    return np.cos(angle), np.sin(angle)


def const_tables():
    i = np.arange
    c, s = _cs(i(16)[:, None], i(128)[None, :], 32)
    gl16 = np.concatenate([c, s], 1)
    gl32 = np.repeat(gl16, 2, axis=0)
    c, s = _cs(i(64)[:, None], i(128)[None, :], 2048)
    twist = np.concatenate([c, s], 0)
    c, s = _cs(i(16)[:, None], i(64)[None, :], 16)
    fwd = np.block([[c, s], [-s, c]])
    inv = np.block([[c.T, -s.T], [s.T, c.T]])
    back = gl16.reshape(16, 2, 128).transpose(1, 0, 2).reshape(32, 128)
    c, s = _cs(i(32)[:, None], i(32)[None, :], 32)
    fold = np.concatenate([c, s], 0)
    turn = twist.astype(np.float32)
    split = [split3(gl32, 0), split3(gl16, 0), split3(fwd, 1), split3(inv, 1), split3(back, 1), split3(fold, 1)]
    return [turn] + split


def split3(table, axis):
    table = table.astype(np.float32)
    high = table.astype(BF16)
    low = (table - high.astype(np.float32)).astype(BF16)
    return np.concatenate([high, high, low], axis)


def _iota(shape, dim):
    return lax.broadcasted_iota(jnp.int32, shape, dim)


def _angle(product, modulus):
    return (product & (modulus - 1)).astype(F32) * (2.0 * math.pi / modulus)


def first_table(zh, n0):
    row = _iota((128, 256), 0)
    col = _iota((128, 256), 1)
    ky = 64 * (row // 4) + row % 4 + 4 * n0
    y = 32 * (col // 16) + col % 16 + 512 * zh
    parts = []
    for h in (0, 1):
        t = _angle(ky * (y + 16 * h), 2048)
        parts += [_left(jnp.cos(t)), _left(-jnp.sin(t))]
    return parts


def last_table(zh, n0):
    row = _iota((16, 64), 0)
    col = _iota((16, 64), 1)
    s = 4 * (col % 16) + col // 16
    out = []
    for a in (0, 1):
        t = _angle(s * (32 * row + n0 + 16 * a + 512 * zh), 2048)
        out.append(_left(jnp.concatenate([jnp.cos(t) * TOP_SCALE, jnp.sin(t) * TOP_SCALE], 0)))
    return out


def side_table(zh, n0):
    row = _iota((16, 64), 0)
    z = _iota((16, 64), 1)
    own = jnp.where(row < 8, zh, 1 - zh)
    t = _angle((64 * own + 4 * n0 + row % 4) * z, 128)
    return _left(jnp.where(row % 8 < 4, jnp.cos(t), -jnp.sin(t)))


def side_last_table(zh, yy):
    row = _iota((16, 64), 0)
    col = _iota((16, 64), 1)
    kz = 64 * zh + 4 * (col % 16) + col // 16
    t = _angle(kz * (row + 16 * yy), 128)
    return _left(jnp.concatenate([jnp.cos(t) * SIDE_SCALE, jnp.sin(t) * SIDE_SCALE], 0))


def first_stage(w, packed, roll):
    packed = _right(packed)
    p = [_mul(t, packed) for t in w]
    low = _iota((128, 128), 1) < 64
    return jnp.where(low, p[0] + roll(p[2], 64), roll(p[1], 64) + p[3])


def side_first(w, data, roll):
    t = _mul(w, _right(data))
    low = _iota((4, 128), 1) < 64
    own, other = [], []
    for x in range(4):
        for base, out in ((0, own), (8, other)):
            o = t[base : base + 8, 128 * x : 128 * x + 128]
            q = roll(o, 64)
            f0 = jnp.where(low, o[0:4], q[4:8])
            f1 = jnp.where(low, q[0:4], o[4:8])
            out.append(jnp.concatenate([f0, f1], 0))
    return own, other


def line_stage(rows, kernel_at, tabs, roll):
    gl, twist, fwd, inv, back = tabs
    twc, tws = twist[:64], twist[64:]
    p = _mul(_right(jnp.concatenate(rows, 1)), gl, 0, 0)
    mid = []
    for r in range(4):
        q = p[128 * r : 128 * r + 128]
        bre = q[:64, :128] + q[64:, 128:]
        bim = q[64:, :128] - q[:64, 128:]
        mid.append(jnp.concatenate([bre * twc + bim * tws, bim * twc - bre * tws], 0))
    spectrum = _mul(fwd, _right(jnp.concatenate(mid, 1)))
    weighted = []
    for c in range(2):
        for r in range(4):
            sre = spectrum[:16, 128 * r : 128 * r + 128]
            sim = spectrum[16:, 128 * r : 128 * r + 128]
            kre, kim = kernel_at(c, 0, r), kernel_at(c, 1, r)
            weighted.append(
                jnp.concatenate([kre * sre + kim * sim, kre * sim - kim * sre], 0)
            )
    v = _mul(inv, _right(jnp.concatenate(weighted, 1)))
    turned = []
    for cr in range(8):
        vre = v[:64, 128 * cr : 128 * cr + 128]
        vim = v[64:, 128 * cr : 128 * cr + 128]
        turned += [vre * twc - vim * tws, vim * twc + vre * tws]
    u = _mul(back, _right(jnp.concatenate(turned, 0), 1), 1, 1)
    return spread(u, 16, roll)


def spread(u, half, roll):
    sign = jnp.where(_iota((half, 128), 1) < 64, -1.0, 1.0)
    out = []
    for cr in range(8):
        lanes = slice(128 * cr, 128 * cr + 128)
        out.append(u[:half, lanes] + sign * roll(u[half:, lanes], 64))
    return out


def fold_stage(rows, fold, roll):
    return spread(_mul(fold, _right(jnp.concatenate(rows, 1))), 32, roll)


def last_stage(table, rows, roll):
    g = _mul(table, _right(jnp.concatenate(rows, 1)))
    low = _iota((16, 128), 1) < 64
    part = [g[:16, 128 * c : 128 * c + 128] - roll(g[16:, 128 * c : 128 * c + 128], 64) for c in (0, 1)]
    return jnp.where(low, part[0], roll(part[1], 64))


def rows8(start, size):
    return pl.ds(pl.multiple_of(start, 8), size)


def body(
    mag, stiff, rtop_in, rside_in, ktop, kside, c_turn, c_gl32, c_gl16, c_fwd, c_inv, c_back, c_fold,
    exch, top,
    field, rtop, rside, twist, gl32, gl16, fwd, inv, back, fold, kraw, kt, ks,
    send1, recv1, recv1s, send2, recv2, send3, recv3, send4, recv4, send5, recv5,
    hop1, line1, send6, recv6, hop2, other2,
    hx_out_hi, hx_out_lo, hx_lo, hx_hi, hy_out_hi, hy_out_lo, hy_lo, hy_hi, col_lo, col_hi,
    local, ssem, rsem, hsend, hrecv, near, cross,
):
    gx, gy, gz = lax.axis_index("gx"), lax.axis_index("gy"), lax.axis_index("gz")
    zh, xx = lax.div(gy, 4), lax.rem(gy, 4)
    n0 = 4 * xx + gz
    m0 = 2 * gx + zh
    z, core = 8 * zh + lax.div(gx, 2), lax.rem(gx, 2)
    device = 16 * m0 + n0

    def column_index(z_plus, which):
        at = lax.rem(z_plus, 16)
        return 4 * lax.rem(at, 8) + 2 * which + lax.div(at, 8)

    def plane_id(n):
        return 16 * m0 + n

    def column_id(m):
        return 16 * m + n0

    far = jnp.where(lax.rem(gx, 16) < 8, column_id(2 * (gx + 8) + 1 - zh), column_id(2 * (gx - 8) + 1 - zh))

    def roll(value, shift):
        return pltpu.roll(value, shift, 1)

    def over_plane(action):
        for dx, dy in PLANE_ORDER:
            x = lax.rem(xx + dx, 4)
            action(4 * x + lax.rem(gz + dy, 4), x)

    def over_column(action):
        for which in (0, 1):
            action(column_index(z + 8, which))

        def step(k, carry):
            for which in (0, 1):
                action(column_index(z + 8 - k, which))
                action(column_index(z + 8 + k, which))
            return carry

        lax.fori_loop(1, 8, step, 0)
        action(column_index(z, 1 - core))

    def signal(sem, target):
        pl.semaphore_signal(sem, inc=1, device_id=target, device_id_type=LOGICAL)

    def remote(src, dst, sems, target):
        send_sem, recv_sem = sems
        return pltpu.make_async_remote_copy(
            src_ref=src, dst_ref=dst, send_sem=send_sem, recv_sem=recv_sem,
            device_id=target, device_id_type=LOGICAL,
        )

    def wait_bytes(ref, sem):
        pltpu.make_async_copy(ref, ref, sem).wait()

    def pair(i):
        return ssem.at[i], rsem.at[i]

    residuals = [
        pltpu.make_async_copy(rtop_in, rtop, local.at[4]),
        pltpu.make_async_copy(rside_in, rside, local.at[5]),
    ]
    loads = [
        pltpu.make_async_copy(src, dst, local.at[6 + i])
        for i, (src, dst) in enumerate(
            [(c_turn, twist), (c_gl32, gl32), (c_gl16, gl16), (c_fwd, fwd), (c_inv, inv), (c_back, back), (c_fold, fold)]
        )
    ] + [
        pltpu.make_async_copy(mag, field.at[0:3, pl.ds(64, 1024)], local.at[0]),
        pltpu.make_async_copy(stiff, field.at[3:4, pl.ds(64, 1024)], local.at[1]),
        pltpu.make_async_copy(ktop, kraw.at[0], local.at[2]),
        pltpu.make_async_copy(kside, kraw.at[1], local.at[3]),
    ]
    for load in residuals + loads:
        load.start()
    barrier = pltpu.get_barrier_semaphore()
    over_plane(lambda n, x: signal(barrier, plane_id(n)))

    def greet(k, carry):
        for which in (0, 1):
            signal(barrier, column_id(column_index(z + k, which)))
            signal(barrier, column_id(column_index(z + 16 - k, which)))
        return carry

    lax.fori_loop(1, 5, greet, 0)
    signal(barrier, column_id(column_index(z, 1 - core)))

    for load in residuals:
        load.wait()
    send1[...] = jnp.concatenate([rtop[0:16, :], rtop[16:32, :]], 1)
    recv1[rows8(16 * n0, 16), :] = send1[...]
    recv1s[rows8(16 * n0, 16), :] = rside[...]

    pl.semaphore_wait(barrier, 32)

    over_plane(
        lambda n, x: remote(send1, recv1.at[rows8(16 * n0, 16)], pair(0), plane_id(n)).start()
    )

    signal(near, column_id(column_index(z + 4, core)))
    signal(near, column_id(column_index(z + 12, core)))

    for load in loads:
        load.wait()
    zero_face = jnp.zeros((64, 128), F32)
    for c in range(4):
        hx_out_hi[16 * c : 16 * c + 16, :] = field[c, pl.ds(64 + 63, 16, stride=64), :]
        hx_out_lo[16 * c : 16 * c + 16, :] = field[c, pl.ds(64, 16, stride=64), :]
    lane = _iota((64, 128), 1)

    def pack(z, carry):
        hi, lo = carry
        for c in range(4):
            at = 16 * c + z
            turned = pltpu.roll(field[c, rows8(64 + 64 * z, 64), :], at + 1, 1)
            hi = jnp.where(lane == at, turned, hi)
            lo = jnp.where(lane == at + 1, turned, lo)
        return hi, lo

    packed_hi, packed_lo = lax.fori_loop(0, 16, pack, (zero_face, zero_face))
    low = _iota((32, 128), 1) < 64
    hy_out_hi[...] = jnp.where(low, packed_hi[:32], roll(packed_hi[32:], 64))
    hy_out_lo[...] = jnp.where(low, roll(packed_lo[:32], 127), roll(packed_lo[32:], 63))

    x_up = (gx < 15, remote(hx_out_hi, hx_lo, (hsend.at[0], hrecv.at[0]), device + 32))
    x_dn = (gx > 0, remote(hx_out_lo, hx_hi, (hsend.at[1], hrecv.at[1]), device - 32))
    y_up = (gy < 7, remote(hy_out_hi, hy_lo, (hsend.at[2], hrecv.at[2]), device + 4))
    y_dn = (gy > 0, remote(hy_out_lo, hy_hi, (hsend.at[3], hrecv.at[3]), device - 4))
    z_up = (
        gz < 3,
        remote(field.at[:, pl.ds(1024, 64)], field.at[:, pl.ds(0, 64)],
               (hsend.at[4], hrecv.at[4]), device + 1),
    )
    z_dn = (
        gz > 0,
        remote(field.at[:, pl.ds(64, 64)], field.at[:, pl.ds(1088, 64)],
               (hsend.at[5], hrecv.at[5]), device - 1),
    )
    faces = (y_up, y_dn, z_up, z_dn, x_up, x_dn)
    for there, copy in faces[4:]:

        @pl.when(there)
        def _(copy=copy):
            copy.start()

    over_plane(
        lambda n, x: remote(rside, recv1s.at[rows8(16 * n0, 16)], pair(8), plane_id(n)).start()
    )

    pl.semaphore_wait(near, 2)
    for at in (0, 7):

        @pl.when(gy == at)
        def _(at=at):
            signal(cross, device + (12 if at == 0 else -12))

    for missing, ref in ((gx == 0, hx_lo), (gx == 15, hx_hi), (gy == 0, hy_lo), (gy == 7, hy_hi)):

        @pl.when(missing)
        def _(ref=ref):
            ref[...] = zero_face[: ref.shape[0]]

    for missing, start in ((gz == 0, 0), (gz == 3, 1088)):

        @pl.when(missing)
        def _(start=start):
            for c in range(4):
                field[c, pl.ds(start, 64), :] = zero_face

    for which, out in ((0, kt), (1, ks)):
        for cp in range(4):
            for j in range(16):
                out[pl.ds(64 * cp + j, 4, stride=16), :] = kraw[
                    which, cp // 2, cp % 2, :, 128 * j : 128 * j + 128
                ]

    table1 = first_table(zh, n0)
    table_side = side_table(zh, n0)
    table_last = last_table(zh, n0)
    table_side_last = side_last_table(zh, gz)

    wait_bytes(recv1.at[pl.ds(0, 240)], rsem.at[0])
    first = first_stage(table1, recv1[...], roll)
    for m in range(32):
        send2[m] = first[4 * m : 4 * m + 4]
    recv2[m0] = send2[m0]
    over_column(lambda m: remote(send2.at[m], recv2.at[m0], pair(1), column_id(m)).start())

    inside = (
        (jnp.logical_and(gy < 7, gy != 3), y_up[1]),
        (jnp.logical_and(gy > 0, gy != 4), y_dn[1]),
    ) + faces[2:4]
    for there, copy in inside:

        @pl.when(there)
        def _(copy=copy):
            copy.start()

    wait_bytes(recv1s.at[pl.ds(0, 240)], rsem.at[8])
    data = jnp.concatenate([recv1s[64 * x : 64 * x + 64, :] for x in range(4)], 1)
    own, other = side_first(table_side, data, roll)
    for x in range(4):
        line1[rows8(32 * zh + 8 * x, 8), :] = own[x]
        hop1[8 * x : 8 * x + 8, :] = other[x]
    remote(hop1, line1.at[rows8(32 * zh, 32)], pair(5), far).start()

    for at, copy in ((3, y_up[1]), (4, y_dn[1])):

        @pl.when(gy == at)
        def _(copy=copy):
            pl.semaphore_wait(cross, 1)
            copy.start()

    wait_bytes(recv2.at[pl.ds(0, 31)], rsem.at[1])
    shared = (twist[...], fwd[...], inv[...], back[...])
    lines = line_stage(
        [recv2[:, r, :] for r in range(4)],
        lambda c, p, r: kt[64 * (2 * c + p) + 16 * r : 64 * (2 * c + p) + 16 * r + 16, :],
        (gl32[...],) + shared,
        roll,
    )
    for cr in range(8):
        send3[pl.ds(cr, 16, stride=8), :] = lines[cr]
    recv3[rows8(8 * m0, 8), :] = send3[rows8(8 * gx, 8), :]
    over_column(
        lambda m: remote(
            send3.at[rows8(8 * lax.div(m, 2), 8)], recv3.at[rows8(8 * m0, 8)], pair(2), column_id(m)
        ).start()
    )

    wait_bytes(line1.at[pl.ds(0, 32)], rsem.at[5])
    lines = line_stage(
        [line1[pl.ds(r, 16, stride=4), :] for r in range(4)],
        lambda c, p, r: ks[64 * (2 * c + p) + 16 * r : 64 * (2 * c + p) + 16 * r + 16, :],
        (gl16[...],) + shared,
        roll,
    )
    for cr in range(8):
        for h in range(2):
            send6[h, pl.ds(cr, 8, stride=8), :] = lines[cr][8 * h : 8 * h + 8]
    recv6[:, rows8(16 * n0, 16), :] = send6[:, rows8(16 * xx, 16), :]
    over_plane(
        lambda n, x: remote(
            send6.at[:, rows8(16 * x, 16)], recv6.at[:, rows8(16 * n0, 16)], pair(6), plane_id(n)
        ).start()
    )

    wait_bytes(recv3.at[pl.ds(0, 248)], rsem.at[2])
    folded = fold_stage([recv3[pl.ds(cr, 32, stride=8), :] for cr in range(8)], fold[...], roll)
    for cr in range(8):
        send4[pl.ds(cr, 16, stride=16), :] = folded[cr][:16]
        send4[pl.ds(8 + cr, 16, stride=16), :] = folded[cr][16:]
    recv4[rows8(16 * n0, 16), :] = send4[rows8(16 * n0, 16), :]
    over_plane(
        lambda n, x: remote(
            send4.at[rows8(16 * n, 16)], recv4.at[rows8(16 * n0, 16)], pair(3), plane_id(n)
        ).start()
    )

    wait_bytes(recv6.at[:, pl.ds(0, 240)], rsem.at[6])
    columns = [
        jnp.concatenate([recv6[h, pl.ds(8 * e + 4 * c + r, 16, stride=16), :] for r in range(4)], 0)
        for h in (zh, 1 - zh)
        for c in range(2)
        for e in range(2)
    ]
    g = _mul(table_side_last, _right(jnp.concatenate(columns, 1)))
    low = _iota((16, 128), 1) < 64
    halves = [
        g[:16, 128 * q : 128 * q + 128] - roll(g[16:, 128 * q : 128 * q + 128], 64) for q in range(8)
    ]
    sums = [jnp.where(low, halves[q], roll(halves[q + 1], 64)) for q in (0, 2, 4, 6)]
    hop2[0:16, :], hop2[16:32, :] = sums[2], sums[3]
    remote(hop2, other2, pair(7), far).start()

    arrivals = (
        (gx > 0, hx_lo, 0), (gx < 15, hx_hi, 1), (gy > 0, hy_lo, 2), (gy < 7, hy_hi, 3),
        (gz > 0, field.at[:, pl.ds(0, 64)], 4), (gz < 3, field.at[:, pl.ds(1088, 64)], 5),
    )
    for there, ref, i in arrivals:

        @pl.when(there)
        def _(ref=ref, i=i):
            wait_bytes(ref, hrecv.at[i])

    for ref, out in ((hy_lo, col_lo), (hy_hi, col_hi)):
        out[0:32, :] = ref[...]
        out[32:64, :] = roll(ref[...], 64)
    sub = _iota((64, 128), 0)

    def exchange(z, carry):
        def slab(c, step):
            return field[c, rows8(64 + 64 * (z + step), 64), :]

        def around(c):
            at = 16 * c + z
            center = slab(c, 0)
            below = jnp.where(sub == 0, hx_lo[pl.ds(at, 1), :], pltpu.roll(center, 1, 0))
            above = jnp.where(sub == 63, hx_hi[pl.ds(at, 1), :], pltpu.roll(center, 63, 0))
            left = jnp.where(lane == 0, pltpu.roll(col_lo[...], 128 - at, 1), pltpu.roll(center, 1, 1))
            right = jnp.where(
                lane == 127, pltpu.roll(col_hi[...], 127 - at, 1), pltpu.roll(center, 127, 1)
            )
            return center, (slab(c, -1), slab(c, 1), below, above, left, right)

        a, near = around(3)
        weights = [4.0 * a * b / (a + b) for b in near]
        for c in range(3):
            m, beside = around(c)
            total = weights[0] * (m - beside[0])
            for w, b in zip(weights[1:], beside[1:]):
                total = total + w * (m - b)
            exch[c, rows8(64 * z, 64), :] = total
        return carry

    lax.fori_loop(0, 16, exchange, 0)

    wait_bytes(recv4.at[pl.ds(0, 240)], rsem.at[3])
    for a in range(2):
        rows = [
            jnp.concatenate(
                [recv4[pl.ds(8 * a + 4 * c + r, 16, stride=16), :] for r in range(4)], 0
            )
            for c in range(2)
        ]
        send5[pl.ds(a, 16, stride=2), :] = last_stage(table_last[a], rows, roll)
    recv5[rows8(8 * n0, 8), :] = send5[rows8(8 * xx, 8), :]
    over_plane(
        lambda n, x: remote(
            send5.at[rows8(8 * x, 8)], recv5.at[rows8(8 * n0, 8)], pair(4), plane_id(n)
        ).start()
    )

    wait_bytes(other2, rsem.at[7])
    for c in range(2):
        side = sums[c] + other2[16 * c : 16 * c + 16, :]
        for at in range(16):
            rows = slice(64 * at, 64 * at + 64)
            exch[c + 1, rows, :] = exch[c + 1, rows, :] + side[at : at + 1, :]

    wait_bytes(recv1.at[pl.ds(0, 240)], ssem.at[0])
    wait_bytes(recv1s.at[pl.ds(0, 240)], ssem.at[8])
    wait_bytes(send2.at[pl.ds(0, 31)], ssem.at[1])
    wait_bytes(recv3.at[pl.ds(0, 248)], ssem.at[2])
    wait_bytes(recv4.at[pl.ds(0, 240)], ssem.at[3])
    wait_bytes(hop1, ssem.at[5])
    wait_bytes(recv6.at[:, pl.ds(0, 240)], ssem.at[6])
    wait_bytes(hop2, ssem.at[7])
    for there, copy in faces:

        @pl.when(there)
        def _(copy=copy):
            copy.wait_send()

    wait_bytes(recv5.at[pl.ds(0, 120)], rsem.at[4])
    lines_y = jnp.concatenate([recv5[pl.ds(q, 16, stride=8), :] for q in range(8)], 0)
    top[...] = lines_y.T
    wait_bytes(recv5.at[pl.ds(0, 120)], ssem.at[4])


CHUNKS = 8


def add_top(exch, top, out, total, sems):
    size = 2048 // CHUNKS
    copies = [pltpu.make_async_copy(exch.at[2], out.at[2], sems.at[CHUNKS])]
    copies[0].start()
    for k in range(CHUNKS):
        c, start = divmod(k * size, 1024)
        image = top[64 * c : 64 * c + 64, :]
        for at in range(start, start + size, 64):
            total[c, at : at + 64, :] = exch[c, at : at + 64, :] + image
        rows = pl.ds(start, size)
        copies.append(pltpu.make_async_copy(total.at[c, rows], out.at[c, rows], sems.at[k]))
        copies[-1].start()
    for copy in copies:
        copy.wait()


def on_device(magnetization, stiffness, residual_top, residual_side, top_kernel, side_kernel):
    tables = [jnp.asarray(t) for t in const_tables()]
    vmem = pl.BlockSpec(memory_space=pltpu.VMEM)
    hbm = pl.BlockSpec(memory_space=pltpu.HBM)

    def pin(array):
        return pltpu.with_memory_space_constraint(array, pltpu.HBM)

    def buf(*shape):
        return pltpu.VMEM(shape, F32)

    scratch = [
        buf(4, 1152, 128), buf(32, 64), buf(16, 128), *[pltpu.VMEM(t.shape, t.dtype) for t in tables], buf(2, 2, 2, 4, 2048), buf(272, 128), buf(272, 128),
        buf(16, 128), buf(256, 128), buf(256, 128), buf(32, 4, 128), buf(32, 4, 128),
        buf(136, 128), buf(264, 128), buf(272, 128), buf(272, 128), buf(40, 128), buf(136, 128),
        buf(32, 128), buf(72, 128), buf(2, 72, 128), buf(2, 272, 128), buf(32, 128), buf(32, 128),
        buf(64, 128), buf(64, 128), buf(64, 128), buf(64, 128),
        buf(32, 128), buf(32, 128), buf(32, 128), buf(32, 128), buf(64, 128), buf(64, 128),
        pltpu.SemaphoreType.DMA((13,)), pltpu.SemaphoreType.DMA((9,)), pltpu.SemaphoreType.DMA((9,)),
        pltpu.SemaphoreType.DMA((6,)), pltpu.SemaphoreType.DMA((6,)),
        pltpu.SemaphoreType.REGULAR, pltpu.SemaphoreType.REGULAR,
    ]
    exch, top = pl.pallas_call(
        body,
        out_shape=[
            jax.ShapeDtypeStruct((3, 1024, 128), F32),
            jax.ShapeDtypeStruct((128, 128), F32),
        ],
        in_specs=[hbm] * (6 + len(tables)),
        out_specs=[vmem] * 2,
        scratch_shapes=scratch,
        compiler_params=pltpu.CompilerParams(
            collective_id=0, has_side_effects=True, vmem_limit_bytes=40 * 1024 * 1024
        ),
        name="adjoint",
    )(
        pin(magnetization.reshape(3, 1024, 128)),
        pin(stiffness.reshape(1, 1024, 128)),
        pin(residual_top.T),
        pin(residual_side.T),
        pin(top_kernel),
        pin(side_kernel),
        *[pin(t) for t in tables],
    )
    out = pl.pallas_call(
        add_top,
        out_shape=jax.ShapeDtypeStruct((3, 1024, 128), F32),
        in_specs=[vmem, vmem],
        out_specs=hbm,
        scratch_shapes=[buf(2, 1024, 128), pltpu.SemaphoreType.DMA((CHUNKS + 1,))],
        compiler_params=pltpu.CompilerParams(vmem_limit_bytes=4 * 1024 * 1024),
        name="add_top",
    )(exch, top)
    return out.reshape(3, 16, 64, 128)


def solution(mesh):
    placed = (
        P(None, "gz", "gx", "gy"),
        P("gz", "gx", "gy"),
        P("gx", ("gy", "gz")),
        P("gy", "gz"),
        P(None, None, ("gx", "gy", "gz"), None),
        P(None, None, ("gy", "gz"), None),
    )
    return jax.shard_map(
        on_device, mesh=mesh, in_specs=placed, out_specs=P(None, "gz", "gx", "gy"), check_vma=False
    )
```
